256 devices in a mesh: seq: 64 (over z, y, core), head: 4 (over x).
Axes of the slice: x: 4, y: 4, z: 8, core: 2. Of those that a mesh axis runs over, the one named last changes fastest.
Arguments:
- query_vectors: bfloat16 [131072, 1024], P('seq', 'head'), may hold values from -6 to 6
- key_vectors: bfloat16 [131072, 128], P('seq'), may hold values from -6 to 6
- value_vectors: bfloat16 [131072, 128], P('seq'), may hold values from -6 to 6
- output_grad: bfloat16 [131072, 1024], P('seq', 'head'), may hold values from -48 to 48
- random_blocks: int32 [1024, 3], P('seq'), may hold values from 0 to 1023, as said below
- global_blocks: int32 [2], replicated, may hold values from 0 to 1023
Outputs:
- query_grad: bfloat16 [131072, 1024], P('seq', 'head')
- key_grad: bfloat16 [131072, 128], P('seq')
- value_grad: bfloat16 [131072, 128], P('seq')
The draws below stay inside these ranges and needn't reach their ends.
Inputs may be any that keep to these rules, and one draw needn't show every extreme that they name: `random_blocks`: take the query blocks in aligned runs of 16 and the key blocks in aligned runs of 16: all entries of one run of query blocks that fall into one run of key blocks name the same key block.
All inputs are finite; a program needn't handle non-finite values.
Results may differ from the reference program's by a relative error of at most 0.012.
Values may be sent and summed in bfloat16 or wider, within the bound.
A program may use at most 128 MiB of HBM per device.

```python
import jax
import jax.numpy as jnp
from jax import lax

DH = 128
HEADS = 8
BLOCK = 128
R = 3
G = 2
BPD = 16
NBLK = 1024
TOKENS = 131072


def draw_query_vectors(key, part):
    result = jnp.clip(jax.random.normal(jax.random.fold_in(key, 1), (TOKENS, HEADS * DH), jnp.float32), -4.0, 4.0)
    return result.astype(jnp.bfloat16)


def draw_key_vectors(key, part):
    result = jnp.clip(jax.random.normal(jax.random.fold_in(key, 2), (TOKENS, DH), jnp.float32), -4.0, 4.0)
    return result.astype(jnp.bfloat16)


def draw_random_blocks(key, part):
    device_count = NBLK // BPD
    owner_block = jax.random.randint(jax.random.fold_in(key, 3), (device_count, device_count), 0, BPD)
    owner_ids = jax.random.randint(jax.random.fold_in(key, 4), (NBLK, R), 0, device_count)
    requester = jnp.arange(NBLK, dtype=jnp.int32) // BPD
    picked = owner_block[requester[:, None], owner_ids]
    return (owner_ids * BPD + picked).astype(jnp.int32)


def steps_of(rng, extent, cuts, least, high):
    factor_of = 1.0
    for dim, blocks in cuts:
        heights = jax.random.uniform(jax.random.fold_in(jax.random.fold_in(rng, 6), dim), (blocks,), jnp.float32, least / len(cuts), high / len(cuts))
        factor_of = factor_of * jnp.repeat(jnp.exp(heights), extent[dim] // blocks).reshape((-1,) + (1,) * (len(extent) - 1 - dim))
    return factor_of


def centred(rng, dims, scale, bound, split=(), kind=jnp.bfloat16):
    factor_of = steps_of(rng, dims, split, -0.22, 0.18) if split else 1.0
    drawn = jax.random.normal(rng, dims, jnp.float32) * scale * factor_of
    return jnp.minimum(jnp.maximum(drawn, -bound), bound).astype(kind)


def setup_inputs(seed: int = 0) -> dict:
    streams_of = jax.random.split(jax.random.key(seed), 7)
    return {
        "query_vectors": draw_query_vectors(jax.random.fold_in(streams_of[6], 71), 0),
        "key_vectors": draw_key_vectors(jax.random.fold_in(streams_of[6], 71), 0),
        "value_vectors": centred(streams_of[2], (TOKENS, DH), 1.0, 6.0, ((0, 64),)),
        "output_grad": centred(streams_of[3], (TOKENS, HEADS * DH), 8.0, 48.0, ((0, 64), (1, 4))),
        "random_blocks": draw_random_blocks(jax.random.fold_in(streams_of[6], 71), 0),
        "global_blocks": jax.random.randint(streams_of[5], (G,), 0, NBLK).astype(jnp.int32),
    }


def softmax_rows(scores):
    largest = jnp.max(scores, axis=-1, keepdims=True)
    powers = jnp.exp(scores - largest)
    return powers / jnp.sum(powers, axis=-1, keepdims=True)


def reference(query_vectors, key_vectors, value_vectors, output_grad, random_blocks, global_blocks):
    block_count = query_vectors.shape[0] // BLOCK
    factor = float(DH) ** -0.5
    listed = 3 + R + G
    query_blocks = query_vectors.reshape(block_count, BLOCK, HEADS, DH)
    grad_blocks = output_grad.reshape(block_count, BLOCK, HEADS, DH)
    key_blocks = key_vectors.reshape(block_count, BLOCK, DH)
    value_blocks = value_vectors.reshape(block_count, BLOCK, DH)
    order_ids = jnp.arange(block_count, dtype=jnp.int32)
    window = order_ids[:, None] + jnp.array([-1, 0, 1], dtype=jnp.int32)[None, :]
    inside = (window >= 0) & (window < block_count)
    window = jnp.clip(window, 0, block_count - 1).astype(jnp.int32)
    global_rows = jnp.broadcast_to(global_blocks.astype(jnp.int32)[None, :], (block_count, G))
    key_lists = jnp.concatenate([window, random_blocks.astype(jnp.int32), global_rows], axis=1)
    allowed = jnp.concatenate([inside, jnp.ones((block_count, R + G), dtype=jnp.bool_)], axis=1)

    def advance(totals, position):
        key_acc, value_acc = totals
        chosen = key_lists[position]
        key_row_matrix = key_blocks[chosen].reshape(listed * BLOCK, DH).astype(jnp.float32)
        value_row_matrix = value_blocks[chosen].reshape(listed * BLOCK, DH).astype(jnp.float32)
        query_row_matrix = query_blocks[position].astype(jnp.float32)
        gradient_rows = grad_blocks[position].astype(jnp.float32)
        visible = jnp.repeat(allowed[position], BLOCK)
        scores = jnp.einsum("qhd,kd->hqk", query_row_matrix, key_row_matrix) * factor
        scores = jnp.where(visible[None, None, :], scores, -jnp.inf)
        attention = softmax_rows(scores)
        attention_reduced = attention.astype(jnp.bfloat16)
        outputs = jnp.einsum("hqk,kd->qhd", attention_reduced.astype(jnp.float32), value_row_matrix)
        row_delta = jnp.sum(gradient_rows * outputs, axis=-1)
        prob_grad = jnp.einsum("qhd,kd->hqk", gradient_rows, value_row_matrix)
        score_gradient = (attention * (prob_grad - jnp.transpose(row_delta)[:, :, None])).astype(jnp.bfloat16)
        query_part = (jnp.einsum("hqk,kd->qhd", score_gradient.astype(jnp.float32), key_row_matrix) * factor).astype(jnp.bfloat16)
        key_part = jnp.einsum("hqk,qhd->kd", score_gradient.astype(jnp.float32), query_row_matrix) * factor
        value_part = jnp.einsum("hqk,qhd->kd", attention_reduced.astype(jnp.float32), gradient_rows)
        key_acc = key_acc.at[chosen].add(key_part.reshape(listed, BLOCK, DH))
        value_acc = value_acc.at[chosen].add(value_part.reshape(listed, BLOCK, DH))
        return (key_acc, value_acc), query_part

    zeros_acc = jnp.zeros((block_count, BLOCK, DH), dtype=jnp.float32)
    (key_acc, value_acc), query_parts = lax.scan(advance, (zeros_acc, zeros_acc), order_ids)
    query_grad = query_parts.reshape(block_count * BLOCK, HEADS * DH)
    key_grad = key_acc.reshape(block_count * BLOCK, DH).astype(jnp.bfloat16)
    value_grad = value_acc.reshape(block_count * BLOCK, DH).astype(jnp.bfloat16)
    return (query_grad, key_grad, value_grad)
```

```python
import functools

import jax
import jax.numpy as jnp
from jax import lax
from jax.experimental import pallas as pl
from jax.experimental.pallas import tpu as pltpu
from jax.sharding import PartitionSpec as P

DH = 128
BLOCK = 128
R = 3
G = 2
PAIR = 2 * DH
LISTED = 3 + R + G
FACTOR = float(DH) ** -0.5
LOG2E = 1.4426950408889634
NEG = -1e30
NT = (((1,), (1,)), ((), ()))
F32 = jnp.float32
BF16 = jnp.bfloat16


def dot(a, b, dims=(((1,), (0,)), ((), ()))):
    return lax.dot_general(a, b, dims, preferred_element_type=F32)


def compute_kernel(
    heads_x, blocks_x, flags, q_ref, do_ref, win_ref, rnd_ref, glb_ref, dq_ref, g_ref,
    kcat, vcat, kt, s_buf, dp_buf, p_buf, ds_buf, acc, wacc, gacc,
):
    quarter = g_ref.shape[2]
    rand_total = blocks_x * R
    wacc[...] = jnp.zeros_like(wacc)
    gacc[...] = jnp.zeros_like(gacc)

    def fold(value, op):
        return op(value.reshape(BLOCK // 8, 8, PAIR), axis=0)

    def block_step(b, _):
        for j in range(LISTED):
            if j < 3:
                kv = win_ref[b + j]
            elif j < 3 + R:
                kv = rnd_ref[b * R + (j - 3)]
            else:
                kv = glb_ref[j - 3 - R]
            kcat[j] = kv[:, :DH]
            vcat[j] = kv[:, DH:]
            kt[:, j * BLOCK : (j + 1) * BLOCK] = kv[:, :DH].T
        acc[...] = jnp.zeros_like(acc)
        rows = pl.ds(pl.multiple_of(b * BLOCK, BLOCK), BLOCK)
        before_ok = jnp.logical_or(b > 0, flags[0] > 0)
        after_ok = jnp.logical_or(b < blocks_x - 1, flags[1] > 0)

        def pair_step(h, _):
            q = jnp.concatenate([q_ref[h, rows, :DH], q_ref[h, rows, DH:]], axis=0)
            do = jnp.concatenate([do_ref[h, rows, :DH], do_ref[h, rows, DH:]], axis=0)
            top = jnp.full((8, PAIR), NEG, F32)
            for j in range(LISTED):
                s = dot(kcat[j], q, NT)
                if j == 0:
                    s = jnp.where(before_ok, s, NEG)
                if j == 2:
                    s = jnp.where(after_ok, s, NEG)
                s_buf[j] = s
                top = jnp.maximum(top, fold(s, jnp.max))
            top = jnp.max(top, axis=0, keepdims=True)
            total = jnp.zeros((8, PAIR), F32)
            inner = jnp.zeros((8, PAIR), F32)
            for j in range(LISTED):
                dp = dot(vcat[j], do, NT)
                e = jnp.exp2((s_buf[j] - top) * (FACTOR * LOG2E))
                total = total + fold(e, jnp.sum)
                inner = inner + fold(e * dp, jnp.sum)
                s_buf[j] = e
                dp_buf[j] = dp
            scale = 1.0 / jnp.sum(total, axis=0, keepdims=True)
            delta = jnp.sum(inner, axis=0, keepdims=True) * scale
            for j in range(LISTED):
                a = s_buf[j] * scale
                p_buf[j] = a.astype(BF16)
                ds_buf[j] = (a * (dp_buf[j] - delta)).astype(BF16)
            for j in range(LISTED):
                acc[j, :, :DH] += dot(ds_buf[j], q)
                acc[j, :, DH:] += dot(p_buf[j], do)
            dqt = dot(kt[...], ds_buf[...].reshape(LISTED * BLOCK, PAIR)) * FACTOR
            dq_ref[h, rows, :DH] = dqt[:, :BLOCK].T.astype(BF16)
            dq_ref[h, rows, DH:] = dqt[:, BLOCK:].T.astype(BF16)
            return 0

        lax.fori_loop(0, heads_x, pair_step, 0)
        for j in range(LISTED):
            grad = acc[j]
            if j < 3:
                wacc[b + j] += grad
            elif j < 3 + R:
                lane = lax.broadcasted_iota(jnp.int32, grad.shape, 1)
                grad = (grad * jnp.where(lane < DH, FACTOR, 1.0)).astype(BF16)
                for part in range(heads_x):
                    g_ref[part, b * R + (j - 3)] = grad[part * quarter : (part + 1) * quarter]
            else:
                gacc[j - 3 - R] += grad
        return 0

    lax.fori_loop(0, blocks_x, block_step, 0)
    lane = lax.broadcasted_iota(jnp.int32, (BLOCK, PAIR), 1)
    scale = jnp.where(lane < DH, FACTOR, 1.0)
    for j in range(blocks_x + 2 + G):
        grad = wacc[j] if j < blocks_x + 2 else gacc[j - blocks_x - 2]
        grad = (grad * scale).astype(BF16)
        for part in range(heads_x):
            g_ref[part, rand_total + j] = grad[part * quarter : (part + 1) * quarter]


def compute(flags, q_all, do_all, win, rnd, glb):
    heads_x, rows_x, _ = q_all.shape
    blocks_x = rows_x // BLOCK
    slots = blocks_x * R + blocks_x + 2 + G
    vmem = pl.BlockSpec(memory_space=pltpu.VMEM)
    flops = 2 * 5 * heads_x * rows_x * 2 * LISTED * BLOCK * DH
    return pl.pallas_call(
        functools.partial(compute_kernel, heads_x, blocks_x),
        out_shape=(
            jax.ShapeDtypeStruct(q_all.shape, BF16),
            jax.ShapeDtypeStruct((heads_x, slots, BLOCK // heads_x, PAIR), BF16),
        ),
        in_specs=[pl.BlockSpec(memory_space=pltpu.SMEM)] + [vmem] * 5,
        out_specs=(vmem, vmem),
        scratch_shapes=[
            pltpu.VMEM((LISTED, BLOCK, DH), BF16),
            pltpu.VMEM((LISTED, BLOCK, DH), BF16),
            pltpu.VMEM((DH, LISTED * BLOCK), BF16),
            pltpu.VMEM((LISTED, BLOCK, PAIR), F32),
            pltpu.VMEM((LISTED, BLOCK, PAIR), F32),
            pltpu.VMEM((LISTED, BLOCK, PAIR), BF16),
            pltpu.VMEM((LISTED, BLOCK, PAIR), BF16),
            pltpu.VMEM((LISTED, BLOCK, PAIR), F32),
            pltpu.VMEM((blocks_x + 2, BLOCK, PAIR), F32),
            pltpu.VMEM((G, BLOCK, PAIR), F32),
        ],
        compiler_params=pltpu.CompilerParams(vmem_limit_bytes=40 * 2**20),
        cost_estimate=pl.CostEstimate(flops=flops, bytes_accessed=8 * 2**20, transcendentals=0),
        name="compute",
    )(flags, q_all, do_all, win, rnd, glb)


def a2a(value, axis):
    return lax.all_to_all(value, axis, split_axis=0, concat_axis=0, tiled=True)


def body(query_vectors, key_vectors, value_vectors, output_grad, random_blocks, global_blocks):
    seq = lax.axis_size("seq")
    heads_x = lax.axis_size("head")
    s = lax.axis_index("seq")
    x = lax.axis_index("head")
    rows = query_vectors.shape[0]
    blocks = rows // BLOCK
    blocks_x = blocks // heads_x
    quarter = BLOCK // heads_x
    entries = blocks_x * R

    kv = jnp.concatenate([key_vectors, value_vectors], axis=1).reshape(blocks, BLOCK, PAIR)
    owners = random_blocks // blocks
    within = random_blocks % blocks
    peers = jnp.arange(seq, dtype=jnp.int32)
    matched = owners[:, :, None] == peers[None, None, :]
    wanted = jnp.max(jnp.where(matched, within[:, :, None], -1), axis=(0, 1))
    requested = a2a(wanted.reshape(seq, 1), "seq")[:, 0]
    kv_part = lax.dynamic_slice_in_dim(kv, x * quarter, quarter, 1)
    served = kv_part[jnp.clip(requested, 0, blocks - 1)]
    fetched = a2a(served, "seq")
    mine = fetched[owners.reshape(heads_x, entries)]
    rnd = a2a(mine, "head").transpose(1, 0, 2, 3).reshape(entries, BLOCK, PAIR)
    q_all = a2a(query_vectors.reshape(heads_x, blocks_x * BLOCK, PAIR), "head")
    do_all = a2a(output_grad.reshape(heads_x, blocks_x * BLOCK, PAIR), "head")
    up = [(i, (i + 1) % seq) for i in range(seq)]
    down = [(j, i) for i, j in up]
    before = lax.ppermute(kv[blocks - 1 :], "seq", up)
    after = lax.ppermute(kv[:1], "seq", down)
    extended = jnp.concatenate([before, kv, after], axis=0)
    win = lax.dynamic_slice_in_dim(extended, x * blocks_x, blocks_x + 2, 0)
    held = jnp.where(
        (global_blocks // blocks == s)[:, None, None], kv[global_blocks % blocks], 0
    ).astype(BF16)
    glb = lax.psum(held, "seq")
    flags = jnp.stack([s + x, seq - 1 - s + heads_x - 1 - x]).astype(jnp.int32)

    dq_all, grads = compute(flags, q_all, do_all, win, rnd, glb)

    query_grad = a2a(dq_all, "head").reshape(rows, PAIR)
    parts = a2a(grads, "head").astype(F32)
    hot = (owners.reshape(-1)[None, :] == peers[:, None]).astype(F32)
    from_entries = parts[:, :entries].reshape(heads_x * entries, quarter, PAIR)
    slots = jnp.einsum("en,nrc->erc", hot, from_entries, precision=lax.Precision.HIGHEST)
    returned = a2a(slots.astype(BF16), "seq").astype(F32)
    served_hot = (requested[None, :] == jnp.arange(blocks)[:, None]).astype(F32)
    total = jnp.einsum("be,erc->brc", served_hot, returned, precision=lax.Precision.HIGHEST)
    window = jnp.zeros((blocks + 2, quarter, PAIR), F32)
    for part in range(heads_x):
        window = window.at[part * blocks_x : part * blocks_x + blocks_x + 2].add(
            parts[part, entries : entries + blocks_x + 2]
        )
    into_last = lax.ppermute(window[0].astype(BF16), "seq", down).astype(F32)
    into_first = lax.ppermute(window[blocks + 1].astype(BF16), "seq", up).astype(F32)
    total = total + window[1 : blocks + 1]
    total = total.at[blocks - 1].add(into_last).at[0].add(into_first)
    glob = lax.psum(jnp.sum(parts[:, entries + blocks_x + 2 :], axis=0), "seq")
    owned = (global_blocks[None, :] == s * blocks + jnp.arange(blocks)[:, None]).astype(F32)
    total = total + jnp.einsum("bg,grc->brc", owned, glob, precision=lax.Precision.HIGHEST)
    final = lax.all_gather(total.astype(BF16), "head", axis=1, tiled=True).reshape(rows, PAIR)
    return query_grad, final[:, :DH], final[:, DH:]


def solution(mesh):
    return jax.shard_map(
        body,
        mesh=mesh,
        in_specs=(
            P("seq", "head"),
            P("seq", None),
            P("seq", None),
            P("seq", "head"),
            P("seq", None),
            P(),
        ),
        out_specs=(P("seq", "head"), P("seq", None), P("seq", None)),
        check_vma=False,
    )
```

```python
import functools

import jax
import jax.numpy as jnp
from jax import lax
from jax.experimental import pallas as pl
from jax.experimental.pallas import tpu as pltpu
from jax.sharding import PartitionSpec as P

DH = 128
BLOCK = 128
R = 3
G = 2
PAIR = 2 * DH
LISTED = 3 + R + G
FACTOR = float(DH) ** -0.5
LOG2E = 1.4426950408889634
NEG = -1e30
NT = (((1,), (1,)), ((), ()))
F32 = jnp.float32
BF16 = jnp.bfloat16
MESH = pl.DeviceIdType.MESH


def dot(a, b, dims=(((1,), (0,)), ((), ()))):
    return lax.dot_general(a, b, dims, preferred_element_type=F32)


def compute_kernel(
    heads_x, blocks_x, flags, q_ref, do_ref, k_ref, v_ref, halo_ref, rnd_ref, pieces_ref,
    dq_ref, g_ref, win_ref, glb_ref, kcat, vcat, kt, s_buf, dp_buf, p_buf, ds_buf, acc, wacc, gacc,
):
    quarter = g_ref.shape[2]
    rand_total = blocks_x * R
    blocks = k_ref.shape[0]
    for i in range(blocks_x + 2):
        at = flags[2] * blocks_x + (i - 1)
        inner_at = jnp.clip(at, 0, blocks - 1)
        for n, ref in enumerate((k_ref, v_ref)):
            value = ref[inner_at]
            if i == 0:
                value = jnp.where(at < 0, halo_ref[0, n], value)
            if i == blocks_x + 1:
                value = jnp.where(at >= blocks, halo_ref[1, n], value)
            win_ref[i, :, n * DH : (n + 1) * DH] = value
    per = BLOCK // 16
    for g in range(G):
        for n in range(2):
            first = (g * 2 + n) * per
            whole = pieces_ref[first : first + per].reshape(BLOCK, DH)
            glb_ref[g, :, n * DH : (n + 1) * DH] = whole
    wacc[...] = jnp.zeros_like(wacc)
    gacc[...] = jnp.zeros_like(gacc)

    def fold(value, op):
        return op(value.reshape(BLOCK // 8, 8, PAIR), axis=0)

    def block_step(b, _):
        for j in range(LISTED):
            if j < 3:
                kv = win_ref[b + j]
            elif j < 3 + R:
                kv = rnd_ref[b * R + (j - 3)]
            else:
                kv = glb_ref[j - 3 - R]
            kcat[j] = kv[:, :DH]
            vcat[j] = kv[:, DH:]
            kt[:, j * BLOCK : (j + 1) * BLOCK] = kv[:, :DH].T
        acc[...] = jnp.zeros_like(acc)
        rows = pl.ds(pl.multiple_of(b * BLOCK, BLOCK), BLOCK)
        before_ok = jnp.logical_or(b > 0, flags[0] > 0)
        after_ok = jnp.logical_or(b < blocks_x - 1, flags[1] > 0)

        def pair_step(h, _):
            q = jnp.concatenate([q_ref[h, rows, :DH], q_ref[h, rows, DH:]], axis=0)
            do = jnp.concatenate([do_ref[h, rows, :DH], do_ref[h, rows, DH:]], axis=0)
            top = jnp.full((8, PAIR), NEG, F32)
            for j in range(LISTED):
                s = dot(kcat[j], q, NT)
                if j == 0:
                    s = jnp.where(before_ok, s, NEG)
                if j == 2:
                    s = jnp.where(after_ok, s, NEG)
                s_buf[j] = s
                top = jnp.maximum(top, fold(s, jnp.max))
            top = jnp.max(top, axis=0, keepdims=True)
            total = jnp.zeros((8, PAIR), F32)
            inner = jnp.zeros((8, PAIR), F32)
            for j in range(LISTED):
                dp = dot(vcat[j], do, NT)
                e = jnp.exp2((s_buf[j] - top) * (FACTOR * LOG2E))
                total = total + fold(e, jnp.sum)
                inner = inner + fold(e * dp, jnp.sum)
                s_buf[j] = e
                dp_buf[j] = dp
            scale = 1.0 / jnp.sum(total, axis=0, keepdims=True)
            delta = jnp.sum(inner, axis=0, keepdims=True) * scale
            for j in range(LISTED):
                a = s_buf[j] * scale
                p_buf[j] = a.astype(BF16)
                ds_buf[j] = (a * (dp_buf[j] - delta)).astype(BF16)
            for j in range(LISTED):
                acc[j, :, :DH] += dot(ds_buf[j], q)
                acc[j, :, DH:] += dot(p_buf[j], do)
            dqt = dot(kt[...], ds_buf[...].reshape(LISTED * BLOCK, PAIR)) * FACTOR
            dq_ref[h, rows, :DH] = dqt[:, :BLOCK].T.astype(BF16)
            dq_ref[h, rows, DH:] = dqt[:, BLOCK:].T.astype(BF16)
            return 0

        lax.fori_loop(0, heads_x, pair_step, 0)
        for j in range(LISTED):
            grad = acc[j]
            if j < 3:
                wacc[b + j] += grad
            elif j < 3 + R:
                lane = lax.broadcasted_iota(jnp.int32, grad.shape, 1)
                grad = (grad * jnp.where(lane < DH, FACTOR, 1.0)).astype(BF16)
                for part in range(heads_x):
                    g_ref[part, b * R + (j - 3)] = grad[part * quarter : (part + 1) * quarter]
            else:
                gacc[j - 3 - R] += grad
        return 0

    lax.fori_loop(0, blocks_x, block_step, 0)
    lane = lax.broadcasted_iota(jnp.int32, (BLOCK, PAIR), 1)
    scale = jnp.where(lane < DH, FACTOR, 1.0)
    for j in range(blocks_x + 2 + G):
        grad = wacc[j] if j < blocks_x + 2 else gacc[j - blocks_x - 2]
        grad = (grad * scale).astype(BF16)
        for part in range(heads_x):
            g_ref[part, rand_total + j] = grad[part * quarter : (part + 1) * quarter]


def compute(flags, q_all, do_all, keys, values, halo, rnd, pieces):
    heads_x, rows_x, _ = q_all.shape
    blocks_x = rows_x // BLOCK
    slots = blocks_x * R + blocks_x + 2 + G
    vmem = pl.BlockSpec(memory_space=pltpu.VMEM)
    flops = 2 * 5 * heads_x * rows_x * 2 * LISTED * BLOCK * DH
    return pl.pallas_call(
        functools.partial(compute_kernel, heads_x, blocks_x),
        out_shape=(
            jax.ShapeDtypeStruct(q_all.shape, BF16),
            jax.ShapeDtypeStruct((heads_x, slots, BLOCK // heads_x, PAIR), BF16),
        ),
        in_specs=[pl.BlockSpec(memory_space=pltpu.SMEM)] + [vmem] * 7,
        out_specs=(vmem, vmem),
        scratch_shapes=[
            pltpu.VMEM((blocks_x + 2, BLOCK, PAIR), BF16),
            pltpu.VMEM((G, BLOCK, PAIR), BF16),
            pltpu.VMEM((LISTED, BLOCK, DH), BF16),
            pltpu.VMEM((LISTED, BLOCK, DH), BF16),
            pltpu.VMEM((DH, LISTED * BLOCK), BF16),
            pltpu.VMEM((LISTED, BLOCK, PAIR), F32),
            pltpu.VMEM((LISTED, BLOCK, PAIR), F32),
            pltpu.VMEM((LISTED, BLOCK, PAIR), BF16),
            pltpu.VMEM((LISTED, BLOCK, PAIR), BF16),
            pltpu.VMEM((LISTED, BLOCK, PAIR), F32),
            pltpu.VMEM((blocks_x + 2, BLOCK, PAIR), F32),
            pltpu.VMEM((G, BLOCK, PAIR), F32),
        ],
        compiler_params=pltpu.CompilerParams(vmem_limit_bytes=40 * 2**20),
        cost_estimate=pl.CostEstimate(flops=flops, bytes_accessed=8 * 2**20, transcendentals=0),
        name="compute",
    )(flags, q_all, do_all, keys, values, halo, rnd, pieces)


def arrived(ref, sem):
    pltpu.make_async_copy(ref, ref, sem).wait()


def greet(seq, heads_x, s, x):
    barrier = pltpu.get_barrier_semaphore()

    def greet_seq(j, _):
        pl.semaphore_signal(
            barrier, inc=1, device_id=(lax.rem(s + j, seq), x), device_id_type=MESH
        )
        return 0

    lax.fori_loop(1, seq, greet_seq, 0)
    for d in range(1, heads_x):
        pl.semaphore_signal(
            barrier, inc=1, device_id=(s, lax.rem(x + d, heads_x)), device_id_type=MESH
        )
    pl.semaphore_wait(barrier, seq - 1 + heads_x - 1)


def relays(seq, pieces):
    return max(1, seq // pieces), max(1, pieces // seq)


def fetch_kernel(
    seq, heads_x, table, wanted_ref, q_ref, do_ref, k_ref, v_ref,
    wbuf, q_all, do_all, halo, rnd, gout,
    wsm, send_buf, fq, send2, cand, gin, relay_buf, sem_w, sem_g, sem_b, sem_h, sem_q, sem_d,
    sem_f, sem_r, local_sem,
):
    s = lax.axis_index("seq")
    x = lax.axis_index("head")
    blocks = k_ref.shape[0]
    quarter = BLOCK // heads_x
    entries = rnd.shape[0]
    rows_x = q_all.shape[1]
    pieces = gout.shape[0]
    per = BLOCK // 16
    stride, ppr = relays(seq, pieces)
    count = pieces // ppr
    part = pl.ds(pl.multiple_of(x * quarter, quarter), quarter)

    def remote(src, dst, sem, to):
        return pltpu.make_async_remote_copy(
            src_ref=src, dst_ref=dst, send_sem=sem.at[0], recv_sem=sem.at[1],
            device_id=to, device_id_type=MESH,
        )

    for g in range(G):
        at = table[heads_x * entries + G + g]
        for n, ref in enumerate((k_ref, v_ref)):
            first = (g * 2 + n) * per
            cand[first : first + per] = ref[at].reshape(per, 16, DH)
    wbuf[s] = wanted_ref[...]

    own_rows = pl.ds(pl.multiple_of(x * rows_x, rows_x), rows_x)
    own_q = pltpu.make_async_copy(q_ref.at[own_rows], q_all.at[x], local_sem.at[0])
    own_do = pltpu.make_async_copy(do_ref.at[own_rows], do_all.at[x], local_sem.at[1])
    own_q.start()
    own_do.start()

    greet(seq, heads_x, s, x)

    def send_wanted(j, _):
        remote(wanted_ref, wbuf.at[s], sem_w, (lax.rem(s + j, seq), x)).start()
        return 0

    lax.fori_loop(1, seq, send_wanted, 0)

    is_relay = lax.rem(s, stride) == 0
    mine = s // stride

    def send_cand(r, _):
        @pl.when(r * stride != s)
        def _():
            remote(
                cand.at[pl.ds(r * ppr, ppr)], gin.at[s], sem_g, (r * stride, x)
            ).start()

        return 0

    lax.fori_loop(0, count, send_cand, 0)

    @pl.when(is_relay)
    def _():
        gin[s] = cand[pl.ds(mine * ppr, ppr)]

    for d in range(1, heads_x):
        to = lax.rem(x + d, heads_x)
        rows = pl.ds(pl.multiple_of(to * rows_x, rows_x), rows_x)
        remote(q_ref.at[rows], q_all.at[x], sem_q, (s, to)).start()
        remote(do_ref.at[rows], do_all.at[x], sem_d, (s, to)).start()

    after = (lax.rem(s + 1, seq), x)
    before = (lax.rem(s + seq - 1, seq), x)
    for n, ref in enumerate((k_ref, v_ref)):
        remote(ref.at[blocks - 1], halo.at[0, n], sem_h, after).start()
        remote(ref.at[0], halo.at[1, n], sem_h, before).start()

    arrived(wbuf.at[pl.ds(0, seq - 1)], sem_w.at[1])
    to_smem = pltpu.make_async_copy(wbuf, wsm, local_sem.at[2])
    to_smem.start()
    to_smem.wait()

    def serve(e, _):
        at = wsm[e, 0, s]
        send_buf[e, :, :DH] = k_ref[at, part, :]
        send_buf[e, :, DH:] = v_ref[at, part, :]
        return 0

    lax.fori_loop(0, seq, serve, 0)
    fq[s] = send_buf[s]

    def send_served(j, _):
        e = lax.rem(s + j, seq)
        remote(send_buf.at[e], fq.at[s], sem_f, (e, x)).start()
        return 0

    lax.fori_loop(1, seq, send_served, 0)

    @pl.when(is_relay)
    def _():
        arrived(gin.at[pl.ds(0, seq - 1)], sem_g.at[1])
        for i in range(ppr):
            g = (mine * ppr + i) // (2 * per)
            relay_buf[i] = gin[table[heads_x * entries + g], i]
        gout[pl.ds(mine * ppr, ppr)] = relay_buf[...]

        def send_piece(j, _):
            remote(
                relay_buf, gout.at[pl.ds(mine * ppr, ppr)], sem_b, (lax.rem(s + j, seq), x)
            ).start()
            return 0

        lax.fori_loop(1, seq, send_piece, 0)

    arrived(fq.at[pl.ds(0, seq - 1)], sem_f.at[1])
    for d in range(1, heads_x):
        to = lax.rem(x + d, heads_x)
        for j in range(entries):
            send2[d - 1, j] = fq[table[to * entries + j]]
    for d in range(1, heads_x):
        to = lax.rem(x + d, heads_x)
        remote(send2.at[d - 1], rnd.at[:, part, :], sem_r, (s, to)).start()
    for j in range(entries):
        rnd[j, part, :] = fq[table[x * entries + j]]

    arrived(send2, sem_r.at[1])
    arrived(q_all.at[pl.ds(0, heads_x - 1)], sem_q.at[1])
    arrived(do_all.at[pl.ds(0, heads_x - 1)], sem_d.at[1])
    arrived(halo, sem_h.at[1])
    own_q.wait()
    own_do.wait()

    @pl.when(is_relay)
    def _():
        arrived(gout.at[pl.ds(0, (count - 1) * ppr)], sem_b.at[1])
        arrived(gin.at[pl.ds(0, seq - 1)], sem_b.at[0])
        if count > 1:
            arrived(gin.at[pl.ds(0, count - 1)], sem_g.at[0])

    @pl.when(jnp.logical_not(is_relay))
    def _():
        arrived(gout, sem_b.at[1])
        arrived(gin.at[pl.ds(0, count)], sem_g.at[0])

    arrived(wbuf.at[pl.ds(0, seq - 1)], sem_w.at[0])
    arrived(send_buf.at[pl.ds(0, seq - 1)], sem_f.at[0])
    arrived(send2, sem_r.at[0])
    arrived(q_all.at[pl.ds(0, heads_x - 1)], sem_q.at[0])
    arrived(do_all.at[pl.ds(0, heads_x - 1)], sem_d.at[0])
    arrived(halo, sem_h.at[0])


def fetch(seq, heads_x, table, wanted, query, grad, keys, values):
    rows, width = query.shape
    rows_x = rows // heads_x
    entries = rows_x // BLOCK * R
    quarter = BLOCK // heads_x
    pieces = G * 2 * BLOCK // 16
    _, ppr = relays(seq, pieces)
    vmem = pl.BlockSpec(memory_space=pltpu.VMEM)
    anyspec = pl.BlockSpec(memory_space=pl.ANY)
    pair = pltpu.SemaphoreType.DMA((2,))
    return pl.pallas_call(
        functools.partial(fetch_kernel, seq, heads_x),
        out_shape=(
            jax.ShapeDtypeStruct((seq, 1, 128), jnp.int32),
            jax.ShapeDtypeStruct((heads_x, rows_x, width), BF16),
            jax.ShapeDtypeStruct((heads_x, rows_x, width), BF16),
            jax.ShapeDtypeStruct((2, 2, BLOCK, DH), BF16),
            jax.ShapeDtypeStruct((entries, BLOCK, PAIR), BF16),
            jax.ShapeDtypeStruct((pieces, 16, DH), BF16),
        ),
        in_specs=[pl.BlockSpec(memory_space=pltpu.SMEM), vmem, anyspec, anyspec, vmem, vmem],
        out_specs=(vmem,) * 6,
        scratch_shapes=[
            pltpu.SMEM((seq, 1, 128), jnp.int32),
            pltpu.VMEM((seq, quarter, PAIR), BF16),
            pltpu.VMEM((seq, quarter, PAIR), BF16),
            pltpu.VMEM((heads_x - 1, entries, quarter, PAIR), BF16),
            pltpu.VMEM((pieces, 16, DH), BF16),
            pltpu.VMEM((seq, ppr, 16, DH), BF16),
            pltpu.VMEM((ppr, 16, DH), BF16),
            pair, pair, pair, pair, pair, pair, pair, pair,
            pltpu.SemaphoreType.DMA((3,)),
        ],
        compiler_params=pltpu.CompilerParams(
            vmem_limit_bytes=30 * 2**20, collective_id=0, has_side_effects=True
        ),
        name="fetch",
    )(table, wanted, query, grad, keys, values)


def return_kernel(
    seq, heads_x, table, own, g_ref, dq_ref, qg, kg, vg,
    parts, run, sbuf, rbuf, run2, edge, gp, gin, relay_buf, gtot,
    sem_e, sem_a, sem_q, sem_s, sem_n, sem_g, sem_b, sem_k, sem_v, local_sem,
):
    s = lax.axis_index("seq")
    x = lax.axis_index("head")
    rows_x = dq_ref.shape[1]
    blocks_x = rows_x // BLOCK
    blocks = blocks_x * heads_x
    entries = blocks_x * R
    quarter = BLOCK // heads_x
    slots = g_ref.shape[1]
    rest = slots - entries
    pieces = gp.shape[0]
    stride, ppr = relays(seq, pieces)
    count = pieces // ppr
    total_entries = heads_x * entries
    last_e = total_entries
    prev_r = last_e + seq
    last_r = prev_r + seq
    part = pl.ds(pl.multiple_of(x * quarter, quarter), quarter)
    rand_part = pl.ds(0, entries)
    rest_part = pl.ds(entries, rest)

    def remote(src, dst, sem, to):
        return pltpu.make_async_remote_copy(
            src_ref=src, dst_ref=dst, send_sem=sem.at[0], recv_sem=sem.at[1],
            device_id=to, device_id_type=MESH,
        )

    greet(seq, heads_x, s, x)
    for d in range(1, heads_x):
        to = lax.rem(x + d, heads_x)
        remote(g_ref.at[to, rand_part], parts.at[x, rand_part], sem_e, (s, to)).start()
    for d in range(1, heads_x):
        to = lax.rem(x + d, heads_x)
        remote(g_ref.at[to, rest_part], parts.at[x, rest_part], sem_a, (s, to)).start()
    out_rows = pl.ds(pl.multiple_of(x * rows_x, rows_x), rows_x)
    for d in range(1, heads_x):
        to = lax.rem(x + d, heads_x)
        remote(dq_ref.at[to], qg.at[out_rows], sem_q, (s, to)).start()
    own_q = pltpu.make_async_copy(dq_ref.at[x], qg.at[out_rows], local_sem)
    own_q.start()
    parts[x] = g_ref[x]
    run[0] = jnp.zeros((quarter, PAIR), F32)
    run2[0] = jnp.zeros((quarter, PAIR), F32)

    arrived(g_ref.at[pl.ds(0, heads_x - 1), rand_part], sem_e.at[1])
    for src in range(heads_x):

        def chain(j, _, src=src):
            at = src * entries + j
            run[at + 1] = parts[src, j].astype(F32) + run[table[at]]
            return 0

        lax.fori_loop(0, entries, chain, 0)

    def fill(e, _):
        sbuf[e] = run[table[last_e + e]].astype(BF16)
        return 0

    lax.fori_loop(0, seq, fill, 0)
    rbuf[s] = sbuf[s]

    def send_slot(j, _):
        e = lax.rem(s + j, seq)
        remote(sbuf.at[e], rbuf.at[s], sem_s, (e, x)).start()
        return 0

    lax.fori_loop(1, seq, send_slot, 0)

    arrived(g_ref.at[pl.ds(0, heads_x - 1), rest_part], sem_a.at[1])
    after = (lax.rem(s + 1, seq), x)
    before = (lax.rem(s + seq - 1, seq), x)
    remote(parts.at[0, entries], edge.at[1], sem_n, before).start()
    remote(
        parts.at[heads_x - 1, entries + blocks_x + 1], edge.at[0], sem_n, after
    ).start()

    chunks = quarter // 8
    for g in range(G):
        value = parts[0, entries + blocks_x + 2 + g].astype(F32)
        for src in range(1, heads_x):
            value = value + parts[src, entries + blocks_x + 2 + g].astype(F32)
        for c in range(chunks):
            for n in range(2):
                gp[(g * chunks + c) * 2 + n] = value[
                    c * 8 : (c + 1) * 8, n * DH : (n + 1) * DH
                ]

    is_relay = lax.rem(s, stride) == 0
    mine = s // stride

    @pl.when(is_relay)
    def _():
        gin[s] = gp[pl.ds(mine * ppr, ppr)]

    def send_global(r, _):
        @pl.when(r * stride != s)
        def _():
            remote(gp.at[pl.ds(r * ppr, ppr)], gin.at[s], sem_g, (r * stride, x)).start()

        return 0

    lax.fori_loop(0, count, send_global, 0)

    @pl.when(is_relay)
    def _():
        arrived(gin.at[pl.ds(0, seq - 1)], sem_g.at[1])
        relay_buf[...] = jnp.zeros_like(relay_buf)

        def add(e, _):
            relay_buf[...] += gin[e]
            return 0

        lax.fori_loop(0, seq, add, 0)
        gtot[pl.ds(mine * ppr, ppr)] = relay_buf[...]

        def send_piece(j, _):
            remote(
                relay_buf, gtot.at[pl.ds(mine * ppr, ppr)], sem_b, (lax.rem(s + j, seq), x)
            ).start()
            return 0

        lax.fori_loop(1, seq, send_piece, 0)

    arrived(edge, sem_n.at[1])

    @pl.when(is_relay)
    def _():
        arrived(gtot.at[pl.ds(0, (count - 1) * ppr)], sem_b.at[1])
        arrived(gin.at[pl.ds(0, seq - 1)], sem_b.at[0])
        if count > 1:
            arrived(gin.at[pl.ds(0, count - 1)], sem_g.at[0])

    @pl.when(jnp.logical_not(is_relay))
    def _():
        arrived(gtot, sem_b.at[1])
        arrived(gin.at[pl.ds(0, count)], sem_g.at[0])

    arrived(rbuf.at[pl.ds(0, seq - 1)], sem_s.at[1])

    def gather(e, _):
        run2[e + 1] = rbuf[e].astype(F32) + run2[table[prev_r + e]]
        return 0

    lax.fori_loop(0, seq, gather, 0)
    for b in range(blocks):
        src, i = b // blocks_x, b % blocks_x
        total = run2[table[last_r + b]] + parts[src, entries + 1 + i].astype(F32)
        if i == 0:
            more = edge[0] if src == 0 else parts[src - 1, entries + blocks_x + 1]
            total = total + more.astype(F32)
        if i == blocks_x - 1:
            more = edge[1] if src == heads_x - 1 else parts[src + 1, entries]
            total = total + more.astype(F32)
        for c in range(chunks):
            lines = pl.ds(pl.multiple_of(x * quarter + c * 8, 8), 8)
            for n, ref in enumerate((kg, vg)):
                value = total[c * 8 : (c + 1) * 8, n * DH : (n + 1) * DH]
                for g in range(G):
                    value = value + own[g * blocks + b] * gtot[(g * chunks + c) * 2 + n]
                run[b, c * 8 : (c + 1) * 8, n * DH : (n + 1) * DH] = value
        kg[b, part, :] = run[b, :, :DH].astype(BF16)
        vg[b, part, :] = run[b, :, DH:].astype(BF16)
    for d in range(1, heads_x):
        to = (s, lax.rem(x + d, heads_x))
        remote(kg.at[:, part, :], kg.at[:, part, :], sem_k, to).start()
        remote(vg.at[:, part, :], vg.at[:, part, :], sem_v, to).start()

    arrived(g_ref.at[pl.ds(0, heads_x - 1), rand_part], sem_e.at[0])
    arrived(g_ref.at[pl.ds(0, heads_x - 1), rest_part], sem_a.at[0])
    arrived(edge, sem_n.at[0])
    arrived(rbuf.at[pl.ds(0, seq - 1)], sem_s.at[0])
    arrived(dq_ref.at[pl.ds(0, heads_x - 1)], sem_q.at[0])
    arrived(dq_ref.at[pl.ds(0, heads_x - 1)], sem_q.at[1])
    own_q.wait()
    others = pl.ds(0, (heads_x - 1) * quarter)
    for sem, ref in ((sem_k, kg), (sem_v, vg)):
        arrived(ref.at[:, others, :], sem.at[0])
        arrived(ref.at[:, others, :], sem.at[1])


def give_back(seq, heads_x, table, own, grads, dq_all):
    _, rows_x, width = dq_all.shape
    _, slots, quarter, _ = grads.shape
    blocks_x = rows_x // BLOCK
    blocks = blocks_x * heads_x
    total_entries = blocks * R
    pieces = G * (quarter // 8) * 2
    _, ppr = relays(seq, pieces)
    vmem = pl.BlockSpec(memory_space=pltpu.VMEM)
    smem = pl.BlockSpec(memory_space=pltpu.SMEM)
    pair = pltpu.SemaphoreType.DMA((2,))
    return pl.pallas_call(
        functools.partial(return_kernel, seq, heads_x),
        out_shape=(
            jax.ShapeDtypeStruct((heads_x * rows_x, width), BF16),
            jax.ShapeDtypeStruct((blocks, BLOCK, DH), BF16),
            jax.ShapeDtypeStruct((blocks, BLOCK, DH), BF16),
        ),
        in_specs=[smem, smem, vmem, vmem],
        out_specs=(pl.BlockSpec(memory_space=pl.ANY), vmem, vmem),
        scratch_shapes=[
            pltpu.VMEM((heads_x, slots, quarter, PAIR), BF16),
            pltpu.VMEM((total_entries + 1, quarter, PAIR), F32),
            pltpu.VMEM((seq, quarter, PAIR), BF16),
            pltpu.VMEM((seq, quarter, PAIR), BF16),
            pltpu.VMEM((seq + 1, quarter, PAIR), F32),
            pltpu.VMEM((2, quarter, PAIR), BF16),
            pltpu.VMEM((pieces, 8, DH), F32),
            pltpu.VMEM((seq, ppr, 8, DH), F32),
            pltpu.VMEM((ppr, 8, DH), F32),
            pltpu.VMEM((pieces, 8, DH), F32),
            pair, pair, pair, pair, pair, pair, pair, pair, pair,
            pltpu.SemaphoreType.DMA,
        ],
        compiler_params=pltpu.CompilerParams(
            vmem_limit_bytes=30 * 2**20, collective_id=1, has_side_effects=True
        ),
        name="give_back",
    )(table, own, grads, dq_all)


def chain_of(keys, groups):
    count = keys.shape[0]
    order = jnp.arange(count, dtype=jnp.int32)
    same = (keys[:, None] == keys[None, :]) & (order[None, :] < order[:, None])
    previous = jnp.max(jnp.where(same, order[None, :] + 1, 0), axis=1)
    hit = keys[None, :] == jnp.arange(groups, dtype=jnp.int32)[:, None]
    last = jnp.max(jnp.where(hit, order[None, :] + 1, 0), axis=1)
    return previous, last


def body(query_vectors, key_vectors, value_vectors, output_grad, random_blocks, global_blocks):
    seq = lax.axis_size("seq")
    heads_x = lax.axis_size("head")
    s = lax.axis_index("seq")
    x = lax.axis_index("head")
    rows = query_vectors.shape[0]
    blocks = rows // BLOCK

    owners = (random_blocks // blocks).reshape(-1)
    within = (random_blocks % blocks).reshape(-1)
    peers = jnp.arange(128, dtype=jnp.int32)
    matched = owners[:, None] == peers[None, :]
    wanted = jnp.max(jnp.where(matched, within[:, None], 0), axis=0, keepdims=True)
    table = jnp.concatenate([owners, global_blocks // blocks, global_blocks % blocks])
    keys = key_vectors.reshape(blocks, BLOCK, DH)
    values = value_vectors.reshape(blocks, BLOCK, DH)
    wbuf, q_all, do_all, halo, rnd, pieces = fetch(
        seq, heads_x, table, wanted, query_vectors, output_grad, keys, values
    )
    flags = jnp.stack([s + x, seq - 1 - s + heads_x - 1 - x, x]).astype(jnp.int32)
    dq_all, grads = compute(flags, q_all, do_all, keys, values, halo, rnd, pieces)
    requested = lax.dynamic_index_in_dim(wbuf[:, 0, :], s, 1, keepdims=False)
    prev_e, last_e = chain_of(owners, seq)
    prev_r, last_r = chain_of(requested, blocks)
    chains = jnp.concatenate([prev_e, last_e, prev_r, last_r])
    owned = global_blocks[:, None] == (s * blocks + jnp.arange(blocks, dtype=jnp.int32))[None, :]
    query_grad, key_grad, value_grad = give_back(
        seq, heads_x, chains, owned.reshape(-1).astype(F32), grads, dq_all
    )
    return query_grad, key_grad.reshape(rows, DH), value_grad.reshape(rows, DH)


def solution(mesh):
    return jax.shard_map(
        body,
        mesh=mesh,
        in_specs=(
            P("seq", "head"),
            P("seq", None),
            P("seq", None),
            P("seq", "head"),
            P("seq", None),
            P(),
        ),
        out_specs=(P("seq", "head"), P("seq", None), P("seq", None)),
        check_vma=False,
    )
```

```python
import functools
import types

import jax
import jax.numpy as jnp
from jax import lax
from jax.experimental import pallas as pl
from jax.experimental.pallas import tpu as pltpu
from jax.sharding import PartitionSpec as P

DH = 128
BLOCK = 128
R = 3
G = 2
NEAR = 3 + G
PAIR = 2 * DH
FACTOR = float(DH) ** -0.5
LOG2E = 1.4426950408889634
NEG = -1e30
NT = (((1,), (1,)), ((), ()))
F32 = jnp.float32
BF16 = jnp.bfloat16
I32 = jnp.int32
MESH = pl.DeviceIdType.MESH


def dot(a, b, dims=(((1,), (0,)), ((), ()))):
    return lax.dot_general(a, b, dims, preferred_element_type=F32)


def fold(value, op):
    return op(value.reshape(BLOCK // 8, 8, PAIR), axis=0)


def arrived(ref, sem):
    pltpu.make_async_copy(ref, ref, sem).wait()


def relays(seq, pieces):
    return max(1, seq // pieces), max(1, pieces // seq)


def loop(count, step, first=0):
    def run(i, carry):
        step(i)
        return carry

    lax.fori_loop(first, count, run, 0)


def shapes(seq, heads_x, blocks):
    blocks_x = blocks // heads_x
    quarter = BLOCK // heads_x
    rows_x = blocks_x * BLOCK
    chunks = heads_x * blocks_x
    pieces = G * 2 * BLOCK // 16
    ppr = relays(seq, pieces)[1]
    pieces2 = G * (quarter // 8) * 2
    ppr2 = relays(seq, pieces2)[1]
    v, dma = pltpu.VMEM, pltpu.SemaphoreType.DMA
    return dict(
        k=v((blocks, BLOCK, DH), BF16),
        v=v((blocks, BLOCK, DH), BF16),
        q=v((heads_x, rows_x, PAIR), BF16),
        do=v((heads_x, rows_x, PAIR), BF16),
        near=v((2, blocks_x + 2, BLOCK, DH), BF16),
        glob=v((G * 2 * BLOCK // 16, 16, DH), BF16),
        halo=v((2, 2, BLOCK, DH), BF16),
        rnd=v((blocks_x, R, BLOCK, PAIR), BF16),
        tcol=v((blocks * R, 128), I32),
        tvec=v((3, 1, 128), I32),
        tsm=pltpu.SMEM((3, 1, 128), I32),
        wvec=v((1, 128), I32),
        wbuf=v((seq, 1, 128), I32),
        wsm=pltpu.SMEM((seq, 1, 128), I32),
        rvec=v((2, 1, 128), I32),
        rsm=pltpu.SMEM((2, 1, 128), I32),
        served=v((seq, quarter, PAIR), BF16),
        fetched=v((seq, quarter, PAIR), BF16),
        picked=v((blocks_x, heads_x - 1, R, quarter, PAIR), BF16),
        cand=v((pieces, 16, DH), BF16),
        gin=v((seq, ppr, 16, DH), BF16),
        relay=v((ppr, 16, DH), BF16),
        e1=v((chunks, NEAR, BLOCK, PAIR), F32),
        dp1=v((chunks, NEAR, BLOCK, PAIR), F32),
        stats=v((chunks, 8, PAIR), F32),
        s_buf=v((NEAR, BLOCK, PAIR), F32),
        dp_buf=v((R, BLOCK, PAIR), F32),
        ds_far=v((chunks, R * BLOCK, PAIR), BF16),
        ds=v((NEAR * BLOCK, PAIR), BF16),
        p=v((NEAR, BLOCK, PAIR), BF16),
        kt=v((DH, (NEAR + R) * BLOCK), BF16),
        acc=v((R, BLOCK, PAIR), F32),
        wacc=v((blocks_x + 2 + G, BLOCK, PAIR), F32),
        dq=v((heads_x, rows_x, PAIR), BF16),
        far_out=v((heads_x, blocks_x, R, quarter, PAIR), BF16),
        far_in=v((heads_x, blocks_x, R, quarter, PAIR), BF16),
        near_out=v((heads_x, blocks_x + 2 + G, quarter, PAIR), BF16),
        near_in=v((heads_x, blocks_x + 2 + G, quarter, PAIR), BF16),
        run=v((blocks * R + 1, quarter, PAIR), F32),
        sbuf=v((seq, quarter, PAIR), BF16),
        rbuf=v((seq, quarter, PAIR), BF16),
        run2=v((seq + 1, quarter, PAIR), F32),
        edge=v((2, quarter, PAIR), BF16),
        gp=v((pieces2, 8, DH), F32),
        gin2=v((seq, ppr2, 8, DH), F32),
        relay2=v((ppr2, 8, DH), F32),
        gtot=v((pieces2, 8, DH), F32),
        fin=v((blocks, quarter, PAIR), F32),
        sem_l=dma((8,)),
        sem_w=dma((2,)),
        sem_g=dma((2,)),
        sem_b=dma((2,)),
        sem_h=dma((2,)),
        sem_q=dma((heads_x, 2)),
        sem_f=dma((2,)),
        sem_r=dma((blocks_x, 2)),
        sem_e=dma((blocks_x, 2)),
        sem_d=dma((2,)),
        sem_s=dma((2,)),
        sem_ng=dma((2,)),
        sem_nw=dma((2,)),
        sem_n=dma((2,)),
        sem_g2=dma((2,)),
        sem_b2=dma((2,)),
        sem_k=dma((2,)),
        sem_v=dma((2,)),
    )


def kernel(seq, heads_x, names, gb_ref, rb_ref, q_hbm, do_hbm, k_hbm, v_hbm, qg, kg, vg, *scratch):
    m = types.SimpleNamespace(**dict(zip(names, scratch)))
    s = lax.axis_index("seq")
    x = lax.axis_index("head")
    blocks = m.k.shape[0]
    blocks_x = blocks // heads_x
    rows_x = blocks_x * BLOCK
    quarter = BLOCK // heads_x
    per = BLOCK // 16
    entries = blocks * R
    part = pl.ds(pl.multiple_of(x * quarter, quarter), quarter)
    own_rows = pl.ds(pl.multiple_of(x * rows_x, rows_x), rows_x)

    def peer(d):
        return lax.rem(x + d, heads_x)

    def remote(src, dst, sems, to):
        pltpu.make_async_remote_copy(
            src_ref=src, dst_ref=dst, send_sem=sems.at[0], recv_sem=sems.at[1],
            device_id=to, device_id_type=MESH,
        ).start()

    barrier = pltpu.get_barrier_semaphore()

    def greet(j):
        pl.semaphore_signal(
            barrier, inc=1, device_id=(lax.rem(s + j, seq), x), device_id_type=MESH
        )

    loop(seq, greet, 1)
    for d in range(1, heads_x):
        pl.semaphore_signal(barrier, inc=1, device_id=(s, peer(d)), device_id_type=MESH)

    local = [
        pltpu.make_async_copy(k_hbm, m.k, m.sem_l.at[0]),
        pltpu.make_async_copy(v_hbm, m.v, m.sem_l.at[1]),
        pltpu.make_async_copy(q_hbm.at[own_rows], m.q.at[x], m.sem_l.at[2]),
        pltpu.make_async_copy(do_hbm.at[own_rows], m.do.at[x], m.sem_l.at[3]),
    ]
    for copy in local:
        copy.start()

    for r in range(R):
        m.tcol[r * blocks : (r + 1) * blocks] = jnp.broadcast_to(
            rb_ref[:, r : r + 1], (blocks, 128)
        )
    column = m.tcol[...]
    owner = lax.div(column, jnp.full_like(column, blocks))
    within = column - owner * blocks
    at = lax.broadcasted_iota(I32, column.shape, 0)
    lane = lax.broadcasted_iota(I32, column.shape, 1)

    def pick(cond, value):
        return jnp.max(jnp.where(cond, value, 0), axis=0, keepdims=True)

    owner_row = pick(at == lane, owner)
    m.wvec[...] = pick(owner == lane, within)
    m.tvec[0] = owner_row
    m.tvec[1] = pick((owner == owner_row) & (at < lane), at + 1)
    m.tvec[2] = pick(owner == lane, at + 1)
    table = pltpu.make_async_copy(m.tvec, m.tsm, m.sem_l.at[4])
    table.start()
    m.wbuf[s] = m.wvec[...]
    local[0].wait()
    local[1].wait()
    for g in range(G):
        for n, ref in enumerate((m.k, m.v)):
            first = (g * 2 + n) * per
            m.cand[first : first + per] = ref[lax.rem(gb_ref[g], blocks)].reshape(per, 16, DH)
    table.wait()

    pl.semaphore_wait(barrier, seq - 1 + heads_x - 1)

    loop(
        seq,
        lambda j: remote(m.wvec, m.wbuf.at[s], m.sem_w, (lax.rem(s + j, seq), x)),
        1,
    )
    pieces = m.cand.shape[0]
    stride, ppr = relays(seq, pieces)
    count = pieces // ppr
    is_relay = lax.rem(s, stride) == 0
    mine = s // stride

    def send_cand(r):
        @pl.when(r * stride != s)
        def _():
            remote(m.cand.at[pl.ds(r * ppr, ppr)], m.gin.at[s], m.sem_g, (r * stride, x))

    loop(count, send_cand)

    @pl.when(is_relay)
    def _():
        m.gin[s] = m.cand[pl.ds(mine * ppr, ppr)]

    for d in range(1, heads_x):
        rows = pl.ds(pl.multiple_of(peer(d) * rows_x, rows_x), rows_x)
        remote(q_hbm.at[rows], m.q.at[x], m.sem_q.at[d], (s, peer(d)))
        remote(do_hbm.at[rows], m.do.at[x], m.sem_q.at[d], (s, peer(d)))
    after = (lax.rem(s + 1, seq), x)
    before = (lax.rem(s + seq - 1, seq), x)
    for n, ref in enumerate((m.k, m.v)):
        remote(ref.at[blocks - 1], m.halo.at[0, n], m.sem_h, after)
        remote(ref.at[0], m.halo.at[1, n], m.sem_h, before)

    arrived(m.wbuf.at[pl.ds(0, seq - 1)], m.sem_w.at[1])
    to_smem = pltpu.make_async_copy(m.wbuf, m.wsm, m.sem_l.at[5])
    to_smem.start()
    to_smem.wait()

    def serve(e):
        block = m.wsm[e, 0, s]
        m.served[e, :, :DH] = m.k[block, part, :]
        m.served[e, :, DH:] = m.v[block, part, :]

    loop(seq, serve)
    m.fetched[s] = m.served[s]
    loop(
        seq,
        lambda j: remote(
            m.served.at[lax.rem(s + j, seq)], m.fetched.at[s], m.sem_f, (lax.rem(s + j, seq), x)
        ),
        1,
    )

    @pl.when(is_relay)
    def _():
        arrived(m.gin.at[pl.ds(0, seq - 1)], m.sem_g.at[1])
        for i in range(ppr):
            g = (mine * ppr + i) // (2 * per)
            m.relay[i] = m.gin[lax.div(gb_ref[g], blocks), i]
        m.glob[pl.ds(mine * ppr, ppr)] = m.relay[...]
        loop(
            seq,
            lambda j: remote(
                m.relay, m.glob.at[pl.ds(mine * ppr, ppr)], m.sem_b, (lax.rem(s + j, seq), x)
            ),
            1,
        )

    asked = m.wbuf[...].reshape(seq, 128)
    at = lax.broadcasted_iota(I32, asked.shape, 0)
    lane = lax.broadcasted_iota(I32, asked.shape, 1)
    asked = jnp.max(jnp.where(lane == s, asked, 0), axis=1, keepdims=True)
    asked = jnp.broadcast_to(asked, (seq, 128))
    asked_row = jnp.max(jnp.where(at == lane, asked, -1), axis=0, keepdims=True)
    m.rvec[0] = pick((asked == asked_row) & (at < lane), at + 1)
    m.rvec[1] = pick(asked == lane, at + 1)
    table = pltpu.make_async_copy(m.rvec, m.rsm, m.sem_l.at[6])
    table.start()

    arrived(m.halo, m.sem_h.at[1])
    for i in range(blocks_x + 2):
        place = x * blocks_x + (i - 1)
        inner = jnp.clip(place, 0, blocks - 1)
        for n, ref in enumerate((m.k, m.v)):
            value = ref[inner]
            if i == 0:
                value = jnp.where(place < 0, m.halo[0, n], value)
            if i == blocks_x + 1:
                value = jnp.where(place >= blocks, m.halo[1, n], value)
            m.near[n, i] = value
    m.wacc[...] = jnp.zeros_like(m.wacc)

    @pl.when(is_relay)
    def _():
        arrived(m.glob.at[pl.ds(0, (count - 1) * ppr)], m.sem_b.at[1])

    @pl.when(jnp.logical_not(is_relay))
    def _():
        arrived(m.glob, m.sem_b.at[1])

    local[2].wait()
    local[3].wait()

    def near_block(n, b, j):
        if j < 3:
            return m.near[n, b + j]
        first = ((j - 3) * 2 + n) * per
        return m.glob[first : first + per].reshape(BLOCK, DH)

    def rows_of(b):
        return pl.ds(pl.multiple_of(b * BLOCK, BLOCK), BLOCK)

    def stacked(ref, h, b):
        return jnp.concatenate([ref[h, rows_of(b), :DH], ref[h, rows_of(b), DH:]], axis=0)

    def source(d):
        return lax.rem(x + heads_x - d, heads_x)

    def near_scores(d):
        @pl.when(d > 0)
        def _():
            arrived(m.q.at[pl.ds(0, 2)], m.sem_q.at[d, 1])

        def step(b):
            i = b * heads_x + d
            q = stacked(m.q, source(d), b)
            do = stacked(m.do, source(d), b)
            before_ok = (s + x + b) > 0
            after_ok = (seq - s + heads_x - x + blocks_x - b) > 3
            top = jnp.full((8, PAIR), NEG, F32)
            for j in range(NEAR):
                score = dot(near_block(0, b, j), q, NT)
                if j == 0:
                    score = jnp.where(before_ok, score, NEG)
                if j == 2:
                    score = jnp.where(after_ok, score, NEG)
                m.s_buf[j] = score
                top = jnp.maximum(top, fold(score, jnp.max))
            top = jnp.max(top, axis=0, keepdims=True)
            total = jnp.zeros((8, PAIR), F32)
            inner = jnp.zeros((8, PAIR), F32)
            for j in range(NEAR):
                dp = dot(near_block(1, b, j), do, NT)
                e = jnp.exp2((m.s_buf[j] - top) * (FACTOR * LOG2E))
                total = total + fold(e, jnp.sum)
                inner = inner + fold(e * dp, jnp.sum)
                m.e1[i, j] = e
                m.dp1[i, j] = dp
            m.stats[i, 0:1] = top
            m.stats[i, 1:2] = jnp.sum(total, axis=0, keepdims=True)
            m.stats[i, 2:3] = jnp.sum(inner, axis=0, keepdims=True)

        loop(blocks_x, step)

    loop(heads_x, near_scores)

    arrived(m.fetched.at[pl.ds(0, seq - 1)], m.sem_f.at[1])

    def hand_out(b):
        for d in range(1, heads_x):
            for j in range(R):
                m.picked[b, d - 1, j] = m.fetched[m.tsm[0, 0, j * blocks + peer(d) * blocks_x + b]]
        for j in range(R):
            m.rnd[b, j, part, :] = m.fetched[m.tsm[0, 0, j * blocks + x * blocks_x + b]]
        for d in range(1, heads_x):
            remote(m.picked.at[b, d - 1], m.rnd.at[b, :, part, :], m.sem_r.at[b], (s, peer(d)))

    loop(blocks_x, hand_out)

    lane = lax.broadcasted_iota(I32, (BLOCK, PAIR), 1)
    scale_lanes = jnp.where(lane < DH, FACTOR, 1.0)

    def far_block(b):
        arrived(m.rnd.at[b, :, pl.ds(0, (heads_x - 1) * quarter), :], m.sem_r.at[b, 1])
        m.acc[...] = jnp.zeros_like(m.acc)

        def step(d):
            i = b * heads_x + d
            q = stacked(m.q, source(d), b)
            do = stacked(m.do, source(d), b)
            top1, total1, inner1 = m.stats[i, 0:1], m.stats[i, 1:2], m.stats[i, 2:3]
            top = jnp.full((8, PAIR), NEG, F32)
            for j in range(R):
                score = dot(m.rnd[b, j, :, :DH], q, NT)
                m.s_buf[j] = score
                top = jnp.maximum(top, fold(score, jnp.max))
            top = jnp.maximum(jnp.max(top, axis=0, keepdims=True), top1)
            total = jnp.zeros((8, PAIR), F32)
            inner = jnp.zeros((8, PAIR), F32)
            for j in range(R):
                dp = dot(m.rnd[b, j, :, DH:], do, NT)
                e = jnp.exp2((m.s_buf[j] - top) * (FACTOR * LOG2E))
                total = total + fold(e, jnp.sum)
                inner = inner + fold(e * dp, jnp.sum)
                m.s_buf[j] = e
                m.dp_buf[j] = dp
            shrink = jnp.exp2((top1 - top) * (FACTOR * LOG2E))
            total = jnp.sum(total, axis=0, keepdims=True) + total1 * shrink
            inner = jnp.sum(inner, axis=0, keepdims=True) + inner1 * shrink
            scale = 1.0 / total
            delta = inner * scale
            m.stats[i, 3:4] = shrink * scale
            m.stats[i, 4:5] = delta
            for j in range(R):
                a = m.s_buf[j] * scale
                ds = (a * (m.dp_buf[j] - delta)).astype(BF16)
                m.ds_far[i, j * BLOCK : (j + 1) * BLOCK] = ds
                m.acc[j, :, :DH] += dot(ds, q)
                m.acc[j, :, DH:] += dot(a.astype(BF16), do)

        loop(heads_x, step)
        for j in range(R):
            grad = (m.acc[j] * scale_lanes).astype(BF16)
            for to in range(heads_x):
                m.far_out[to, b, j] = grad[to * quarter : (to + 1) * quarter]
        m.far_in[x, b] = m.far_out[x, b]
        for d in range(1, heads_x):
            remote(m.far_out.at[peer(d), b], m.far_in.at[x, b], m.sem_e.at[b], (s, peer(d)))

    loop(blocks_x, far_block)

    m.run[0] = jnp.zeros((quarter, PAIR), F32)
    m.run2[0] = jnp.zeros((quarter, PAIR), F32)
    for b in range(blocks_x):
        arrived(m.far_out.at[pl.ds(0, heads_x - 1), b], m.sem_e.at[b, 1])
    for j in range(R):

        def chain(i, j=j):
            entry = j * blocks + i
            grad = m.far_in[i // blocks_x, lax.rem(i, blocks_x), j].astype(F32)
            m.run[entry + 1] = grad + m.run[m.tsm[1, 0, entry]]

        loop(blocks, chain)

    def fill(e):
        m.sbuf[e] = m.run[m.tsm[2, 0, e]].astype(BF16)

    loop(seq, fill)
    m.rbuf[s] = m.sbuf[s]
    loop(
        seq,
        lambda j: remote(
            m.sbuf.at[lax.rem(s + j, seq)], m.rbuf.at[s], m.sem_s, (lax.rem(s + j, seq), x)
        ),
        1,
    )

    def near_grads(b):
        for j in range(NEAR):
            m.kt[:, j * BLOCK : (j + 1) * BLOCK] = near_block(0, b, j).T
        for j in range(R):
            at = NEAR + j
            m.kt[:, at * BLOCK : (at + 1) * BLOCK] = m.rnd[b, j, :, :DH].T

        def step(d):
            i = b * heads_x + d
            h = source(d)
            q = stacked(m.q, h, b)
            do = stacked(m.do, h, b)
            scale, delta = m.stats[i, 3:4], m.stats[i, 4:5]
            for j in range(NEAR):
                a = m.e1[i, j] * scale
                m.p[j] = a.astype(BF16)
                m.ds[j * BLOCK : (j + 1) * BLOCK] = (a * (m.dp1[i, j] - delta)).astype(BF16)
            for j in range(NEAR):
                at = b + j if j < 3 else blocks_x + 2 + (j - 3)
                m.wacc[at, :, :DH] += dot(m.ds[j * BLOCK : (j + 1) * BLOCK], q)
                m.wacc[at, :, DH:] += dot(m.p[j], do)
            dqt = dot(m.kt[:, : NEAR * BLOCK], m.ds[...])
            dqt = (dqt + dot(m.kt[:, NEAR * BLOCK :], m.ds_far[i])) * FACTOR
            m.dq[h, rows_of(b), :DH] = dqt[:, :BLOCK].T.astype(BF16)
            m.dq[h, rows_of(b), DH:] = dqt[:, BLOCK:].T.astype(BF16)

        loop(heads_x, step)
        out = pl.ds(pl.multiple_of(x * rows_x + b * BLOCK, BLOCK), BLOCK)
        for d in range(1, heads_x):
            remote(m.dq.at[peer(d), rows_of(b)], qg.at[out], m.sem_d, (s, peer(d)))
        pltpu.make_async_copy(m.dq.at[x, rows_of(b)], qg.at[out], m.sem_l.at[7]).start()

    loop(blocks_x, near_grads)
    near_slots = blocks_x + 2
    for j in list(range(near_slots, near_slots + G)) + list(range(near_slots)):
        grad = (m.wacc[j] * scale_lanes).astype(BF16)
        for to in range(heads_x):
            m.near_out[to, j] = grad[to * quarter : (to + 1) * quarter]
    glob_part = pl.ds(near_slots, G)
    near_part = pl.ds(0, near_slots)
    for d in range(1, heads_x):
        remote(
            m.near_out.at[peer(d), glob_part], m.near_in.at[x, glob_part], m.sem_ng, (s, peer(d))
        )
    for d in range(1, heads_x):
        remote(
            m.near_out.at[peer(d), near_part], m.near_in.at[x, near_part], m.sem_nw, (s, peer(d))
        )
    m.near_in[x] = m.near_out[x]

    arrived(m.near_out.at[pl.ds(0, heads_x - 1), glob_part], m.sem_ng.at[1])
    lines = quarter // 8
    for g in range(G):
        value = m.near_in[0, near_slots + g].astype(F32)
        for src in range(1, heads_x):
            value = value + m.near_in[src, near_slots + g].astype(F32)
        for c in range(lines):
            for n in range(2):
                m.gp[(g * lines + c) * 2 + n] = value[
                    c * 8 : (c + 1) * 8, n * DH : (n + 1) * DH
                ]
    pieces2 = m.gp.shape[0]
    stride2, ppr2 = relays(seq, pieces2)
    count2 = pieces2 // ppr2
    is_relay2 = lax.rem(s, stride2) == 0
    mine2 = s // stride2

    @pl.when(is_relay2)
    def _():
        m.gin2[s] = m.gp[pl.ds(mine2 * ppr2, ppr2)]

    def send_global(r):
        @pl.when(r * stride2 != s)
        def _():
            remote(m.gp.at[pl.ds(r * ppr2, ppr2)], m.gin2.at[s], m.sem_g2, (r * stride2, x))

    loop(count2, send_global)
    arrived(m.near_out.at[pl.ds(0, heads_x - 1), near_part], m.sem_nw.at[1])
    remote(m.near_in.at[0, 0], m.edge.at[1], m.sem_n, before)
    remote(m.near_in.at[heads_x - 1, blocks_x + 1], m.edge.at[0], m.sem_n, after)

    @pl.when(is_relay2)
    def _():
        arrived(m.gin2.at[pl.ds(0, seq - 1)], m.sem_g2.at[1])
        m.relay2[...] = jnp.zeros_like(m.relay2)

        def add(e):
            m.relay2[...] += m.gin2[e]

        loop(seq, add)
        m.gtot[pl.ds(mine2 * ppr2, ppr2)] = m.relay2[...]
        loop(
            seq,
            lambda j: remote(
                m.relay2, m.gtot.at[pl.ds(mine2 * ppr2, ppr2)], m.sem_b2, (lax.rem(s + j, seq), x)
            ),
            1,
        )

    arrived(m.edge, m.sem_n.at[1])

    @pl.when(is_relay2)
    def _():
        arrived(m.gtot.at[pl.ds(0, (count2 - 1) * ppr2)], m.sem_b2.at[1])

    @pl.when(jnp.logical_not(is_relay2))
    def _():
        arrived(m.gtot, m.sem_b2.at[1])

    for b in range(blocks):
        src, i = b // blocks_x, b % blocks_x
        total = m.near_in[src, 1 + i].astype(F32)
        if i == 0:
            more = m.edge[0] if src == 0 else m.near_in[src - 1, blocks_x + 1]
            total = total + more.astype(F32)
        if i == blocks_x - 1:
            more = m.edge[1] if src == heads_x - 1 else m.near_in[src + 1, 0]
            total = total + more.astype(F32)
        held = [jnp.where(gb_ref[g] == s * blocks + b, 1.0, 0.0) for g in range(G)]
        for c in range(lines):
            for n in range(2):
                value = total[c * 8 : (c + 1) * 8, n * DH : (n + 1) * DH]
                for g in range(G):
                    value = value + held[g] * m.gtot[(g * lines + c) * 2 + n]
                m.fin[b, c * 8 : (c + 1) * 8, n * DH : (n + 1) * DH] = value

    table.wait()
    arrived(m.rbuf.at[pl.ds(0, seq - 1)], m.sem_s.at[1])

    def gather(e):
        m.run2[e + 1] = m.rbuf[e].astype(F32) + m.run2[m.rsm[0, 0, e]]

    loop(seq, gather)
    for b in range(blocks):
        total = m.fin[b] + m.run2[m.rsm[1, 0, b]]
        kg[b, part, :] = total[:, :DH].astype(BF16)
        vg[b, part, :] = total[:, DH:].astype(BF16)
    for d in range(1, heads_x):
        remote(kg.at[:, part, :], kg.at[:, part, :], m.sem_k, (s, peer(d)))
        remote(vg.at[:, part, :], vg.at[:, part, :], m.sem_v, (s, peer(d)))

    others = pl.ds(0, heads_x - 1)
    arrived(m.wbuf.at[pl.ds(0, seq - 1)], m.sem_w.at[0])
    arrived(m.served.at[pl.ds(0, seq - 1)], m.sem_f.at[0])
    for d in range(1, heads_x):
        arrived(m.q.at[pl.ds(0, 2)], m.sem_q.at[d, 0])
    arrived(m.halo, m.sem_h.at[0])
    for b in range(blocks_x):
        arrived(m.picked.at[b], m.sem_r.at[b, 0])
        arrived(m.far_out.at[others, b], m.sem_e.at[b, 0])
    arrived(m.near_out.at[others, glob_part], m.sem_ng.at[0])
    arrived(m.near_out.at[others, near_part], m.sem_nw.at[0])
    arrived(m.edge, m.sem_n.at[0])
    arrived(m.rbuf.at[pl.ds(0, seq - 1)], m.sem_s.at[0])
    arrived(m.dq.at[others], m.sem_d.at[0])
    arrived(m.dq.at[others], m.sem_d.at[1])
    arrived(m.dq.at[0], m.sem_l.at[7])

    def drain(relay, count, gin, send_sem, relay_sem):
        @pl.when(relay)
        def _():
            arrived(gin.at[pl.ds(0, seq - 1)], relay_sem.at[0])
            if count > 1:
                arrived(gin.at[pl.ds(0, count - 1)], send_sem.at[0])

        @pl.when(jnp.logical_not(relay))
        def _():
            arrived(gin.at[pl.ds(0, count)], send_sem.at[0])

    drain(is_relay, count, m.gin, m.sem_g, m.sem_b)
    drain(is_relay2, count2, m.gin2, m.sem_g2, m.sem_b2)
    rest = pl.ds(0, (heads_x - 1) * quarter)
    for sem, ref in ((m.sem_k, kg), (m.sem_v, vg)):
        arrived(ref.at[:, rest, :], sem.at[0])
        arrived(ref.at[:, rest, :], sem.at[1])


def body(query_vectors, key_vectors, value_vectors, output_grad, random_blocks, global_blocks):
    seq = lax.axis_size("seq")
    heads_x = lax.axis_size("head")
    rows, width = query_vectors.shape
    blocks = rows // BLOCK
    scratch = shapes(seq, heads_x, blocks)
    vmem = pl.BlockSpec(memory_space=pltpu.VMEM)
    anyspec = pl.BlockSpec(memory_space=pl.ANY)
    folded = jax.ShapeDtypeStruct((blocks, BLOCK, DH), BF16)
    query_grad, key_grad, value_grad = pl.pallas_call(
        functools.partial(kernel, seq, heads_x, tuple(scratch)),
        out_shape=(jax.ShapeDtypeStruct((rows, width), BF16), folded, folded),
        in_specs=[pl.BlockSpec(memory_space=pltpu.SMEM), vmem] + [anyspec] * 4,
        out_specs=(anyspec, vmem, vmem),
        scratch_shapes=tuple(scratch.values()),
        compiler_params=pltpu.CompilerParams(
            vmem_limit_bytes=60 * 2**20, collective_id=0, has_side_effects=True
        ),
        name="attention_grad",
    )(
        global_blocks,
        random_blocks,
        query_vectors,
        output_grad,
        key_vectors.reshape(blocks, BLOCK, DH),
        value_vectors.reshape(blocks, BLOCK, DH),
    )
    return query_grad, key_grad.reshape(rows, DH), value_grad.reshape(rows, DH)


def solution(mesh):
    return jax.shard_map(
        body,
        mesh=mesh,
        in_specs=(
            P("seq", "head"),
            P("seq", None),
            P("seq", None),
            P("seq", "head"),
            P("seq", None),
            P(),
        ),
        out_specs=(P("seq", "head"), P("seq", None), P("seq", None)),
        check_vma=False,
    )
```

```python
import functools
import types

import jax
import jax.numpy as jnp
from jax import lax
from jax.experimental import pallas as pl
from jax.experimental.pallas import tpu as pltpu
from jax.sharding import PartitionSpec as P

DH = 128
BLOCK = 128
R = 3
G = 2
NEAR = 3 + G
PAIR = 2 * DH
FACTOR = float(DH) ** -0.5
LOG2E = 1.4426950408889634
NEG = -1e30
NT = (((1,), (1,)), ((), ()))
F32 = jnp.float32
BF16 = jnp.bfloat16
I32 = jnp.int32
MESH = pl.DeviceIdType.MESH


def dot(a, b, dims=(((1,), (0,)), ((), ()))):
    return lax.dot_general(a, b, dims, preferred_element_type=F32)


def fold(value, op):
    return op(value.reshape(BLOCK // 8, 8, PAIR), axis=0)


def arrived(ref, sem):
    pltpu.make_async_copy(ref, ref, sem).wait()


def relays(seq, pieces):
    return max(1, seq // pieces), max(1, pieces // seq)


def loop(count, step, first=0):
    def run(i, carry):
        step(i)
        return carry

    lax.fori_loop(first, count, run, 0)


def shapes(seq, heads_x, blocks):
    blocks_x = blocks // heads_x
    quarter = BLOCK // heads_x
    rows_x = blocks_x * BLOCK
    chunks = heads_x * blocks_x
    pieces = G * 2 * BLOCK // 16
    ppr = relays(seq, pieces)[1]
    pieces2 = G * (quarter // 8) * 2
    ppr2 = relays(seq, pieces2)[1]
    v, dma = pltpu.VMEM, pltpu.SemaphoreType.DMA
    return dict(
        k=v((blocks, BLOCK, DH), BF16),
        v=v((blocks, BLOCK, DH), BF16),
        q=v((heads_x, rows_x, PAIR), BF16),
        do=v((heads_x, rows_x, PAIR), BF16),
        near=v((2, blocks_x + 2, BLOCK, DH), BF16),
        glob=v((G * 2 * BLOCK // 16, 16, DH), BF16),
        halo=v((2, 2, BLOCK, DH), BF16),
        rnd=v((2, blocks_x, R, BLOCK, DH), BF16),
        tcol=v((blocks * R, 128), I32),
        tvec=v((3, 1, 128), I32),
        tsm=pltpu.SMEM((3, 1, 128), I32),
        wvec=v((1, 128), I32),
        wbuf=v((seq, 1, 128), I32),
        wsm=pltpu.SMEM((seq, 1, 128), I32),
        rvec=v((2, 1, 128), I32),
        rsm=pltpu.SMEM((2, 1, 128), I32),
        served=v((2, seq, quarter, DH), BF16),
        fetched_k=v((seq, quarter, DH), BF16),
        fetched_v=v((seq, quarter, DH), BF16),
        picked=v((2, blocks_x, heads_x - 1, R, quarter, DH), BF16),
        cand=v((pieces, 16, DH), BF16),
        gin=v((seq, ppr, 16, DH), BF16),
        relay=v((ppr, 16, DH), BF16),
        e1=v((chunks, NEAR, BLOCK, PAIR), F32),
        dp1=v((chunks, NEAR, BLOCK, PAIR), F32),
        stats=v((chunks, 8, PAIR), F32),
        s_buf=v((NEAR, BLOCK, PAIR), F32),
        dp_buf=v((R, BLOCK, PAIR), F32),
        s_far=v((chunks, R, BLOCK, PAIR), F32),
        ds_far=v((chunks, (R + G) * BLOCK, PAIR), BF16),
        ds=v((3 * BLOCK, PAIR), BF16),
        p=v((3, BLOCK, PAIR), BF16),
        kt=v((DH, (NEAR + R) * BLOCK), BF16),
        acc=v((R, BLOCK, PAIR), F32),
        wacc=v((blocks_x + 2 + G, BLOCK, PAIR), F32),
        dq=v((heads_x, rows_x, PAIR), BF16),
        far_out=v((heads_x, blocks_x, R, quarter, PAIR), BF16),
        far_in=v((heads_x, blocks_x, R, quarter, PAIR), BF16),
        near_out=v((heads_x, blocks_x + 2 + G, quarter, PAIR), BF16),
        near_in=v((heads_x, blocks_x + 2 + G, quarter, PAIR), BF16),
        run=v((blocks * R + 1, quarter, PAIR), F32),
        sbuf=v((2, seq, quarter, DH), BF16),
        rbuf=v((2, seq, quarter, DH), BF16),
        run2=v((2, seq + 1, quarter, DH), F32),
        edge=v((2, quarter, PAIR), BF16),
        gp=v((pieces2, 8, DH), F32),
        gin2=v((seq, ppr2, 8, DH), F32),
        relay2=v((ppr2, 8, DH), F32),
        gtot=v((pieces2, 8, DH), F32),
        fin=v((2, blocks, quarter, DH), F32),
        sem_l=dma((8,)),
        sem_w=dma((2,)),
        sem_g=dma((2,)),
        sem_b=dma((2,)),
        sem_h=dma((2,)),
        sem_q=dma((heads_x, 2)),
        sem_f=dma((2, 2)),
        sem_r=dma((2, blocks_x, 2)),
        sem_e=dma((blocks_x, 2)),
        sem_d=dma((2,)),
        sem_s=dma((2, 2)),
        sem_ng=dma((2,)),
        sem_nw=dma((2,)),
        sem_n=dma((2,)),
        sem_g2=dma((2,)),
        sem_b2=dma((2,)),
        sem_o=dma((2, 2)),
    )


def kernel(seq, heads_x, names, gb_ref, rb_ref, q_hbm, do_hbm, k_hbm, v_hbm, qg, kg, vg, *scratch):
    m = types.SimpleNamespace(**dict(zip(names, scratch)))
    fetched = (m.fetched_k, m.fetched_v)
    s = lax.axis_index("seq")
    x = lax.axis_index("head")
    blocks = m.k.shape[0]
    blocks_x = blocks // heads_x
    rows_x = blocks_x * BLOCK
    quarter = BLOCK // heads_x
    per = BLOCK // 16
    entries = blocks * R
    part = pl.ds(pl.multiple_of(x * quarter, quarter), quarter)
    own_rows = pl.ds(pl.multiple_of(x * rows_x, rows_x), rows_x)

    def peer(d):
        return lax.rem(x + d, heads_x)

    def remote(src, dst, sems, to):
        pltpu.make_async_remote_copy(
            src_ref=src, dst_ref=dst, send_sem=sems.at[0], recv_sem=sems.at[1],
            device_id=to, device_id_type=MESH,
        ).start()

    barrier = pltpu.get_barrier_semaphore()

    def greet(j):
        pl.semaphore_signal(
            barrier, inc=1, device_id=(lax.rem(s + j, seq), x), device_id_type=MESH
        )

    loop(seq, greet, 1)
    for d in range(1, heads_x):
        pl.semaphore_signal(barrier, inc=1, device_id=(s, peer(d)), device_id_type=MESH)

    local = [
        pltpu.make_async_copy(k_hbm, m.k, m.sem_l.at[0]),
        pltpu.make_async_copy(v_hbm, m.v, m.sem_l.at[1]),
        pltpu.make_async_copy(q_hbm.at[own_rows], m.q.at[x], m.sem_l.at[2]),
        pltpu.make_async_copy(do_hbm.at[own_rows], m.do.at[x], m.sem_l.at[3]),
    ]
    for copy in local:
        copy.start()

    for r in range(R):
        m.tcol[r * blocks : (r + 1) * blocks] = jnp.broadcast_to(
            rb_ref[:, r : r + 1], (blocks, 128)
        )
    column = m.tcol[...]
    owner = lax.div(column, jnp.full_like(column, blocks))
    within = column - owner * blocks
    at = lax.broadcasted_iota(I32, column.shape, 0)
    lane = lax.broadcasted_iota(I32, column.shape, 1)

    def pick(cond, value):
        return jnp.max(jnp.where(cond, value, 0), axis=0, keepdims=True)

    owner_row = pick(at == lane, owner)
    m.wvec[...] = pick(owner == lane, within)
    m.tvec[0] = owner_row
    m.tvec[1] = pick((owner == owner_row) & (at < lane), at + 1)
    m.tvec[2] = pick(owner == lane, at + 1)
    table = pltpu.make_async_copy(m.tvec, m.tsm, m.sem_l.at[4])
    table.start()
    m.wbuf[s] = m.wvec[...]
    local[0].wait()
    local[1].wait()
    for g in range(G):
        for n, ref in enumerate((m.k, m.v)):
            first = (g * 2 + n) * per
            m.cand[first : first + per] = ref[lax.rem(gb_ref[g], blocks)].reshape(per, 16, DH)
    table.wait()

    pl.semaphore_wait(barrier, seq - 1 + heads_x - 1)

    loop(
        seq,
        lambda j: remote(m.wvec, m.wbuf.at[s], m.sem_w, (lax.rem(s + j, seq), x)),
        1,
    )
    pieces = m.cand.shape[0]
    stride, ppr = relays(seq, pieces)
    count = pieces // ppr
    is_relay = lax.rem(s, stride) == 0
    mine = s // stride

    def send_cand(r):
        @pl.when(r * stride != s)
        def _():
            remote(m.cand.at[pl.ds(r * ppr, ppr)], m.gin.at[s], m.sem_g, (r * stride, x))

    loop(count, send_cand)

    @pl.when(is_relay)
    def _():
        m.gin[s] = m.cand[pl.ds(mine * ppr, ppr)]

    for d in range(1, heads_x):
        rows = pl.ds(pl.multiple_of(peer(d) * rows_x, rows_x), rows_x)
        remote(q_hbm.at[rows], m.q.at[x], m.sem_q.at[d], (s, peer(d)))
        remote(do_hbm.at[rows], m.do.at[x], m.sem_q.at[d], (s, peer(d)))
    after = (lax.rem(s + 1, seq), x)
    before = (lax.rem(s + seq - 1, seq), x)
    for n, ref in enumerate((m.k, m.v)):
        remote(ref.at[blocks - 1], m.halo.at[0, n], m.sem_h, after)
        remote(ref.at[0], m.halo.at[1, n], m.sem_h, before)

    arrived(m.wbuf.at[pl.ds(0, seq - 1)], m.sem_w.at[1])
    to_smem = pltpu.make_async_copy(m.wbuf, m.wsm, m.sem_l.at[5])
    to_smem.start()

    @pl.when(is_relay)
    def _():
        arrived(m.gin.at[pl.ds(0, seq - 1)], m.sem_g.at[1])
        for i in range(ppr):
            g = (mine * ppr + i) // (2 * per)
            m.relay[i] = m.gin[lax.div(gb_ref[g], blocks), i]
        m.glob[pl.ds(mine * ppr, ppr)] = m.relay[...]

    def serve(n, ref):
        def step(e):
            m.served[n, e] = ref[m.wsm[e, 0, s], part, :]

        loop(seq, step)
        fetched[n][s] = m.served[n, s]

    def send_served(n):
        loop(
            seq,
            lambda j: remote(
                m.served.at[n, lax.rem(s + j, seq)],
                fetched[n].at[s],
                m.sem_f.at[n],
                (lax.rem(s + j, seq), x),
            ),
            1,
        )

    to_smem.wait()
    serve(0, m.k)

    @pl.when(is_relay)
    def _():
        loop(
            seq,
            lambda j: remote(
                m.relay, m.glob.at[pl.ds(mine * ppr, ppr)], m.sem_b, (lax.rem(s + j, seq), x)
            ),
            1,
        )

    send_served(0)
    serve(1, m.v)
    send_served(1)

    asked = m.wbuf[...].reshape(seq, 128)
    at = lax.broadcasted_iota(I32, asked.shape, 0)
    lane = lax.broadcasted_iota(I32, asked.shape, 1)
    asked = jnp.max(jnp.where(lane == s, asked, 0), axis=1, keepdims=True)
    asked = jnp.broadcast_to(asked, (seq, 128))
    asked_row = jnp.max(jnp.where(at == lane, asked, -1), axis=0, keepdims=True)
    m.rvec[0] = pick((asked == asked_row) & (at < lane), at + 1)
    m.rvec[1] = pick(asked == lane, at + 1)
    table = pltpu.make_async_copy(m.rvec, m.rsm, m.sem_l.at[6])
    table.start()

    arrived(m.halo, m.sem_h.at[1])
    for i in range(blocks_x + 2):
        place = x * blocks_x + (i - 1)
        inner = jnp.clip(place, 0, blocks - 1)
        for n, ref in enumerate((m.k, m.v)):
            value = ref[inner]
            if i == 0:
                value = jnp.where(place < 0, m.halo[0, n], value)
            if i == blocks_x + 1:
                value = jnp.where(place >= blocks, m.halo[1, n], value)
            m.near[n, i] = value
    m.wacc[...] = jnp.zeros_like(m.wacc)

    @pl.when(is_relay)
    def _():
        arrived(m.glob.at[pl.ds(0, (count - 1) * ppr)], m.sem_b.at[1])

    @pl.when(jnp.logical_not(is_relay))
    def _():
        arrived(m.glob, m.sem_b.at[1])

    local[2].wait()
    local[3].wait()

    def near_block(n, b, j):
        if j < 3:
            return m.near[n, b + j]
        first = ((j - 3) * 2 + n) * per
        return m.glob[first : first + per].reshape(BLOCK, DH)

    def rows_of(b):
        return pl.ds(pl.multiple_of(b * BLOCK, BLOCK), BLOCK)

    def stacked(ref, h, b):
        return jnp.concatenate([ref[h, rows_of(b), :DH], ref[h, rows_of(b), DH:]], axis=0)

    def source(d):
        return lax.rem(x + heads_x - d, heads_x)

    def near_scores(d):
        @pl.when(d > 0)
        def _():
            arrived(m.q.at[pl.ds(0, 2)], m.sem_q.at[d, 1])

        def step(b):
            i = b * heads_x + d
            q = stacked(m.q, source(d), b)
            do = stacked(m.do, source(d), b)
            before_ok = (s + x + b) > 0
            after_ok = (seq - s + heads_x - x + blocks_x - b) > 3
            top = jnp.full((8, PAIR), NEG, F32)
            for j in range(NEAR):
                score = dot(near_block(0, b, j), q, NT)
                if j == 0:
                    score = jnp.where(before_ok, score, NEG)
                if j == 2:
                    score = jnp.where(after_ok, score, NEG)
                m.s_buf[j] = score
                top = jnp.maximum(top, fold(score, jnp.max))
            top = jnp.max(top, axis=0, keepdims=True)
            total = jnp.zeros((8, PAIR), F32)
            inner = jnp.zeros((8, PAIR), F32)
            for j in range(NEAR):
                dp = dot(near_block(1, b, j), do, NT)
                e = jnp.exp2((m.s_buf[j] - top) * (FACTOR * LOG2E))
                total = total + fold(e, jnp.sum)
                inner = inner + fold(e * dp, jnp.sum)
                m.e1[i, j] = e
                m.dp1[i, j] = dp
            m.stats[i, 0:1] = top
            m.stats[i, 1:2] = jnp.sum(total, axis=0, keepdims=True)
            m.stats[i, 2:3] = jnp.sum(inner, axis=0, keepdims=True)

        loop(blocks_x, step)

    loop(heads_x, near_scores)

    def hand_out(n):
        arrived(fetched[n].at[pl.ds(0, seq - 1)], m.sem_f.at[n, 1])

        def step(b):
            for d in range(1, heads_x):
                for j in range(R):
                    entry = m.tsm[0, 0, j * blocks + peer(d) * blocks_x + b]
                    m.picked[n, b, d - 1, j] = fetched[n][entry]
            for j in range(R):
                entry = m.tsm[0, 0, j * blocks + x * blocks_x + b]
                m.rnd[n, b, j, part, :] = fetched[n][entry]
            for d in range(1, heads_x):
                remote(
                    m.picked.at[n, b, d - 1],
                    m.rnd.at[n, b, :, part, :],
                    m.sem_r.at[n, b],
                    (s, peer(d)),
                )

        loop(blocks_x, step)

    def rnd_ready(n, b):
        rest = pl.ds(0, (heads_x - 1) * quarter)
        arrived(m.rnd.at[n, b, :, rest, :], m.sem_r.at[n, b, 1])

    hand_out(0)

    def far_scores(b):
        rnd_ready(0, b)

        def step(d):
            i = b * heads_x + d
            q = stacked(m.q, source(d), b)
            top = jnp.full((8, PAIR), NEG, F32)
            for j in range(R):
                score = dot(m.rnd[0, b, j], q, NT)
                m.s_far[i, j] = score
                top = jnp.maximum(top, fold(score, jnp.max))
            m.stats[i, 5:6] = jnp.max(top, axis=0, keepdims=True)

        loop(heads_x, step)

    loop(blocks_x, far_scores)
    hand_out(1)

    lane = lax.broadcasted_iota(I32, (BLOCK, PAIR), 1)
    scale_lanes = jnp.where(lane < DH, FACTOR, 1.0)

    near_slots = blocks_x + 2

    def far_block(b):
        rnd_ready(1, b)
        m.acc[...] = jnp.zeros_like(m.acc)

        def step(d):
            i = b * heads_x + d
            q = stacked(m.q, source(d), b)
            do = stacked(m.do, source(d), b)
            top1, total1, inner1 = m.stats[i, 0:1], m.stats[i, 1:2], m.stats[i, 2:3]
            top = jnp.maximum(m.stats[i, 5:6], top1)
            total = jnp.zeros((8, PAIR), F32)
            inner = jnp.zeros((8, PAIR), F32)
            for j in range(R):
                dp = dot(m.rnd[1, b, j], do, NT)
                e = jnp.exp2((m.s_far[i, j] - top) * (FACTOR * LOG2E))
                total = total + fold(e, jnp.sum)
                inner = inner + fold(e * dp, jnp.sum)
                m.s_buf[j] = e
                m.dp_buf[j] = dp
            shrink = jnp.exp2((top1 - top) * (FACTOR * LOG2E))
            total = jnp.sum(total, axis=0, keepdims=True) + total1 * shrink
            inner = jnp.sum(inner, axis=0, keepdims=True) + inner1 * shrink
            scale = 1.0 / total
            delta = inner * scale
            near_scale = shrink * scale
            m.stats[i, 3:4] = near_scale
            m.stats[i, 4:5] = delta
            for j in range(R):
                a = m.s_buf[j] * scale
                ds = (a * (m.dp_buf[j] - delta)).astype(BF16)
                m.ds_far[i, j * BLOCK : (j + 1) * BLOCK] = ds
                m.acc[j, :, :DH] += dot(ds, q)
                m.acc[j, :, DH:] += dot(a.astype(BF16), do)
            for g in range(G):
                a = m.e1[i, 3 + g] * near_scale
                ds = (a * (m.dp1[i, 3 + g] - delta)).astype(BF16)
                m.ds_far[i, (R + g) * BLOCK : (R + g + 1) * BLOCK] = ds
                m.wacc[near_slots + g, :, :DH] += dot(ds, q)
                m.wacc[near_slots + g, :, DH:] += dot(a.astype(BF16), do)

        loop(heads_x, step)
        for j in range(R):
            grad = (m.acc[j] * scale_lanes).astype(BF16)
            for to in range(heads_x):
                m.far_out[to, b, j] = grad[to * quarter : (to + 1) * quarter]
        m.far_in[x, b] = m.far_out[x, b]
        for d in range(1, heads_x):
            remote(m.far_out.at[peer(d), b], m.far_in.at[x, b], m.sem_e.at[b], (s, peer(d)))

    loop(blocks_x, far_block)

    glob_part = pl.ds(near_slots, G)
    near_part = pl.ds(0, near_slots)

    def near_grad_out(j):
        grad = (m.wacc[j] * scale_lanes).astype(BF16)
        for to in range(heads_x):
            m.near_out[to, j] = grad[to * quarter : (to + 1) * quarter]
        m.near_in[x, j] = m.near_out[x, j]

    for g in range(G):
        near_grad_out(near_slots + g)
    for d in range(1, heads_x):
        remote(
            m.near_out.at[peer(d), glob_part], m.near_in.at[x, glob_part], m.sem_ng, (s, peer(d))
        )

    m.run[0] = jnp.zeros((quarter, PAIR), F32)
    for n in range(2):
        m.run2[n, 0] = jnp.zeros((quarter, DH), F32)
    for b in range(blocks_x):
        arrived(m.far_out.at[pl.ds(0, heads_x - 1), b], m.sem_e.at[b, 1])
    for j in range(R):

        def chain(i, j=j):
            entry = j * blocks + i
            grad = m.far_in[i // blocks_x, lax.rem(i, blocks_x), j].astype(F32)
            m.run[entry + 1] = grad + m.run[m.tsm[1, 0, entry]]

        loop(blocks, chain)

    def fill(e):
        value = m.run[m.tsm[2, 0, e]].astype(BF16)
        m.sbuf[0, e] = value[:, :DH]
        m.sbuf[1, e] = value[:, DH:]

    loop(seq, fill)
    for n in range(2):
        m.rbuf[n, s] = m.sbuf[n, s]

    def send_slot(n, j):
        to = lax.rem(s + j, seq)
        remote(m.sbuf.at[n, to], m.rbuf.at[n, s], m.sem_s.at[n], (to, x))

    lines = quarter // 8
    pieces2 = m.gp.shape[0]
    stride2, ppr2 = relays(seq, pieces2)
    count2 = pieces2 // ppr2
    is_relay2 = lax.rem(s, stride2) == 0
    mine2 = s // stride2
    arrived(m.near_out.at[pl.ds(0, heads_x - 1), glob_part], m.sem_ng.at[1])
    for g in range(G):
        value = m.near_in[0, near_slots + g].astype(F32)
        for src in range(1, heads_x):
            value = value + m.near_in[src, near_slots + g].astype(F32)
        for c in range(lines):
            for n in range(2):
                m.gp[(g * lines + c) * 2 + n] = value[
                    c * 8 : (c + 1) * 8, n * DH : (n + 1) * DH
                ]

    @pl.when(is_relay2)
    def _():
        m.gin2[s] = m.gp[pl.ds(mine2 * ppr2, ppr2)]

    loop(seq // 2, lambda j: send_slot(1, 2 * j + 1))

    def send_global(r):
        @pl.when(r * stride2 != s)
        def _():
            remote(m.gp.at[pl.ds(r * ppr2, ppr2)], m.gin2.at[s], m.sem_g2, (r * stride2, x))

    loop(count2, send_global)
    loop(seq // 2, lambda j: send_slot(1, 2 * j), 1)

    def near_grads(b):
        for j in range(3 + R + G):
            if j < 3:
                keys = near_block(0, b, j)
            elif j < 3 + R:
                keys = m.rnd[0, b, j - 3]
            else:
                keys = near_block(0, b, j - R)
            m.kt[:, j * BLOCK : (j + 1) * BLOCK] = keys.T

        def step(d):
            i = b * heads_x + d
            h = source(d)
            q = stacked(m.q, h, b)
            do = stacked(m.do, h, b)
            scale, delta = m.stats[i, 3:4], m.stats[i, 4:5]
            for j in range(3):
                a = m.e1[i, j] * scale
                m.p[j] = a.astype(BF16)
                m.ds[j * BLOCK : (j + 1) * BLOCK] = (a * (m.dp1[i, j] - delta)).astype(BF16)
            for j in range(3):
                m.wacc[b + j, :, :DH] += dot(m.ds[j * BLOCK : (j + 1) * BLOCK], q)
                m.wacc[b + j, :, DH:] += dot(m.p[j], do)
            dqt = dot(m.kt[:, : 3 * BLOCK], m.ds[...])
            dqt = (dqt + dot(m.kt[:, 3 * BLOCK :], m.ds_far[i])) * FACTOR
            m.dq[h, rows_of(b), :DH] = dqt[:, :BLOCK].T.astype(BF16)
            m.dq[h, rows_of(b), DH:] = dqt[:, BLOCK:].T.astype(BF16)

        loop(heads_x, step)
        out = pl.ds(pl.multiple_of(x * rows_x + b * BLOCK, BLOCK), BLOCK)
        for d in range(1, heads_x):
            remote(m.dq.at[peer(d), rows_of(b)], qg.at[out], m.sem_d, (s, peer(d)))
        pltpu.make_async_copy(m.dq.at[x, rows_of(b)], qg.at[out], m.sem_l.at[7]).start()

    loop(1, near_grads)

    @pl.when(is_relay2)
    def _():
        arrived(m.gin2.at[pl.ds(0, seq - 1)], m.sem_g2.at[1])
        m.relay2[...] = jnp.zeros_like(m.relay2)

        def add(e):
            m.relay2[...] += m.gin2[e]

        loop(seq, add)
        m.gtot[pl.ds(mine2 * ppr2, ppr2)] = m.relay2[...]
        loop(
            seq,
            lambda j: remote(
                m.relay2, m.gtot.at[pl.ds(mine2 * ppr2, ppr2)], m.sem_b2, (lax.rem(s + j, seq), x)
            ),
            1,
        )

    loop(seq // 2, lambda j: send_slot(0, 2 * j + 1))
    loop(blocks_x, near_grads, 1)
    for j in range(near_slots):
        near_grad_out(j)
    for d in range(1, heads_x):
        remote(
            m.near_out.at[peer(d), near_part], m.near_in.at[x, near_part], m.sem_nw, (s, peer(d))
        )
    arrived(m.near_out.at[pl.ds(0, heads_x - 1), near_part], m.sem_nw.at[1])
    remote(m.near_in.at[0, 0], m.edge.at[1], m.sem_n, before)
    remote(m.near_in.at[heads_x - 1, blocks_x + 1], m.edge.at[0], m.sem_n, after)
    loop(seq // 2, lambda j: send_slot(0, 2 * j), 1)
    arrived(m.edge, m.sem_n.at[1])

    @pl.when(is_relay2)
    def _():
        arrived(m.gtot.at[pl.ds(0, (count2 - 1) * ppr2)], m.sem_b2.at[1])

    @pl.when(jnp.logical_not(is_relay2))
    def _():
        arrived(m.gtot, m.sem_b2.at[1])

    for b in range(blocks):
        src, i = b // blocks_x, b % blocks_x
        total = m.near_in[src, 1 + i].astype(F32)
        if i == 0:
            more = m.edge[0] if src == 0 else m.near_in[src - 1, blocks_x + 1]
            total = total + more.astype(F32)
        if i == blocks_x - 1:
            more = m.edge[1] if src == heads_x - 1 else m.near_in[src + 1, 0]
            total = total + more.astype(F32)
        held = [jnp.where(gb_ref[g] == s * blocks + b, 1.0, 0.0) for g in range(G)]
        for c in range(lines):
            for n in range(2):
                value = total[c * 8 : (c + 1) * 8, n * DH : (n + 1) * DH]
                for g in range(G):
                    value = value + held[g] * m.gtot[(g * lines + c) * 2 + n]
                m.fin[n, b, c * 8 : (c + 1) * 8] = value

    table.wait()

    def finish(n, ref):
        arrived(m.rbuf.at[n, pl.ds(0, seq - 1)], m.sem_s.at[n, 1])

        def gather(e):
            m.run2[n, e + 1] = m.rbuf[n, e].astype(F32) + m.run2[n, m.rsm[0, 0, e]]

        loop(seq, gather)
        for b in range(blocks):
            ref[b, part, :] = (m.fin[n, b] + m.run2[n, m.rsm[1, 0, b]]).astype(BF16)
        for d in range(1, heads_x):
            remote(ref.at[:, part, :], ref.at[:, part, :], m.sem_o.at[n], (s, peer(d)))

    finish(1, vg)
    finish(0, kg)

    others = pl.ds(0, heads_x - 1)
    arrived(m.wbuf.at[pl.ds(0, seq - 1)], m.sem_w.at[0])
    for n in range(2):
        arrived(m.served.at[n, pl.ds(0, seq - 1)], m.sem_f.at[n, 0])
        arrived(m.rbuf.at[n, pl.ds(0, seq - 1)], m.sem_s.at[n, 0])
    for d in range(1, heads_x):
        arrived(m.q.at[pl.ds(0, 2)], m.sem_q.at[d, 0])
    arrived(m.halo, m.sem_h.at[0])
    for b in range(blocks_x):
        for n in range(2):
            arrived(m.picked.at[n, b], m.sem_r.at[n, b, 0])
        arrived(m.far_out.at[others, b], m.sem_e.at[b, 0])
    arrived(m.near_out.at[others, glob_part], m.sem_ng.at[0])
    arrived(m.near_out.at[others, near_part], m.sem_nw.at[0])
    arrived(m.edge, m.sem_n.at[0])
    arrived(m.dq.at[others], m.sem_d.at[0])
    arrived(m.dq.at[others], m.sem_d.at[1])
    arrived(m.dq.at[0], m.sem_l.at[7])

    def drain(relay, count, gin, send_sem, relay_sem):
        @pl.when(relay)
        def _():
            arrived(gin.at[pl.ds(0, seq - 1)], relay_sem.at[0])
            if count > 1:
                arrived(gin.at[pl.ds(0, count - 1)], send_sem.at[0])

        @pl.when(jnp.logical_not(relay))
        def _():
            arrived(gin.at[pl.ds(0, count)], send_sem.at[0])

    drain(is_relay, count, m.gin, m.sem_g, m.sem_b)
    drain(is_relay2, count2, m.gin2, m.sem_g2, m.sem_b2)
    rest = pl.ds(0, (heads_x - 1) * quarter)
    for n, ref in enumerate((kg, vg)):
        arrived(ref.at[:, rest, :], m.sem_o.at[n, 0])
        arrived(ref.at[:, rest, :], m.sem_o.at[n, 1])


def body(query_vectors, key_vectors, value_vectors, output_grad, random_blocks, global_blocks):
    seq = lax.axis_size("seq")
    heads_x = lax.axis_size("head")
    rows, width = query_vectors.shape
    blocks = rows // BLOCK
    scratch = shapes(seq, heads_x, blocks)
    vmem = pl.BlockSpec(memory_space=pltpu.VMEM)
    anyspec = pl.BlockSpec(memory_space=pl.ANY)
    folded = jax.ShapeDtypeStruct((blocks, BLOCK, DH), BF16)
    query_grad, key_grad, value_grad = pl.pallas_call(
        functools.partial(kernel, seq, heads_x, tuple(scratch)),
        out_shape=(jax.ShapeDtypeStruct((rows, width), BF16), folded, folded),
        in_specs=[pl.BlockSpec(memory_space=pltpu.SMEM), vmem] + [anyspec] * 4,
        out_specs=(vmem, vmem, vmem),
        scratch_shapes=tuple(scratch.values()),
        compiler_params=pltpu.CompilerParams(
            vmem_limit_bytes=60 * 2**20, collective_id=0, has_side_effects=True
        ),
        name="attention_grad",
    )(
        global_blocks,
        random_blocks,
        query_vectors,
        output_grad,
        key_vectors.reshape(blocks, BLOCK, DH),
        value_vectors.reshape(blocks, BLOCK, DH),
    )
    return query_grad, key_grad.reshape(rows, DH), value_grad.reshape(rows, DH)


def solution(mesh):
    return jax.shard_map(
        body,
        mesh=mesh,
        in_specs=(
            P("seq", "head"),
            P("seq", None),
            P("seq", None),
            P("seq", "head"),
            P("seq", None),
            P(),
        ),
        out_specs=(P("seq", "head"), P("seq", None), P("seq", None)),
        check_vma=False,
    )
```

```python
import functools
import types

import jax
import jax.numpy as jnp
from jax import lax
from jax.experimental import pallas as pl
from jax.experimental.pallas import tpu as pltpu
from jax.sharding import PartitionSpec as P

DH = 128
BLOCK = 128
R = 3
G = 2
NEAR = 3 + G
PAIR = 2 * DH
FACTOR = float(DH) ** -0.5
LOG2E = 1.4426950408889634
NEG = -1e30
NT = (((1,), (1,)), ((), ()))
F32 = jnp.float32
BF16 = jnp.bfloat16
I32 = jnp.int32
MESH = pl.DeviceIdType.MESH


def dot(a, b, dims=(((1,), (0,)), ((), ()))):
    return lax.dot_general(a, b, dims, preferred_element_type=F32)


def fold(value, op):
    return op(value.reshape(BLOCK // 8, 8, PAIR), axis=0)


def arrived(ref, sem):
    pltpu.make_async_copy(ref, ref, sem).wait()


def relays(seq, pieces):
    return max(1, seq // pieces), max(1, pieces // seq)


def loop(count, step, first=0):
    def run(i, carry):
        step(i)
        return carry

    lax.fori_loop(first, count, run, 0)


def shapes(seq, heads_x, blocks):
    blocks_x = blocks // heads_x
    quarter = BLOCK // heads_x
    rows_x = blocks_x * BLOCK
    chunks = heads_x * blocks_x
    pieces = G * 2 * BLOCK // 16
    ppr = relays(seq, pieces)[1]
    pieces2 = G * (quarter // 8)
    ppr2 = relays(seq, pieces2)[1]
    v, dma = pltpu.VMEM, pltpu.SemaphoreType.DMA
    return dict(
        k=v((blocks, BLOCK, DH), BF16),
        v=v((blocks, BLOCK, DH), BF16),
        q=v((heads_x, rows_x, PAIR), BF16),
        do=v((heads_x, rows_x, PAIR), BF16),
        near=v((2, blocks_x + 2, BLOCK, DH), BF16),
        glob=v((G * 2 * BLOCK // 16, 16, DH), BF16),
        halo=v((2, 2, BLOCK, DH), BF16),
        rnd=v((2, blocks_x, R, BLOCK, DH), BF16),
        tcol=v((blocks * R, 128), I32),
        tvec=v((3, 1, 128), I32),
        tsm=pltpu.SMEM((3, 1, 128), I32),
        wvec=v((1, 128), I32),
        wbuf=v((seq, 1, 128), I32),
        wsm=pltpu.SMEM((seq, 1, 128), I32),
        rvec=v((2, 1, 128), I32),
        rsm=pltpu.SMEM((2, 1, 128), I32),
        served=v((2, seq, quarter, DH), BF16),
        fetched_k=v((seq, quarter, DH), BF16),
        fetched_v=v((seq, quarter, DH), BF16),
        picked=v((2, blocks_x, heads_x - 1, R, quarter, DH), BF16),
        cand=v((pieces, 16, DH), BF16),
        gin=v((seq, ppr, 16, DH), BF16),
        relay=v((ppr, 16, DH), BF16),
        e1=v((chunks, NEAR, BLOCK, PAIR), F32),
        dp1=v((chunks, NEAR, BLOCK, PAIR), F32),
        stats=v((chunks, 8, PAIR), F32),
        s_buf=v((NEAR, BLOCK, PAIR), F32),
        dp_buf=v((R, BLOCK, PAIR), F32),
        s_far=v((chunks, R, BLOCK, PAIR), F32),
        ds_far=v((chunks, (R + G) * BLOCK, PAIR), BF16),
        ds=v((3 * BLOCK, PAIR), BF16),
        p=v((3, BLOCK, PAIR), BF16),
        kt=v((DH, (NEAR + R) * BLOCK), BF16),
        acc=v((2, R, BLOCK, DH), F32),
        wacc=v((2, blocks_x + 2 + G, BLOCK, DH), F32),
        dq=v((heads_x, rows_x, PAIR), BF16),
        far_out=v((2, heads_x, blocks_x, R, quarter, DH), BF16),
        far_in=v((2, heads_x, blocks_x, R, quarter, DH), BF16),
        near_out=v((2, heads_x, blocks_x + 2 + G, quarter, DH), BF16),
        near_in=v((2, heads_x, blocks_x + 2 + G, quarter, DH), BF16),
        run=v((2, blocks * R + 1, quarter, DH), F32),
        sbuf=v((2, seq, quarter, DH), BF16),
        rbuf=v((2, seq, quarter, DH), BF16),
        run2=v((2, seq + 1, quarter, DH), F32),
        edge=v((2, 2, quarter, DH), BF16),
        gp=v((2, pieces2, 8, DH), F32),
        gin2=v((2, seq, ppr2, 8, DH), F32),
        relay2=v((2, ppr2, 8, DH), F32),
        gtot=v((2, pieces2, 8, DH), F32),
        sem_l=dma((8,)),
        sem_w=dma((2,)),
        sem_g=dma((2,)),
        sem_b=dma((2,)),
        sem_h=dma((2,)),
        sem_q=dma((heads_x, 2)),
        sem_f=dma((2, 2)),
        sem_r=dma((2, blocks_x, 2)),
        sem_e=dma((2, blocks_x, 2)),
        sem_d=dma((2,)),
        sem_s=dma((2, 2)),
        sem_nv=dma((2,)),
        sem_ng=dma((2,)),
        sem_nw=dma((2,)),
        sem_n=dma((2, 2)),
        sem_g2=dma((2, 2)),
        sem_b2=dma((2, 2)),
        sem_o=dma((2, 2)),
    )


def kernel(seq, heads_x, names, gb_ref, rb_ref, q_hbm, do_hbm, k_hbm, v_hbm, qg, kg, vg, *scratch):
    m = types.SimpleNamespace(**dict(zip(names, scratch)))
    fetched = (m.fetched_k, m.fetched_v)
    s = lax.axis_index("seq")
    x = lax.axis_index("head")
    blocks = m.k.shape[0]
    blocks_x = blocks // heads_x
    rows_x = blocks_x * BLOCK
    quarter = BLOCK // heads_x
    per = BLOCK // 16
    entries = blocks * R
    part = pl.ds(pl.multiple_of(x * quarter, quarter), quarter)
    own_rows = pl.ds(pl.multiple_of(x * rows_x, rows_x), rows_x)

    def peer(d):
        return lax.rem(x + d, heads_x)

    def remote(src, dst, sems, to):
        pltpu.make_async_remote_copy(
            src_ref=src, dst_ref=dst, send_sem=sems.at[0], recv_sem=sems.at[1],
            device_id=to, device_id_type=MESH,
        ).start()

    barrier = pltpu.get_barrier_semaphore()

    def greet(j):
        pl.semaphore_signal(
            barrier, inc=1, device_id=(lax.rem(s + j, seq), x), device_id_type=MESH
        )

    loop(seq, greet, 1)
    for d in range(1, heads_x):
        pl.semaphore_signal(barrier, inc=1, device_id=(s, peer(d)), device_id_type=MESH)

    local = [
        pltpu.make_async_copy(k_hbm, m.k, m.sem_l.at[0]),
        pltpu.make_async_copy(v_hbm, m.v, m.sem_l.at[1]),
        pltpu.make_async_copy(q_hbm.at[own_rows], m.q.at[x], m.sem_l.at[2]),
        pltpu.make_async_copy(do_hbm.at[own_rows], m.do.at[x], m.sem_l.at[3]),
    ]
    for copy in local:
        copy.start()

    for r in range(R):
        m.tcol[r * blocks : (r + 1) * blocks] = jnp.broadcast_to(
            rb_ref[:, r : r + 1], (blocks, 128)
        )
    column = m.tcol[...]
    owner = lax.div(column, jnp.full_like(column, blocks))
    within = column - owner * blocks
    at = lax.broadcasted_iota(I32, column.shape, 0)
    lane = lax.broadcasted_iota(I32, column.shape, 1)

    def pick(cond, value):
        return jnp.max(jnp.where(cond, value, 0), axis=0, keepdims=True)

    owner_row = pick(at == lane, owner)
    m.wvec[...] = pick(owner == lane, within)
    m.tvec[0] = owner_row
    m.tvec[1] = pick((owner == owner_row) & (at < lane), at + 1)
    m.tvec[2] = pick(owner == lane, at + 1)
    table = pltpu.make_async_copy(m.tvec, m.tsm, m.sem_l.at[4])
    table.start()
    m.wbuf[s] = m.wvec[...]
    local[0].wait()
    local[1].wait()
    for g in range(G):
        for n, ref in enumerate((m.k, m.v)):
            first = (g * 2 + n) * per
            m.cand[first : first + per] = ref[lax.rem(gb_ref[g], blocks)].reshape(per, 16, DH)
    table.wait()

    pl.semaphore_wait(barrier, seq - 1 + heads_x - 1)

    loop(
        seq,
        lambda j: remote(m.wvec, m.wbuf.at[s], m.sem_w, (lax.rem(s + j, seq), x)),
        1,
    )
    pieces = m.cand.shape[0]
    stride, ppr = relays(seq, pieces)
    count = pieces // ppr
    is_relay = lax.rem(s, stride) == 0
    mine = s // stride

    def send_cand(r):
        @pl.when(r * stride != s)
        def _():
            remote(m.cand.at[pl.ds(r * ppr, ppr)], m.gin.at[s], m.sem_g, (r * stride, x))

    loop(count, send_cand)

    @pl.when(is_relay)
    def _():
        m.gin[s] = m.cand[pl.ds(mine * ppr, ppr)]

    for d in range(1, heads_x):
        rows = pl.ds(pl.multiple_of(peer(d) * rows_x, rows_x), rows_x)
        remote(q_hbm.at[rows], m.q.at[x], m.sem_q.at[d], (s, peer(d)))
        remote(do_hbm.at[rows], m.do.at[x], m.sem_q.at[d], (s, peer(d)))
    after = (lax.rem(s + 1, seq), x)
    before = (lax.rem(s + seq - 1, seq), x)
    for n, ref in enumerate((m.k, m.v)):
        remote(ref.at[blocks - 1], m.halo.at[0, n], m.sem_h, after)
        remote(ref.at[0], m.halo.at[1, n], m.sem_h, before)

    arrived(m.wbuf.at[pl.ds(0, seq - 1)], m.sem_w.at[1])
    to_smem = pltpu.make_async_copy(m.wbuf, m.wsm, m.sem_l.at[5])
    to_smem.start()

    @pl.when(is_relay)
    def _():
        arrived(m.gin.at[pl.ds(0, seq - 1)], m.sem_g.at[1])
        for i in range(ppr):
            g = (mine * ppr + i) // (2 * per)
            m.relay[i] = m.gin[lax.div(gb_ref[g], blocks), i]
        m.glob[pl.ds(mine * ppr, ppr)] = m.relay[...]

    def serve(n, ref):
        def step(e):
            m.served[n, e] = ref[m.wsm[e, 0, s], part, :]

        loop(seq, step)
        fetched[n][s] = m.served[n, s]

    def send_served(n):
        loop(
            seq,
            lambda j: remote(
                m.served.at[n, lax.rem(s + j, seq)],
                fetched[n].at[s],
                m.sem_f.at[n],
                (lax.rem(s + j, seq), x),
            ),
            1,
        )

    to_smem.wait()
    serve(0, m.k)

    @pl.when(is_relay)
    def _():
        loop(
            seq,
            lambda j: remote(
                m.relay, m.glob.at[pl.ds(mine * ppr, ppr)], m.sem_b, (lax.rem(s + j, seq), x)
            ),
            1,
        )

    send_served(0)
    serve(1, m.v)
    send_served(1)

    asked = m.wbuf[...].reshape(seq, 128)
    at = lax.broadcasted_iota(I32, asked.shape, 0)
    lane = lax.broadcasted_iota(I32, asked.shape, 1)
    asked = jnp.max(jnp.where(lane == s, asked, 0), axis=1, keepdims=True)
    asked = jnp.broadcast_to(asked, (seq, 128))
    asked_row = jnp.max(jnp.where(at == lane, asked, -1), axis=0, keepdims=True)
    m.rvec[0] = pick((asked == asked_row) & (at < lane), at + 1)
    m.rvec[1] = pick(asked == lane, at + 1)
    table = pltpu.make_async_copy(m.rvec, m.rsm, m.sem_l.at[6])
    table.start()

    arrived(m.halo, m.sem_h.at[1])
    for i in range(blocks_x + 2):
        place = x * blocks_x + (i - 1)
        inner = jnp.clip(place, 0, blocks - 1)
        for n, ref in enumerate((m.k, m.v)):
            value = ref[inner]
            if i == 0:
                value = jnp.where(place < 0, m.halo[0, n], value)
            if i == blocks_x + 1:
                value = jnp.where(place >= blocks, m.halo[1, n], value)
            m.near[n, i] = value
    m.wacc[...] = jnp.zeros_like(m.wacc)

    @pl.when(is_relay)
    def _():
        arrived(m.glob.at[pl.ds(0, (count - 1) * ppr)], m.sem_b.at[1])

    @pl.when(jnp.logical_not(is_relay))
    def _():
        arrived(m.glob, m.sem_b.at[1])

    local[2].wait()
    local[3].wait()

    def near_block(n, b, j):
        if j < 3:
            return m.near[n, b + j]
        first = ((j - 3) * 2 + n) * per
        return m.glob[first : first + per].reshape(BLOCK, DH)

    def rows_of(b):
        return pl.ds(pl.multiple_of(b * BLOCK, BLOCK), BLOCK)

    def stacked(ref, h, b):
        return jnp.concatenate([ref[h, rows_of(b), :DH], ref[h, rows_of(b), DH:]], axis=0)

    def source(d):
        return lax.rem(x + heads_x - d, heads_x)

    def near_scores(d):
        @pl.when(d > 0)
        def _():
            arrived(m.q.at[pl.ds(0, 2)], m.sem_q.at[d, 1])

        def step(b):
            i = b * heads_x + d
            q = stacked(m.q, source(d), b)
            do = stacked(m.do, source(d), b)
            before_ok = (s + x + b) > 0
            after_ok = (seq - s + heads_x - x + blocks_x - b) > 3
            top = jnp.full((8, PAIR), NEG, F32)
            for j in range(NEAR):
                score = dot(near_block(0, b, j), q, NT)
                if j == 0:
                    score = jnp.where(before_ok, score, NEG)
                if j == 2:
                    score = jnp.where(after_ok, score, NEG)
                m.s_buf[j] = score
                top = jnp.maximum(top, fold(score, jnp.max))
            top = jnp.max(top, axis=0, keepdims=True)
            total = jnp.zeros((8, PAIR), F32)
            inner = jnp.zeros((8, PAIR), F32)
            for j in range(NEAR):
                dp = dot(near_block(1, b, j), do, NT)
                e = jnp.exp2((m.s_buf[j] - top) * (FACTOR * LOG2E))
                total = total + fold(e, jnp.sum)
                inner = inner + fold(e * dp, jnp.sum)
                m.e1[i, j] = e
                m.dp1[i, j] = dp
            m.stats[i, 0:1] = top
            m.stats[i, 1:2] = jnp.sum(total, axis=0, keepdims=True)
            m.stats[i, 2:3] = jnp.sum(inner, axis=0, keepdims=True)

        loop(blocks_x, step)

    loop(heads_x, near_scores)

    def hand_out(n):
        arrived(fetched[n].at[pl.ds(0, seq - 1)], m.sem_f.at[n, 1])

        def step(b):
            for d in range(1, heads_x):
                for j in range(R):
                    entry = m.tsm[0, 0, j * blocks + peer(d) * blocks_x + b]
                    m.picked[n, b, d - 1, j] = fetched[n][entry]
            for j in range(R):
                entry = m.tsm[0, 0, j * blocks + x * blocks_x + b]
                m.rnd[n, b, j, part, :] = fetched[n][entry]
            for d in range(1, heads_x):
                remote(
                    m.picked.at[n, b, d - 1],
                    m.rnd.at[n, b, :, part, :],
                    m.sem_r.at[n, b],
                    (s, peer(d)),
                )

        loop(blocks_x, step)

    def rnd_ready(n, b):
        rest = pl.ds(0, (heads_x - 1) * quarter)
        arrived(m.rnd.at[n, b, :, rest, :], m.sem_r.at[n, b, 1])

    hand_out(0)
    near_slots = blocks_x + 2
    all_slots = near_slots + G
    others = pl.ds(0, heads_x - 1)

    def far_send(n, b):
        for j in range(R):
            grad = m.acc[n, j] * FACTOR if n == 0 else m.acc[n, j]
            grad = grad.astype(BF16)
            for to in range(heads_x):
                m.far_out[n, to, b, j] = grad[to * quarter : (to + 1) * quarter]
        m.far_in[n, x, b] = m.far_out[n, x, b]
        for d in range(1, heads_x):
            remote(
                m.far_out.at[n, peer(d), b], m.far_in.at[n, x, b], m.sem_e.at[n, b], (s, peer(d))
            )

    def far_probs(b):
        rnd_ready(0, b)
        m.acc[1] = jnp.zeros_like(m.acc[1])

        def step(d):
            i = b * heads_x + d
            q = stacked(m.q, source(d), b)
            do = stacked(m.do, source(d), b)
            top1, total1 = m.stats[i, 0:1], m.stats[i, 1:2]
            top = jnp.full((8, PAIR), NEG, F32)
            for j in range(R):
                score = dot(m.rnd[0, b, j], q, NT)
                m.s_buf[j] = score
                top = jnp.maximum(top, fold(score, jnp.max))
            top = jnp.maximum(jnp.max(top, axis=0, keepdims=True), top1)
            total = jnp.zeros((8, PAIR), F32)
            for j in range(R):
                e = jnp.exp2((m.s_buf[j] - top) * (FACTOR * LOG2E))
                total = total + fold(e, jnp.sum)
                m.s_buf[j] = e
            shrink = jnp.exp2((top1 - top) * (FACTOR * LOG2E))
            scale = 1.0 / (jnp.sum(total, axis=0, keepdims=True) + total1 * shrink)
            m.stats[i, 3:4] = shrink * scale
            for j in range(R):
                a = m.s_buf[j] * scale
                m.s_far[i, j] = a
                m.acc[1, j] += dot(a.astype(BF16), do)

        loop(heads_x, step)
        far_send(1, b)

    loop(blocks_x, far_probs)
    hand_out(1)

    for n in range(2):
        m.run[n, 0] = jnp.zeros((quarter, DH), F32)
        m.run2[n, 0] = jnp.zeros((quarter, DH), F32)

    def merge(n):
        for b in range(blocks_x):
            arrived(m.far_out.at[n, others, b], m.sem_e.at[n, b, 1])
        for j in range(R):

            def chain(i, j=j):
                entry = j * blocks + i
                grad = m.far_in[n, i // blocks_x, lax.rem(i, blocks_x), j].astype(F32)
                m.run[n, entry + 1] = grad + m.run[n, m.tsm[1, 0, entry]]

            loop(blocks, chain)

        def fill(e):
            m.sbuf[n, e] = m.run[n, m.tsm[2, 0, e]].astype(BF16)

        loop(seq, fill)
        m.rbuf[n, s] = m.sbuf[n, s]

    def send_slots(n):
        def step(j):
            to = lax.rem(s + j, seq)
            remote(m.sbuf.at[n, to], m.rbuf.at[n, s], m.sem_s.at[n], (to, x))

        loop(seq, step, 1)

    merge(1)
    send_slots(1)

    def near_slot(b, j):
        return b + j if j < 3 else near_slots + (j - 3)

    def near_values(b):
        def step(d):
            i = b * heads_x + d
            do = stacked(m.do, source(d), b)
            scale = m.stats[i, 3:4]
            for j in range(NEAR):
                p = (m.e1[i, j] * scale).astype(BF16)
                m.wacc[1, near_slot(b, j)] += dot(p, do)

        loop(heads_x, step)

    loop(blocks_x, near_values)

    def near_grad_out(n, j):
        grad = m.wacc[n, j] * FACTOR if n == 0 else m.wacc[n, j]
        grad = grad.astype(BF16)
        for to in range(heads_x):
            m.near_out[n, to, j] = grad[to * quarter : (to + 1) * quarter]
        m.near_in[n, x, j] = m.near_out[n, x, j]

    def near_send(n, slots, sem):
        for j in range(slots[0], slots[1]):
            near_grad_out(n, j)
        span = pl.ds(slots[0], slots[1] - slots[0])
        for d in range(1, heads_x):
            remote(
                m.near_out.at[n, peer(d), span], m.near_in.at[n, x, span], sem, (s, peer(d))
            )

    def near_arrived(n, slots, sem, way):
        span = pl.ds(slots[0], slots[1] - slots[0])
        arrived(m.near_out.at[n, others, span], sem.at[way])

    every, window, globs = (0, all_slots), (0, near_slots), (near_slots, all_slots)
    near_send(1, every, m.sem_nv)

    def far_keys(b):
        rnd_ready(1, b)
        m.acc[0] = jnp.zeros_like(m.acc[0])

        def step(d):
            i = b * heads_x + d
            q = stacked(m.q, source(d), b)
            do = stacked(m.do, source(d), b)
            near_scale = m.stats[i, 3:4]
            inner = jnp.zeros((8, PAIR), F32)
            for j in range(R):
                dp = dot(m.rnd[1, b, j], do, NT)
                inner = inner + fold(m.s_far[i, j] * dp, jnp.sum)
                m.dp_buf[j] = dp
            delta = jnp.sum(inner, axis=0, keepdims=True) + m.stats[i, 2:3] * near_scale
            m.stats[i, 4:5] = delta
            for j in range(R):
                ds = (m.s_far[i, j] * (m.dp_buf[j] - delta)).astype(BF16)
                m.ds_far[i, j * BLOCK : (j + 1) * BLOCK] = ds
                m.acc[0, j] += dot(ds, q)
            for g in range(G):
                a = m.e1[i, 3 + g] * near_scale
                ds = (a * (m.dp1[i, 3 + g] - delta)).astype(BF16)
                m.ds_far[i, (R + g) * BLOCK : (R + g + 1) * BLOCK] = ds
                m.wacc[0, near_slots + g] += dot(ds, q)

        loop(heads_x, step)
        far_send(0, b)

    loop(blocks_x, far_keys)
    near_send(0, globs, m.sem_ng)

    lines = quarter // 8
    pieces2 = m.gp.shape[1]
    stride2, ppr2 = relays(seq, pieces2)
    count2 = pieces2 // ppr2
    mine2 = s // stride2
    first_relay = (0, stride2 // 2)
    is_relay2 = [lax.rem(s, stride2) == first_relay[n] for n in range(2)]

    def global_parts(n):
        for g in range(G):
            value = m.near_in[n, 0, near_slots + g].astype(F32)
            for src in range(1, heads_x):
                value = value + m.near_in[n, src, near_slots + g].astype(F32)
            for c in range(lines):
                m.gp[n, g * lines + c] = value[c * 8 : (c + 1) * 8]

        @pl.when(is_relay2[n])
        def _():
            m.gin2[n, s] = m.gp[n, pl.ds(mine2 * ppr2, ppr2)]

        def send_global(r):
            to = r * stride2 + first_relay[n]

            @pl.when(to != s)
            def _():
                remote(
                    m.gp.at[n, pl.ds(r * ppr2, ppr2)], m.gin2.at[n, s], m.sem_g2.at[n], (to, x)
                )

        loop(count2, send_global)

    def global_totals(n):
        @pl.when(is_relay2[n])
        def _():
            arrived(m.gin2.at[n, pl.ds(0, seq - 1)], m.sem_g2.at[n, 1])
            m.relay2[n] = jnp.zeros_like(m.relay2[n])

            def add(e):
                m.relay2[n] += m.gin2[n, e]

            loop(seq, add)
            m.gtot[n, pl.ds(mine2 * ppr2, ppr2)] = m.relay2[n]
            loop(
                seq,
                lambda j: remote(
                    m.relay2.at[n],
                    m.gtot.at[n, pl.ds(mine2 * ppr2, ppr2)],
                    m.sem_b2.at[n],
                    (lax.rem(s + j, seq), x),
                ),
                1,
            )

    def send_edges(n):
        remote(m.near_in.at[n, 0, 0], m.edge.at[n, 1], m.sem_n.at[n], before)
        remote(m.near_in.at[n, heads_x - 1, blocks_x + 1], m.edge.at[n, 0], m.sem_n.at[n], after)

    near_arrived(1, every, m.sem_nv, 1)
    global_parts(1)
    send_edges(1)
    merge(0)
    near_arrived(0, globs, m.sem_ng, 1)
    global_parts(0)
    global_totals(1)
    send_slots(0)

    def near_keys(b):
        for j in range(3 + R + G):
            if j < 3:
                keys = near_block(0, b, j)
            elif j < 3 + R:
                keys = m.rnd[0, b, j - 3]
            else:
                keys = near_block(0, b, j - R)
            m.kt[:, j * BLOCK : (j + 1) * BLOCK] = keys.T

        def step(d):
            i = b * heads_x + d
            h = source(d)
            q = stacked(m.q, h, b)
            scale, delta = m.stats[i, 3:4], m.stats[i, 4:5]
            for j in range(3):
                a = m.e1[i, j] * scale
                ds = (a * (m.dp1[i, j] - delta)).astype(BF16)
                m.ds[j * BLOCK : (j + 1) * BLOCK] = ds
                m.wacc[0, b + j] += dot(ds, q)
            dqt = dot(m.kt[:, : 3 * BLOCK], m.ds[...])
            dqt = (dqt + dot(m.kt[:, 3 * BLOCK :], m.ds_far[i])) * FACTOR
            m.dq[h, rows_of(b), :DH] = dqt[:, :BLOCK].T.astype(BF16)
            m.dq[h, rows_of(b), DH:] = dqt[:, BLOCK:].T.astype(BF16)

        loop(heads_x, step)
        out = pl.ds(pl.multiple_of(x * rows_x + b * BLOCK, BLOCK), BLOCK)
        for d in range(1, heads_x):
            remote(m.dq.at[peer(d), rows_of(b)], qg.at[out], m.sem_d, (s, peer(d)))
        pltpu.make_async_copy(m.dq.at[x, rows_of(b)], qg.at[out], m.sem_l.at[7]).start()

    def finish(n, ref):
        arrived(m.edge.at[n], m.sem_n.at[n, 1])

        @pl.when(is_relay2[n])
        def _():
            arrived(m.gtot.at[n, pl.ds(0, (count2 - 1) * ppr2)], m.sem_b2.at[n, 1])

        @pl.when(jnp.logical_not(is_relay2[n]))
        def _():
            arrived(m.gtot.at[n], m.sem_b2.at[n, 1])

        arrived(m.rbuf.at[n, pl.ds(0, seq - 1)], m.sem_s.at[n, 1])

        def gather(e):
            m.run2[n, e + 1] = m.rbuf[n, e].astype(F32) + m.run2[n, m.rsm[0, 0, e]]

        loop(seq, gather)
        for b in range(blocks):
            src, i = b // blocks_x, b % blocks_x
            total = m.near_in[n, src, 1 + i].astype(F32)
            if i == 0:
                more = m.edge[n, 0] if src == 0 else m.near_in[n, src - 1, blocks_x + 1]
                total = total + more.astype(F32)
            if i == blocks_x - 1:
                more = m.edge[n, 1] if src == heads_x - 1 else m.near_in[n, src + 1, 0]
                total = total + more.astype(F32)
            total = total + m.run2[n, m.rsm[1, 0, b]]
            for g in range(G):
                held = jnp.where(gb_ref[g] == s * blocks + b, 1.0, 0.0)
                total = total + held * m.gtot[n, g * lines : (g + 1) * lines].reshape(quarter, DH)
            ref[b, part, :] = total.astype(BF16)
        for d in range(1, heads_x):
            remote(ref.at[:, part, :], ref.at[:, part, :], m.sem_o.at[n], (s, peer(d)))

    loop(1, near_keys)
    global_totals(0)
    table.wait()
    finish(1, vg)
    loop(blocks_x, near_keys, 1)
    near_send(0, window, m.sem_nw)
    near_arrived(0, window, m.sem_nw, 1)
    send_edges(0)
    finish(0, kg)

    arrived(m.wbuf.at[pl.ds(0, seq - 1)], m.sem_w.at[0])
    for n in range(2):
        arrived(m.served.at[n, pl.ds(0, seq - 1)], m.sem_f.at[n, 0])
        arrived(m.rbuf.at[n, pl.ds(0, seq - 1)], m.sem_s.at[n, 0])
    for d in range(1, heads_x):
        arrived(m.q.at[pl.ds(0, 2)], m.sem_q.at[d, 0])
    arrived(m.halo, m.sem_h.at[0])
    for b in range(blocks_x):
        for n in range(2):
            arrived(m.picked.at[n, b], m.sem_r.at[n, b, 0])
        for n in range(2):
            arrived(m.far_out.at[n, others, b], m.sem_e.at[n, b, 0])
    near_arrived(1, every, m.sem_nv, 0)
    near_arrived(0, globs, m.sem_ng, 0)
    near_arrived(0, window, m.sem_nw, 0)
    for n in range(2):
        arrived(m.edge.at[n], m.sem_n.at[n, 0])
    arrived(m.dq.at[others], m.sem_d.at[0])
    arrived(m.dq.at[others], m.sem_d.at[1])
    arrived(m.dq.at[0], m.sem_l.at[7])

    def drain(relay, count, gin, send_sem, relay_sem):
        @pl.when(relay)
        def _():
            arrived(gin.at[pl.ds(0, seq - 1)], relay_sem.at[0])
            if count > 1:
                arrived(gin.at[pl.ds(0, count - 1)], send_sem.at[0])

        @pl.when(jnp.logical_not(relay))
        def _():
            arrived(gin.at[pl.ds(0, count)], send_sem.at[0])

    drain(is_relay, count, m.gin, m.sem_g, m.sem_b)
    for n in range(2):
        drain(is_relay2[n], count2, m.gin2.at[n], m.sem_g2.at[n], m.sem_b2.at[n])
    rest = pl.ds(0, (heads_x - 1) * quarter)
    for n, ref in enumerate((kg, vg)):
        arrived(ref.at[:, rest, :], m.sem_o.at[n, 0])
        arrived(ref.at[:, rest, :], m.sem_o.at[n, 1])


def body(query_vectors, key_vectors, value_vectors, output_grad, random_blocks, global_blocks):
    seq = lax.axis_size("seq")
    heads_x = lax.axis_size("head")
    rows, width = query_vectors.shape
    blocks = rows // BLOCK
    scratch = shapes(seq, heads_x, blocks)
    vmem = pl.BlockSpec(memory_space=pltpu.VMEM)
    anyspec = pl.BlockSpec(memory_space=pl.ANY)
    folded = jax.ShapeDtypeStruct((blocks, BLOCK, DH), BF16)
    query_grad, key_grad, value_grad = pl.pallas_call(
        functools.partial(kernel, seq, heads_x, tuple(scratch)),
        out_shape=(jax.ShapeDtypeStruct((rows, width), BF16), folded, folded),
        in_specs=[pl.BlockSpec(memory_space=pltpu.SMEM), vmem] + [anyspec] * 4,
        out_specs=(vmem, vmem, vmem),
        scratch_shapes=tuple(scratch.values()),
        compiler_params=pltpu.CompilerParams(
            vmem_limit_bytes=60 * 2**20, collective_id=0, has_side_effects=True
        ),
        name="attention_grad",
    )(
        global_blocks,
        random_blocks,
        query_vectors,
        output_grad,
        key_vectors.reshape(blocks, BLOCK, DH),
        value_vectors.reshape(blocks, BLOCK, DH),
    )
    return query_grad, key_grad.reshape(rows, DH), value_grad.reshape(rows, DH)


def solution(mesh):
    return jax.shard_map(
        body,
        mesh=mesh,
        in_specs=(
            P("seq", "head"),
            P("seq", None),
            P("seq", None),
            P("seq", "head"),
            P("seq", None),
            P(),
        ),
        out_specs=(P("seq", "head"), P("seq", None), P("seq", None)),
        check_vma=False,
    )
```

```python
import functools
import types

import jax
import jax.numpy as jnp
from jax import lax
from jax.experimental import pallas as pl
from jax.experimental.pallas import tpu as pltpu
from jax.sharding import PartitionSpec as P

DH = 128
BLOCK = 128
R = 3
G = 2
NEAR = 3 + G
PAIR = 2 * DH
FACTOR = float(DH) ** -0.5
LOG2E = 1.4426950408889634
NEG = -1e30
NT = (((1,), (1,)), ((), ()))
F32 = jnp.float32
BF16 = jnp.bfloat16
I32 = jnp.int32
MESH = pl.DeviceIdType.MESH


def dot(a, b, dims=(((1,), (0,)), ((), ()))):
    return lax.dot_general(a, b, dims, preferred_element_type=F32)


def fold(value, op):
    return op(value.reshape(BLOCK // 8, 8, PAIR), axis=0)


def arrived(ref, sem):
    pltpu.make_async_copy(ref, ref, sem).wait()


def relays(seq, pieces):
    return max(1, seq // pieces), max(1, pieces // seq)


def loop(count, step, first=0):
    def run(i, carry):
        step(i)
        return carry

    lax.fori_loop(first, count, run, 0)


def shapes(seq, heads_x, blocks):
    blocks_x = blocks // heads_x
    quarter = BLOCK // heads_x
    rows_x = blocks_x * BLOCK
    chunks = heads_x * blocks_x
    pieces = G * 2 * BLOCK // 16
    ppr = relays(seq, pieces // heads_x)[1]
    pieces2 = G * (quarter // 8) * 2
    ppr2 = relays(seq, pieces2)[1]
    v, dma = pltpu.VMEM, pltpu.SemaphoreType.DMA
    return dict(
        k=v((blocks, BLOCK, DH), BF16),
        v=v((blocks, BLOCK, DH), BF16),
        q=v((heads_x, rows_x, PAIR), BF16),
        do=v((heads_x, rows_x, PAIR), BF16),
        near=v((2, blocks_x + 2, BLOCK, DH), BF16),
        glob=v((G * 2 * BLOCK // 16, 16, DH), BF16),
        halo=v((2, 2, BLOCK, DH), BF16),
        rnd=v((2, blocks_x, R, BLOCK, DH), BF16),
        tcol=v((blocks * R, 128), I32),
        tvec=v((3, 1, 128), I32),
        tsm=pltpu.SMEM((3, 1, 128), I32),
        wvec=v((1, 128), I32),
        wbuf=v((seq, 1, 128), I32),
        wsm=pltpu.SMEM((seq, 1, 128), I32),
        rvec=v((2, 1, 128), I32),
        rsm=pltpu.SMEM((2, 1, 128), I32),
        served=v((2, seq, quarter, DH), BF16),
        fetched_k=v((seq, quarter, DH), BF16),
        fetched_v=v((seq, quarter, DH), BF16),
        picked=v((2, blocks_x, heads_x - 1, R, quarter, DH), BF16),
        cand=v((pieces, 16, DH), BF16),
        gin=v((seq, ppr, 16, DH), BF16),
        relay=v((ppr, 16, DH), BF16),
        e1=v((chunks, NEAR, BLOCK, PAIR), F32),
        dp1=v((chunks, NEAR, BLOCK, PAIR), F32),
        stats=v((chunks, 8, PAIR), F32),
        s_buf=v((NEAR, BLOCK, PAIR), F32),
        dp_buf=v((R, BLOCK, PAIR), F32),
        s_far=v((chunks, R, BLOCK, PAIR), F32),
        ds_far=v((chunks, (R + G) * BLOCK, PAIR), BF16),
        ds=v((3 * BLOCK, PAIR), BF16),
        p=v((3, BLOCK, PAIR), BF16),
        kt=v((DH, (NEAR + R) * BLOCK), BF16),
        acc=v((R, BLOCK, PAIR), F32),
        wacc=v((blocks_x + 2 + G, BLOCK, PAIR), F32),
        dq=v((heads_x, rows_x, PAIR), BF16),
        far_out=v((heads_x, blocks_x, R, quarter, PAIR), BF16),
        far_in=v((heads_x, blocks_x, R, quarter, PAIR), BF16),
        near_out=v((heads_x, blocks_x + 2 + G, quarter, PAIR), BF16),
        near_in=v((heads_x, blocks_x + 2 + G, quarter, PAIR), BF16),
        run=v((blocks * R + 1, quarter, PAIR), F32),
        sbuf=v((2, seq, quarter, DH), BF16),
        rbuf=v((2, seq, quarter, DH), BF16),
        run2=v((2, seq + 1, quarter, DH), F32),
        edge=v((2, quarter, PAIR), BF16),
        gp=v((pieces2, 8, DH), F32),
        gin2=v((seq, ppr2, 8, DH), F32),
        relay2=v((ppr2, 8, DH), F32),
        gtot=v((pieces2, 8, DH), F32),
        fin=v((2, blocks, quarter, DH), F32),
        sem_l=dma((8,)),
        sem_w=dma((2,)),
        sem_g=dma((2,)),
        sem_b=dma((2,)),
        sem_x=dma((2,)),
        sem_ne=dma((2,)),
        sem_h=dma((2,)),
        sem_q=dma((heads_x, 2)),
        sem_f=dma((2, 2)),
        sem_r=dma((2, blocks_x, 2)),
        sem_e=dma((blocks_x, 2)),
        sem_d=dma((2,)),
        sem_s=dma((2, 2)),
        sem_ng=dma((2,)),
        sem_nw=dma((2,)),
        sem_n=dma((2,)),
        sem_g2=dma((2,)),
        sem_b2=dma((2,)),
        sem_o=dma((2, 2)),
    )


def kernel(seq, heads_x, names, gb_ref, rb_ref, q_hbm, do_hbm, k_hbm, v_hbm, qg, kg, vg, *scratch):
    m = types.SimpleNamespace(**dict(zip(names, scratch)))
    fetched = (m.fetched_k, m.fetched_v)
    s = lax.axis_index("seq")
    x = lax.axis_index("head")
    blocks = m.k.shape[0]
    blocks_x = blocks // heads_x
    rows_x = blocks_x * BLOCK
    quarter = BLOCK // heads_x
    per = BLOCK // 16
    entries = blocks * R
    part = pl.ds(pl.multiple_of(x * quarter, quarter), quarter)
    own_rows = pl.ds(pl.multiple_of(x * rows_x, rows_x), rows_x)

    def peer(d):
        return lax.rem(x + d, heads_x)

    def remote(src, dst, sems, to):
        pltpu.make_async_remote_copy(
            src_ref=src, dst_ref=dst, send_sem=sems.at[0], recv_sem=sems.at[1],
            device_id=to, device_id_type=MESH,
        ).start()

    barrier = pltpu.get_barrier_semaphore()

    def greet(j):
        pl.semaphore_signal(
            barrier, inc=1, device_id=(lax.rem(s + j, seq), x), device_id_type=MESH
        )

    loop(seq, greet, 1)
    for d in range(1, heads_x):
        pl.semaphore_signal(barrier, inc=1, device_id=(s, peer(d)), device_id_type=MESH)

    local = [
        pltpu.make_async_copy(k_hbm, m.k, m.sem_l.at[0]),
        pltpu.make_async_copy(v_hbm, m.v, m.sem_l.at[1]),
        pltpu.make_async_copy(q_hbm.at[own_rows], m.q.at[x], m.sem_l.at[2]),
        pltpu.make_async_copy(do_hbm.at[own_rows], m.do.at[x], m.sem_l.at[3]),
    ]
    for copy in local:
        copy.start()

    for r in range(R):
        m.tcol[r * blocks : (r + 1) * blocks] = jnp.broadcast_to(
            rb_ref[:, r : r + 1], (blocks, 128)
        )
    column = m.tcol[...]
    owner = lax.div(column, jnp.full_like(column, blocks))
    within = column - owner * blocks
    at = lax.broadcasted_iota(I32, column.shape, 0)
    lane = lax.broadcasted_iota(I32, column.shape, 1)

    def pick(cond, value):
        return jnp.max(jnp.where(cond, value, 0), axis=0, keepdims=True)

    owner_row = pick(at == lane, owner)
    m.wvec[...] = pick(owner == lane, within)
    m.tvec[0] = owner_row
    m.tvec[1] = pick((owner == owner_row) & (at < lane), at + 1)
    m.tvec[2] = pick(owner == lane, at + 1)
    table = pltpu.make_async_copy(m.tvec, m.tsm, m.sem_l.at[4])
    table.start()
    m.wbuf[s] = m.wvec[...]
    local[0].wait()
    local[1].wait()
    for g in range(G):
        for n, ref in enumerate((m.k, m.v)):
            first = (g * 2 + n) * per
            m.cand[first : first + per] = ref[lax.rem(gb_ref[g], blocks)].reshape(per, 16, DH)
    table.wait()

    pl.semaphore_wait(barrier, seq - 1 + heads_x - 1)

    loop(
        seq,
        lambda j: remote(m.wvec, m.wbuf.at[s], m.sem_w, (lax.rem(s + j, seq), x)),
        1,
    )
    pieces = m.cand.shape[0] // heads_x
    base = x * pieces
    stride, ppr = relays(seq, pieces)
    count = pieces // ppr
    is_relay = lax.rem(s, stride) == 0
    mine = s // stride

    def send_cand(r):
        @pl.when(r * stride != s)
        def _():
            remote(m.cand.at[pl.ds(base + r * ppr, ppr)], m.gin.at[s], m.sem_g, (r * stride, x))

    loop(count, send_cand)

    @pl.when(is_relay)
    def _():
        m.gin[s] = m.cand[pl.ds(base + mine * ppr, ppr)]

    for d in range(1, heads_x):
        rows = pl.ds(pl.multiple_of(peer(d) * rows_x, rows_x), rows_x)
        remote(q_hbm.at[rows], m.q.at[x], m.sem_q.at[d], (s, peer(d)))
        remote(do_hbm.at[rows], m.do.at[x], m.sem_q.at[d], (s, peer(d)))
    after = (lax.rem(s + 1, seq), x)
    before = (lax.rem(s + seq - 1, seq), x)
    for n, ref in enumerate((m.k, m.v)):
        remote(ref.at[blocks - 1], m.halo.at[0, n], m.sem_h, after)
        remote(ref.at[0], m.halo.at[1, n], m.sem_h, before)

    arrived(m.wbuf.at[pl.ds(0, seq - 1)], m.sem_w.at[1])
    to_smem = pltpu.make_async_copy(m.wbuf, m.wsm, m.sem_l.at[5])
    to_smem.start()

    @pl.when(is_relay)
    def _():
        arrived(m.gin.at[pl.ds(0, seq - 1)], m.sem_g.at[1])
        for i in range(ppr):
            g = (base + mine * ppr + i) // (2 * per)
            m.relay[i] = m.gin[lax.div(gb_ref[g], blocks), i]
        m.glob[pl.ds(base + mine * ppr, ppr)] = m.relay[...]

    def serve(n, ref):
        def step(e):
            m.served[n, e] = ref[m.wsm[e, 0, s], part, :]

        loop(seq, step)
        fetched[n][s] = m.served[n, s]

    def send_served(n):
        loop(
            seq,
            lambda j: remote(
                m.served.at[n, lax.rem(s + j, seq)],
                fetched[n].at[s],
                m.sem_f.at[n],
                (lax.rem(s + j, seq), x),
            ),
            1,
        )

    to_smem.wait()
    serve(0, m.k)

    @pl.when(is_relay)
    def _():
        loop(
            seq,
            lambda j: remote(
                m.relay,
                m.glob.at[pl.ds(base + mine * ppr, ppr)],
                m.sem_b,
                (lax.rem(s + j, seq), x),
            ),
            1,
        )

    send_served(0)
    serve(1, m.v)
    send_served(1)

    asked = m.wbuf[...].reshape(seq, 128)
    at = lax.broadcasted_iota(I32, asked.shape, 0)
    lane = lax.broadcasted_iota(I32, asked.shape, 1)
    asked = jnp.max(jnp.where(lane == s, asked, 0), axis=1, keepdims=True)
    asked = jnp.broadcast_to(asked, (seq, 128))
    asked_row = jnp.max(jnp.where(at == lane, asked, -1), axis=0, keepdims=True)
    m.rvec[0] = pick((asked == asked_row) & (at < lane), at + 1)
    m.rvec[1] = pick(asked == lane, at + 1)
    table = pltpu.make_async_copy(m.rvec, m.rsm, m.sem_l.at[6])
    table.start()

    @pl.when(is_relay)
    def _():
        arrived(m.glob.at[pl.ds(0, (count - 1) * ppr)], m.sem_b.at[1])

    @pl.when(jnp.logical_not(is_relay))
    def _():
        arrived(m.glob.at[pl.ds(0, pieces)], m.sem_b.at[1])

    plane = pl.ds(base, pieces)
    for d in range(1, heads_x):
        remote(m.glob.at[plane], m.glob.at[plane], m.sem_x, (s, peer(d)))

    arrived(m.halo, m.sem_h.at[1])
    for i in range(blocks_x + 2):
        place = x * blocks_x + (i - 1)
        inner = jnp.clip(place, 0, blocks - 1)
        for n, ref in enumerate((m.k, m.v)):
            value = ref[inner]
            if i == 0:
                value = jnp.where(place < 0, m.halo[0, n], value)
            if i == blocks_x + 1:
                value = jnp.where(place >= blocks, m.halo[1, n], value)
            m.near[n, i] = value
    m.wacc[...] = jnp.zeros_like(m.wacc)

    arrived(m.glob.at[pl.ds(0, (heads_x - 1) * pieces)], m.sem_x.at[1])
    local[2].wait()
    local[3].wait()

    def near_block(n, b, j):
        if j < 3:
            return m.near[n, b + j]
        first = ((j - 3) * 2 + n) * per
        return m.glob[first : first + per].reshape(BLOCK, DH)

    def rows_of(b):
        return pl.ds(pl.multiple_of(b * BLOCK, BLOCK), BLOCK)

    def stacked(ref, h, b):
        return jnp.concatenate([ref[h, rows_of(b), :DH], ref[h, rows_of(b), DH:]], axis=0)

    def source(d):
        return lax.rem(x + heads_x - d, heads_x)

    def near_scores(d):
        @pl.when(d > 0)
        def _():
            arrived(m.q.at[pl.ds(0, 2)], m.sem_q.at[d, 1])

        def step(b):
            i = b * heads_x + d
            q = stacked(m.q, source(d), b)
            do = stacked(m.do, source(d), b)
            before_ok = (s + x + b) > 0
            after_ok = (seq - s + heads_x - x + blocks_x - b) > 3
            top = jnp.full((8, PAIR), NEG, F32)
            for j in range(NEAR):
                score = dot(near_block(0, b, j), q, NT)
                if j == 0:
                    score = jnp.where(before_ok, score, NEG)
                if j == 2:
                    score = jnp.where(after_ok, score, NEG)
                m.s_buf[j] = score
                top = jnp.maximum(top, fold(score, jnp.max))
            top = jnp.max(top, axis=0, keepdims=True)
            total = jnp.zeros((8, PAIR), F32)
            inner = jnp.zeros((8, PAIR), F32)
            for j in range(NEAR):
                dp = dot(near_block(1, b, j), do, NT)
                e = jnp.exp2((m.s_buf[j] - top) * (FACTOR * LOG2E))
                total = total + fold(e, jnp.sum)
                inner = inner + fold(e * dp, jnp.sum)
                m.e1[i, j] = e
                m.dp1[i, j] = dp
            m.stats[i, 0:1] = top
            m.stats[i, 1:2] = jnp.sum(total, axis=0, keepdims=True)
            m.stats[i, 2:3] = jnp.sum(inner, axis=0, keepdims=True)

        loop(blocks_x, step)

    loop(heads_x, near_scores)

    def hand_out(n):
        arrived(fetched[n].at[pl.ds(0, seq - 1)], m.sem_f.at[n, 1])

        def step(b):
            for d in range(1, heads_x):
                for j in range(R):
                    entry = m.tsm[0, 0, j * blocks + peer(d) * blocks_x + b]
                    m.picked[n, b, d - 1, j] = fetched[n][entry]
            for j in range(R):
                entry = m.tsm[0, 0, j * blocks + x * blocks_x + b]
                m.rnd[n, b, j, part, :] = fetched[n][entry]
            for d in range(1, heads_x):
                remote(
                    m.picked.at[n, b, d - 1],
                    m.rnd.at[n, b, :, part, :],
                    m.sem_r.at[n, b],
                    (s, peer(d)),
                )

        loop(blocks_x, step)

    def rnd_ready(n, b):
        rest = pl.ds(0, (heads_x - 1) * quarter)
        arrived(m.rnd.at[n, b, :, rest, :], m.sem_r.at[n, b, 1])

    hand_out(0)

    def far_scores(b):
        rnd_ready(0, b)

        def step(d):
            i = b * heads_x + d
            q = stacked(m.q, source(d), b)
            top = jnp.full((8, PAIR), NEG, F32)
            for j in range(R):
                score = dot(m.rnd[0, b, j], q, NT)
                m.s_far[i, j] = score
                top = jnp.maximum(top, fold(score, jnp.max))
            m.stats[i, 5:6] = jnp.max(top, axis=0, keepdims=True)

        loop(heads_x, step)

    loop(blocks_x, far_scores)
    hand_out(1)

    lane = lax.broadcasted_iota(I32, (BLOCK, PAIR), 1)
    scale_lanes = jnp.where(lane < DH, FACTOR, 1.0)

    near_slots = blocks_x + 2

    def far_block(b):
        rnd_ready(1, b)
        m.acc[...] = jnp.zeros_like(m.acc)

        def step(d):
            i = b * heads_x + d
            q = stacked(m.q, source(d), b)
            do = stacked(m.do, source(d), b)
            top1, total1, inner1 = m.stats[i, 0:1], m.stats[i, 1:2], m.stats[i, 2:3]
            top = jnp.maximum(m.stats[i, 5:6], top1)
            total = jnp.zeros((8, PAIR), F32)
            inner = jnp.zeros((8, PAIR), F32)
            for j in range(R):
                dp = dot(m.rnd[1, b, j], do, NT)
                e = jnp.exp2((m.s_far[i, j] - top) * (FACTOR * LOG2E))
                total = total + fold(e, jnp.sum)
                inner = inner + fold(e * dp, jnp.sum)
                m.s_buf[j] = e
                m.dp_buf[j] = dp
            shrink = jnp.exp2((top1 - top) * (FACTOR * LOG2E))
            total = jnp.sum(total, axis=0, keepdims=True) + total1 * shrink
            inner = jnp.sum(inner, axis=0, keepdims=True) + inner1 * shrink
            scale = 1.0 / total
            delta = inner * scale
            near_scale = shrink * scale
            m.stats[i, 3:4] = near_scale
            m.stats[i, 4:5] = delta
            for j in range(R):
                a = m.s_buf[j] * scale
                ds = (a * (m.dp_buf[j] - delta)).astype(BF16)
                m.ds_far[i, j * BLOCK : (j + 1) * BLOCK] = ds
                m.acc[j, :, :DH] += dot(ds, q)
                m.acc[j, :, DH:] += dot(a.astype(BF16), do)
            for g in range(G):
                a = m.e1[i, 3 + g] * near_scale
                ds = (a * (m.dp1[i, 3 + g] - delta)).astype(BF16)
                m.ds_far[i, (R + g) * BLOCK : (R + g + 1) * BLOCK] = ds
                m.wacc[near_slots + g, :, :DH] += dot(ds, q)
                m.wacc[near_slots + g, :, DH:] += dot(a.astype(BF16), do)

        loop(heads_x, step)
        for j in range(R):
            grad = (m.acc[j] * scale_lanes).astype(BF16)
            for to in range(heads_x):
                m.far_out[to, b, j] = grad[to * quarter : (to + 1) * quarter]
        m.far_in[x, b] = m.far_out[x, b]
        for d in range(1, heads_x):
            remote(m.far_out.at[peer(d), b], m.far_in.at[x, b], m.sem_e.at[b], (s, peer(d)))

    loop(blocks_x, far_block)

    glob_part = pl.ds(near_slots, G)
    near_part = pl.ds(1, blocks_x)

    def near_grad_out(j):
        grad = (m.wacc[j] * scale_lanes).astype(BF16)
        for to in range(heads_x):
            m.near_out[to, j] = grad[to * quarter : (to + 1) * quarter]
        m.near_in[x, j] = m.near_out[x, j]

    for g in range(G):
        near_grad_out(near_slots + g)
    for d in range(1, heads_x):
        remote(
            m.near_out.at[peer(d), glob_part], m.near_in.at[x, glob_part], m.sem_ng, (s, peer(d))
        )

    m.run[0] = jnp.zeros((quarter, PAIR), F32)
    for n in range(2):
        m.run2[n, 0] = jnp.zeros((quarter, DH), F32)
    for b in range(blocks_x):
        arrived(m.far_out.at[pl.ds(0, heads_x - 1), b], m.sem_e.at[b, 1])
    for j in range(R):

        def chain(i, j=j):
            entry = j * blocks + i
            grad = m.far_in[i // blocks_x, lax.rem(i, blocks_x), j].astype(F32)
            m.run[entry + 1] = grad + m.run[m.tsm[1, 0, entry]]

        loop(blocks, chain)

    def fill(e):
        value = m.run[m.tsm[2, 0, e]].astype(BF16)
        m.sbuf[0, e] = value[:, :DH]
        m.sbuf[1, e] = value[:, DH:]

    loop(seq, fill)
    for n in range(2):
        m.rbuf[n, s] = m.sbuf[n, s]

    def send_slot(n, j):
        to = lax.rem(s + j, seq)
        remote(m.sbuf.at[n, to], m.rbuf.at[n, s], m.sem_s.at[n], (to, x))

    lines = quarter // 8
    pieces2 = m.gp.shape[0]
    stride2, ppr2 = relays(seq, pieces2)
    count2 = pieces2 // ppr2
    is_relay2 = lax.rem(s, stride2) == 0
    mine2 = s // stride2
    arrived(m.near_out.at[pl.ds(0, heads_x - 1), glob_part], m.sem_ng.at[1])
    for g in range(G):
        value = m.near_in[0, near_slots + g].astype(F32)
        for src in range(1, heads_x):
            value = value + m.near_in[src, near_slots + g].astype(F32)
        for c in range(lines):
            for n in range(2):
                m.gp[(g * lines + c) * 2 + n] = value[
                    c * 8 : (c + 1) * 8, n * DH : (n + 1) * DH
                ]

    @pl.when(is_relay2)
    def _():
        m.gin2[s] = m.gp[pl.ds(mine2 * ppr2, ppr2)]

    loop(seq // 2, lambda j: send_slot(1, 2 * j + 1))

    def send_global(r):
        @pl.when(r * stride2 != s)
        def _():
            remote(m.gp.at[pl.ds(r * ppr2, ppr2)], m.gin2.at[s], m.sem_g2, (r * stride2, x))

    loop(count2, send_global)
    loop(seq // 2, lambda j: send_slot(1, 2 * j), 1)

    def near_grads(b):
        for j in range(3 + R + G):
            if j < 3:
                keys = near_block(0, b, j)
            elif j < 3 + R:
                keys = m.rnd[0, b, j - 3]
            else:
                keys = near_block(0, b, j - R)
            m.kt[:, j * BLOCK : (j + 1) * BLOCK] = keys.T

        def step(d):
            i = b * heads_x + d
            h = source(d)
            q = stacked(m.q, h, b)
            do = stacked(m.do, h, b)
            scale, delta = m.stats[i, 3:4], m.stats[i, 4:5]
            for j in range(3):
                a = m.e1[i, j] * scale
                m.p[j] = a.astype(BF16)
                m.ds[j * BLOCK : (j + 1) * BLOCK] = (a * (m.dp1[i, j] - delta)).astype(BF16)
            for j in range(3):
                m.wacc[b + j, :, :DH] += dot(m.ds[j * BLOCK : (j + 1) * BLOCK], q)
                m.wacc[b + j, :, DH:] += dot(m.p[j], do)
            dqt = dot(m.kt[:, : 3 * BLOCK], m.ds[...])
            dqt = (dqt + dot(m.kt[:, 3 * BLOCK :], m.ds_far[i])) * FACTOR
            m.dq[h, rows_of(b), :DH] = dqt[:, :BLOCK].T.astype(BF16)
            m.dq[h, rows_of(b), DH:] = dqt[:, BLOCK:].T.astype(BF16)

        loop(heads_x, step)

    def send_dq(b):
        out = pl.ds(pl.multiple_of(x * rows_x + b * BLOCK, BLOCK), BLOCK)
        for d in range(1, heads_x):
            remote(m.dq.at[peer(d), rows_of(b)], qg.at[out], m.sem_d, (s, peer(d)))
        pltpu.make_async_copy(m.dq.at[x, rows_of(b)], qg.at[out], m.sem_l.at[7]).start()

    last = blocks_x - 1

    def near_all(b):
        near_grads(b)
        send_dq(b)

    loop(1, near_all)
    loop(blocks_x, near_all, max(last, 1))
    for j in (0, near_slots - 1):
        near_grad_out(j)
        for d in range(1, heads_x):
            remote(m.near_out.at[peer(d), j], m.near_in.at[x, j], m.sem_ne, (s, peer(d)))

    @pl.when(is_relay2)
    def _():
        arrived(m.gin2.at[pl.ds(0, seq - 1)], m.sem_g2.at[1])
        m.relay2[...] = jnp.zeros_like(m.relay2)

        def add(e):
            m.relay2[...] += m.gin2[e]

        loop(seq, add)
        m.gtot[pl.ds(mine2 * ppr2, ppr2)] = m.relay2[...]
        loop(
            seq,
            lambda j: remote(
                m.relay2, m.gtot.at[pl.ds(mine2 * ppr2, ppr2)], m.sem_b2, (lax.rem(s + j, seq), x)
            ),
            1,
        )

    if last > 2:
        loop(last - 1, near_all, 1)
    arrived(m.near_out.at[pl.ds(0, heads_x - 1), pl.ds(0, 2)], m.sem_ne.at[1])
    remote(m.near_in.at[0, 0], m.edge.at[1], m.sem_n, before)
    remote(m.near_in.at[heads_x - 1, blocks_x + 1], m.edge.at[0], m.sem_n, after)
    loop(seq, lambda j: send_slot(0, j), 1)
    if last > 1:
        loop(last, near_grads, last - 1)
    for j in range(1, near_slots - 1):
        near_grad_out(j)
    for d in range(1, heads_x):
        remote(
            m.near_out.at[peer(d), near_part], m.near_in.at[x, near_part], m.sem_nw, (s, peer(d))
        )
    if last > 1:
        loop(last, send_dq, last - 1)
    arrived(m.near_out.at[pl.ds(0, heads_x - 1), near_part], m.sem_nw.at[1])
    arrived(m.edge, m.sem_n.at[1])

    @pl.when(is_relay2)
    def _():
        arrived(m.gtot.at[pl.ds(0, (count2 - 1) * ppr2)], m.sem_b2.at[1])

    @pl.when(jnp.logical_not(is_relay2))
    def _():
        arrived(m.gtot, m.sem_b2.at[1])

    for b in range(blocks):
        src, i = b // blocks_x, b % blocks_x
        total = m.near_in[src, 1 + i].astype(F32)
        if i == 0:
            more = m.edge[0] if src == 0 else m.near_in[src - 1, blocks_x + 1]
            total = total + more.astype(F32)
        if i == blocks_x - 1:
            more = m.edge[1] if src == heads_x - 1 else m.near_in[src + 1, 0]
            total = total + more.astype(F32)
        held = [jnp.where(gb_ref[g] == s * blocks + b, 1.0, 0.0) for g in range(G)]
        for c in range(lines):
            for n in range(2):
                value = total[c * 8 : (c + 1) * 8, n * DH : (n + 1) * DH]
                for g in range(G):
                    value = value + held[g] * m.gtot[(g * lines + c) * 2 + n]
                m.fin[n, b, c * 8 : (c + 1) * 8] = value

    table.wait()

    def finish(n, ref):
        arrived(m.rbuf.at[n, pl.ds(0, seq - 1)], m.sem_s.at[n, 1])

        def gather(e):
            m.run2[n, e + 1] = m.rbuf[n, e].astype(F32) + m.run2[n, m.rsm[0, 0, e]]

        loop(seq, gather)
        for b in range(blocks):
            ref[b, part, :] = (m.fin[n, b] + m.run2[n, m.rsm[1, 0, b]]).astype(BF16)
        for d in range(1, heads_x):
            remote(ref.at[:, part, :], ref.at[:, part, :], m.sem_o.at[n], (s, peer(d)))

    finish(1, vg)
    finish(0, kg)

    others = pl.ds(0, heads_x - 1)
    arrived(m.wbuf.at[pl.ds(0, seq - 1)], m.sem_w.at[0])
    for n in range(2):
        arrived(m.served.at[n, pl.ds(0, seq - 1)], m.sem_f.at[n, 0])
        arrived(m.rbuf.at[n, pl.ds(0, seq - 1)], m.sem_s.at[n, 0])
    for d in range(1, heads_x):
        arrived(m.q.at[pl.ds(0, 2)], m.sem_q.at[d, 0])
    arrived(m.halo, m.sem_h.at[0])
    arrived(m.glob.at[pl.ds(0, (heads_x - 1) * pieces)], m.sem_x.at[0])
    for b in range(blocks_x):
        for n in range(2):
            arrived(m.picked.at[n, b], m.sem_r.at[n, b, 0])
        arrived(m.far_out.at[others, b], m.sem_e.at[b, 0])
    arrived(m.near_out.at[others, glob_part], m.sem_ng.at[0])
    arrived(m.near_out.at[others, near_part], m.sem_nw.at[0])
    arrived(m.near_out.at[others, pl.ds(0, 2)], m.sem_ne.at[0])
    arrived(m.edge, m.sem_n.at[0])
    arrived(m.dq.at[others], m.sem_d.at[0])
    arrived(m.dq.at[others], m.sem_d.at[1])
    arrived(m.dq.at[0], m.sem_l.at[7])

    def drain(relay, count, gin, send_sem, relay_sem):
        @pl.when(relay)
        def _():
            arrived(gin.at[pl.ds(0, seq - 1)], relay_sem.at[0])
            if count > 1:
                arrived(gin.at[pl.ds(0, count - 1)], send_sem.at[0])

        @pl.when(jnp.logical_not(relay))
        def _():
            arrived(gin.at[pl.ds(0, count)], send_sem.at[0])

    drain(is_relay, count, m.gin, m.sem_g, m.sem_b)
    drain(is_relay2, count2, m.gin2, m.sem_g2, m.sem_b2)
    rest = pl.ds(0, (heads_x - 1) * quarter)
    for n, ref in enumerate((kg, vg)):
        arrived(ref.at[:, rest, :], m.sem_o.at[n, 0])
        arrived(ref.at[:, rest, :], m.sem_o.at[n, 1])


def body(query_vectors, key_vectors, value_vectors, output_grad, random_blocks, global_blocks):
    seq = lax.axis_size("seq")
    heads_x = lax.axis_size("head")
    rows, width = query_vectors.shape
    blocks = rows // BLOCK
    scratch = shapes(seq, heads_x, blocks)
    vmem = pl.BlockSpec(memory_space=pltpu.VMEM)
    anyspec = pl.BlockSpec(memory_space=pl.ANY)
    folded = jax.ShapeDtypeStruct((blocks, BLOCK, DH), BF16)
    query_grad, key_grad, value_grad = pl.pallas_call(
        functools.partial(kernel, seq, heads_x, tuple(scratch)),
        out_shape=(jax.ShapeDtypeStruct((rows, width), BF16), folded, folded),
        in_specs=[pl.BlockSpec(memory_space=pltpu.SMEM), vmem] + [anyspec] * 4,
        out_specs=(vmem, vmem, vmem),
        scratch_shapes=tuple(scratch.values()),
        compiler_params=pltpu.CompilerParams(
            vmem_limit_bytes=60 * 2**20, collective_id=0, has_side_effects=True
        ),
        name="attention_grad",
    )(
        global_blocks,
        random_blocks,
        query_vectors,
        output_grad,
        key_vectors.reshape(blocks, BLOCK, DH),
        value_vectors.reshape(blocks, BLOCK, DH),
    )
    return query_grad, key_grad.reshape(rows, DH), value_grad.reshape(rows, DH)


def solution(mesh):
    return jax.shard_map(
        body,
        mesh=mesh,
        in_specs=(
            P("seq", "head"),
            P("seq", None),
            P("seq", None),
            P("seq", "head"),
            P("seq", None),
            P(),
        ),
        out_specs=(P("seq", "head"), P("seq", None), P("seq", None)),
        check_vma=False,
    )
```

```python
import functools
import types

import jax
import jax.numpy as jnp
from jax import lax
from jax.experimental import pallas as pl
from jax.experimental.pallas import tpu as pltpu
from jax.sharding import PartitionSpec as P

DH = 128
BLOCK = 128
R = 3
G = 2
NEAR = 3 + G
PAIR = 2 * DH
FACTOR = float(DH) ** -0.5
LOG2E = 1.4426950408889634
NEG = -1e30
NT = (((1,), (1,)), ((), ()))
F32 = jnp.float32
BF16 = jnp.bfloat16
I32 = jnp.int32
MESH = pl.DeviceIdType.MESH


def dot(a, b, dims=(((1,), (0,)), ((), ()))):
    return lax.dot_general(a, b, dims, preferred_element_type=F32)


def fold(value, op):
    return op(value.reshape(BLOCK // 8, 8, PAIR), axis=0)


def arrived(ref, sem):
    pltpu.make_async_copy(ref, ref, sem).wait()


def relays(seq, pieces):
    return max(1, seq // pieces), max(1, pieces // seq)


def unrolled(count, step):
    for i in range(count):
        step(i)


def loop(count, step, first=0):
    def run(i, carry):
        step(i)
        return carry

    lax.fori_loop(first, count, run, 0)


def shapes(seq, heads_x, blocks):
    blocks_x = blocks // heads_x
    quarter = BLOCK // heads_x
    rows_x = blocks_x * BLOCK
    chunks = heads_x * blocks_x
    pieces = G * 2 * BLOCK // 16
    ppr = relays(seq, pieces // heads_x)[1]
    pieces2 = G * (quarter // 8) * 2
    ppr2 = relays(seq, pieces2)[1]
    v, dma = pltpu.VMEM, pltpu.SemaphoreType.DMA
    return dict(
        k=v((blocks, BLOCK, DH), BF16),
        v=v((blocks, BLOCK, DH), BF16),
        q=v((heads_x, rows_x, PAIR), BF16),
        do=v((heads_x, rows_x, PAIR), BF16),
        near=v((2, blocks_x + 2, BLOCK, DH), BF16),
        glob=v((G * 2 * BLOCK // 16, 16, DH), BF16),
        halo=v((2, 2, BLOCK, DH), BF16),
        rnd=v((2, blocks_x, R, BLOCK, DH), BF16),
        tcol=v((blocks * R, 128), I32),
        tvec=v((3, 1, 128), I32),
        tsm=pltpu.SMEM((3, 1, 128), I32),
        wvec=v((1, 128), I32),
        wbuf=v((seq, 1, 128), I32),
        wsm=pltpu.SMEM((seq, 1, 128), I32),
        rvec=v((2, 1, 128), I32),
        rsm=pltpu.SMEM((2, 1, 128), I32),
        served=v((2, seq, quarter, DH), BF16),
        fetched_k=v((seq, quarter, DH), BF16),
        fetched_v=v((seq, quarter, DH), BF16),
        picked=v((2, blocks_x, heads_x - 1, R, quarter, DH), BF16),
        cand=v((pieces, 16, DH), BF16),
        gin=v((seq, ppr, 16, DH), BF16),
        relay=v((ppr, 16, DH), BF16),
        e1=v((chunks, NEAR, BLOCK, PAIR), F32),
        dp1=v((chunks, NEAR, BLOCK, PAIR), F32),
        stats=v((chunks, 8, PAIR), F32),
        dp_buf=v((heads_x, R, BLOCK, PAIR), F32),
        s_far=v((chunks, R, BLOCK, PAIR), F32),
        ds_far=v((chunks, (R + G) * BLOCK, PAIR), BF16),
        ds=v((heads_x, 3 * BLOCK, PAIR), BF16),
        p=v((heads_x, 3, BLOCK, PAIR), BF16),
        kt=v((DH, (NEAR + R) * BLOCK), BF16),
        acc=v((R, BLOCK, PAIR), F32),
        wacc=v((blocks_x + 2 + G, BLOCK, PAIR), F32),
        dq=v((heads_x, rows_x, PAIR), BF16),
        far_out=v((heads_x, blocks_x, R, quarter, PAIR), BF16),
        far_in=v((heads_x, blocks_x, R, quarter, PAIR), BF16),
        near_out=v((heads_x, blocks_x + 2 + G, quarter, PAIR), BF16),
        near_in=v((heads_x, blocks_x + 2 + G, quarter, PAIR), BF16),
        run=v((blocks * R + 1, quarter, PAIR), F32),
        sbuf=v((2, seq, quarter, DH), BF16),
        rbuf=v((2, seq, quarter, DH), BF16),
        run2=v((2, seq + 1, quarter, DH), F32),
        edge=v((2, quarter, PAIR), BF16),
        gp=v((pieces2, 8, DH), F32),
        gin2=v((seq, ppr2, 8, DH), F32),
        relay2=v((ppr2, 8, DH), F32),
        gtot=v((pieces2, 8, DH), F32),
        fin=v((2, blocks, quarter, DH), F32),
        sem_l=dma((8,)),
        sem_w=dma((2,)),
        sem_g=dma((2,)),
        sem_b=dma((2,)),
        sem_x=dma((2,)),
        sem_ne=dma((2,)),
        sem_h=dma((2,)),
        sem_q=dma((heads_x, 2)),
        sem_f=dma((2, 2)),
        sem_r=dma((2, blocks_x, 2)),
        sem_e=dma((blocks_x, 2)),
        sem_d=dma((2,)),
        sem_s=dma((2, 2)),
        sem_ng=dma((2,)),
        sem_nw=dma((2,)),
        sem_n=dma((2,)),
        sem_g2=dma((2,)),
        sem_b2=dma((2,)),
        sem_o=dma((2, 2)),
    )


def kernel(seq, heads_x, names, gb_ref, rb_ref, q_hbm, do_hbm, k_hbm, v_hbm, qg, kg, vg, *scratch):
    m = types.SimpleNamespace(**dict(zip(names, scratch)))
    fetched = (m.fetched_k, m.fetched_v)
    s = lax.axis_index("seq")
    x = lax.axis_index("head")
    blocks = m.k.shape[0]
    blocks_x = blocks // heads_x
    rows_x = blocks_x * BLOCK
    quarter = BLOCK // heads_x
    per = BLOCK // 16
    entries = blocks * R
    part = pl.ds(pl.multiple_of(x * quarter, quarter), quarter)
    own_rows = pl.ds(pl.multiple_of(x * rows_x, rows_x), rows_x)

    def peer(d):
        return lax.rem(x + d, heads_x)

    def remote(src, dst, sems, to):
        pltpu.make_async_remote_copy(
            src_ref=src, dst_ref=dst, send_sem=sems.at[0], recv_sem=sems.at[1],
            device_id=to, device_id_type=MESH,
        ).start()

    barrier = pltpu.get_barrier_semaphore()

    def greet(j):
        pl.semaphore_signal(
            barrier, inc=1, device_id=(lax.rem(s + j, seq), x), device_id_type=MESH
        )

    loop(seq, greet, 1)
    for d in range(1, heads_x):
        pl.semaphore_signal(barrier, inc=1, device_id=(s, peer(d)), device_id_type=MESH)

    local = [
        pltpu.make_async_copy(k_hbm, m.k, m.sem_l.at[0]),
        pltpu.make_async_copy(v_hbm, m.v, m.sem_l.at[1]),
        pltpu.make_async_copy(q_hbm.at[own_rows], m.q.at[x], m.sem_l.at[2]),
        pltpu.make_async_copy(do_hbm.at[own_rows], m.do.at[x], m.sem_l.at[3]),
    ]
    for copy in local:
        copy.start()

    for r in range(R):
        row = jnp.broadcast_to(rb_ref[r : r + 1, :], (blocks, blocks))
        mine = lax.broadcasted_iota(I32, row.shape, 0) == lax.broadcasted_iota(I32, row.shape, 1)
        picked = jnp.max(jnp.where(mine, row, 0), axis=1, keepdims=True)
        m.tcol[r * blocks : (r + 1) * blocks] = jnp.broadcast_to(picked, (blocks, 128))
    column = m.tcol[...]
    owner = lax.div(column, jnp.full_like(column, blocks))
    within = column - owner * blocks
    at = lax.broadcasted_iota(I32, column.shape, 0)
    lane = lax.broadcasted_iota(I32, column.shape, 1)

    def pick(cond, value):
        return jnp.max(jnp.where(cond, value, 0), axis=0, keepdims=True)

    owner_row = pick(at == lane, owner)
    m.wvec[...] = pick(owner == lane, within)
    m.tvec[0] = owner_row
    m.tvec[1] = pick((owner == owner_row) & (at < lane), at + 1)
    m.tvec[2] = pick(owner == lane, at + 1)
    table = pltpu.make_async_copy(m.tvec, m.tsm, m.sem_l.at[4])
    table.start()
    m.wbuf[s] = m.wvec[...]
    local[0].wait()
    local[1].wait()
    for g in range(G):
        for n, ref in enumerate((m.k, m.v)):
            first = (g * 2 + n) * per
            m.cand[first : first + per] = ref[lax.rem(gb_ref[g], blocks)].reshape(per, 16, DH)
    table.wait()

    pl.semaphore_wait(barrier, seq - 1 + heads_x - 1)

    loop(
        seq,
        lambda j: remote(m.wvec, m.wbuf.at[s], m.sem_w, (lax.rem(s + j, seq), x)),
        1,
    )
    pieces = m.cand.shape[0] // heads_x
    base = x * pieces
    stride, ppr = relays(seq, pieces)
    count = pieces // ppr
    is_relay = lax.rem(s, stride) == 0
    mine = s // stride

    def send_cand(r):
        @pl.when(r * stride != s)
        def _():
            remote(m.cand.at[pl.ds(base + r * ppr, ppr)], m.gin.at[s], m.sem_g, (r * stride, x))

    loop(count, send_cand)

    @pl.when(is_relay)
    def _():
        m.gin[s] = m.cand[pl.ds(base + mine * ppr, ppr)]

    for d in range(1, heads_x):
        rows = pl.ds(pl.multiple_of(peer(d) * rows_x, rows_x), rows_x)
        remote(q_hbm.at[rows], m.q.at[x], m.sem_q.at[d], (s, peer(d)))
        remote(do_hbm.at[rows], m.do.at[x], m.sem_q.at[d], (s, peer(d)))
    after = (lax.rem(s + 1, seq), x)
    before = (lax.rem(s + seq - 1, seq), x)
    for n, ref in enumerate((m.k, m.v)):
        remote(ref.at[blocks - 1], m.halo.at[0, n], m.sem_h, after)
        remote(ref.at[0], m.halo.at[1, n], m.sem_h, before)

    arrived(m.wbuf.at[pl.ds(0, seq - 1)], m.sem_w.at[1])
    to_smem = pltpu.make_async_copy(m.wbuf, m.wsm, m.sem_l.at[5])
    to_smem.start()

    @pl.when(is_relay)
    def _():
        arrived(m.gin.at[pl.ds(0, seq - 1)], m.sem_g.at[1])
        for i in range(ppr):
            g = (base + mine * ppr + i) // (2 * per)
            m.relay[i] = m.gin[lax.div(gb_ref[g], blocks), i]
        m.glob[pl.ds(base + mine * ppr, ppr)] = m.relay[...]

    def serve(n, ref):
        def step(e):
            m.served[n, e] = ref[m.wsm[e, 0, s], part, :]

        loop(seq, step)
        fetched[n][s] = m.served[n, s]

    def send_served(n):
        loop(
            seq,
            lambda j: remote(
                m.served.at[n, lax.rem(s + j, seq)],
                fetched[n].at[s],
                m.sem_f.at[n],
                (lax.rem(s + j, seq), x),
            ),
            1,
        )

    to_smem.wait()
    serve(0, m.k)

    @pl.when(is_relay)
    def _():
        loop(
            seq,
            lambda j: remote(
                m.relay,
                m.glob.at[pl.ds(base + mine * ppr, ppr)],
                m.sem_b,
                (lax.rem(s + j, seq), x),
            ),
            1,
        )

    send_served(0)
    serve(1, m.v)
    send_served(1)

    asked = m.wbuf[...].reshape(seq, 128)
    at = lax.broadcasted_iota(I32, asked.shape, 0)
    lane = lax.broadcasted_iota(I32, asked.shape, 1)
    asked = jnp.max(jnp.where(lane == s, asked, 0), axis=1, keepdims=True)
    asked = jnp.broadcast_to(asked, (seq, 128))
    asked_row = jnp.max(jnp.where(at == lane, asked, -1), axis=0, keepdims=True)
    m.rvec[0] = pick((asked == asked_row) & (at < lane), at + 1)
    m.rvec[1] = pick(asked == lane, at + 1)
    table = pltpu.make_async_copy(m.rvec, m.rsm, m.sem_l.at[6])
    table.start()

    @pl.when(is_relay)
    def _():
        arrived(m.glob.at[pl.ds(0, (count - 1) * ppr)], m.sem_b.at[1])

    @pl.when(jnp.logical_not(is_relay))
    def _():
        arrived(m.glob.at[pl.ds(0, pieces)], m.sem_b.at[1])

    plane = pl.ds(base, pieces)
    for d in range(1, heads_x):
        remote(m.glob.at[plane], m.glob.at[plane], m.sem_x, (s, peer(d)))

    arrived(m.halo, m.sem_h.at[1])
    for i in range(blocks_x + 2):
        place = x * blocks_x + (i - 1)
        inner = jnp.clip(place, 0, blocks - 1)
        for n, ref in enumerate((m.k, m.v)):
            value = ref[inner]
            if i == 0:
                value = jnp.where(place < 0, m.halo[0, n], value)
            if i == blocks_x + 1:
                value = jnp.where(place >= blocks, m.halo[1, n], value)
            m.near[n, i] = value
    m.wacc[...] = jnp.zeros_like(m.wacc)

    arrived(m.glob.at[pl.ds(0, (heads_x - 1) * pieces)], m.sem_x.at[1])
    local[2].wait()
    local[3].wait()

    def near_block(n, b, j):
        if j < 3:
            return m.near[n, b + j]
        first = ((j - 3) * 2 + n) * per
        return m.glob[first : first + per].reshape(BLOCK, DH)

    def rows_of(b):
        return pl.ds(pl.multiple_of(b * BLOCK, BLOCK), BLOCK)

    def stacked(ref, h, b):
        return jnp.concatenate([ref[h, rows_of(b), :DH], ref[h, rows_of(b), DH:]], axis=0)

    def source(d):
        return lax.rem(x + heads_x - d, heads_x)

    def near_scores(d):
        @pl.when(d > 0)
        def _():
            arrived(m.q.at[pl.ds(0, 2)], m.sem_q.at[d, 1])

        def step(b):
            i = b * heads_x + d
            q = stacked(m.q, source(d), b)
            do = stacked(m.do, source(d), b)
            before_ok = (s + x + b) > 0
            after_ok = (seq - s + heads_x - x + blocks_x - b) > 3
            top = jnp.full((8, PAIR), NEG, F32)
            for j in range(NEAR):
                score = dot(near_block(0, b, j), q, NT)
                if j == 0:
                    score = jnp.where(before_ok, score, NEG)
                if j == 2:
                    score = jnp.where(after_ok, score, NEG)
                m.e1[i, j] = score
                top = jnp.maximum(top, fold(score, jnp.max))
            top = jnp.max(top, axis=0, keepdims=True)
            total = jnp.zeros((8, PAIR), F32)
            inner = jnp.zeros((8, PAIR), F32)
            for j in range(NEAR):
                dp = dot(near_block(1, b, j), do, NT)
                e = jnp.exp2((m.e1[i, j] - top) * (FACTOR * LOG2E))
                total = total + fold(e, jnp.sum)
                inner = inner + fold(e * dp, jnp.sum)
                m.e1[i, j] = e
                m.dp1[i, j] = dp
            m.stats[i, 0:1] = top
            m.stats[i, 1:2] = jnp.sum(total, axis=0, keepdims=True)
            m.stats[i, 2:3] = jnp.sum(inner, axis=0, keepdims=True)

        unrolled(blocks_x, step)

    loop(heads_x, near_scores)

    def hand_out(n):
        arrived(fetched[n].at[pl.ds(0, seq - 1)], m.sem_f.at[n, 1])

        def step(b):
            for d in range(1, heads_x):
                for j in range(R):
                    entry = m.tsm[0, 0, j * blocks + peer(d) * blocks_x + b]
                    m.picked[n, b, d - 1, j] = fetched[n][entry]
            for j in range(R):
                entry = m.tsm[0, 0, j * blocks + x * blocks_x + b]
                m.rnd[n, b, j, part, :] = fetched[n][entry]
            for d in range(1, heads_x):
                remote(
                    m.picked.at[n, b, d - 1],
                    m.rnd.at[n, b, :, part, :],
                    m.sem_r.at[n, b],
                    (s, peer(d)),
                )

        loop(blocks_x, step)

    def rnd_ready(n, b):
        rest = pl.ds(0, (heads_x - 1) * quarter)
        arrived(m.rnd.at[n, b, :, rest, :], m.sem_r.at[n, b, 1])

    hand_out(0)

    def far_scores(b):
        rnd_ready(0, b)

        def step(d):
            i = b * heads_x + d
            q = stacked(m.q, source(d), b)
            top = jnp.full((8, PAIR), NEG, F32)
            for j in range(R):
                score = dot(m.rnd[0, b, j], q, NT)
                m.s_far[i, j] = score
                top = jnp.maximum(top, fold(score, jnp.max))
            m.stats[i, 5:6] = jnp.max(top, axis=0, keepdims=True)

        unrolled(heads_x, step)

    loop(blocks_x, far_scores)
    hand_out(1)

    lane = lax.broadcasted_iota(I32, (BLOCK, PAIR), 1)
    scale_lanes = jnp.where(lane < DH, FACTOR, 1.0)

    near_slots = blocks_x + 2

    def far_block(b):
        rnd_ready(1, b)
        m.acc[...] = jnp.zeros_like(m.acc)

        def step(d):
            i = b * heads_x + d
            q = stacked(m.q, source(d), b)
            do = stacked(m.do, source(d), b)
            top1, total1, inner1 = m.stats[i, 0:1], m.stats[i, 1:2], m.stats[i, 2:3]
            top = jnp.maximum(m.stats[i, 5:6], top1)
            total = jnp.zeros((8, PAIR), F32)
            inner = jnp.zeros((8, PAIR), F32)
            for j in range(R):
                dp = dot(m.rnd[1, b, j], do, NT)
                e = jnp.exp2((m.s_far[i, j] - top) * (FACTOR * LOG2E))
                total = total + fold(e, jnp.sum)
                inner = inner + fold(e * dp, jnp.sum)
                m.s_far[i, j] = e
                m.dp_buf[d, j] = dp
            shrink = jnp.exp2((top1 - top) * (FACTOR * LOG2E))
            total = jnp.sum(total, axis=0, keepdims=True) + total1 * shrink
            inner = jnp.sum(inner, axis=0, keepdims=True) + inner1 * shrink
            scale = 1.0 / total
            delta = inner * scale
            near_scale = shrink * scale
            m.stats[i, 3:4] = near_scale
            m.stats[i, 4:5] = delta
            for j in range(R):
                a = m.s_far[i, j] * scale
                ds = (a * (m.dp_buf[d, j] - delta)).astype(BF16)
                m.ds_far[i, j * BLOCK : (j + 1) * BLOCK] = ds
                m.acc[j, :, :DH] += dot(ds, q)
                m.acc[j, :, DH:] += dot(a.astype(BF16), do)
            for g in range(G):
                a = m.e1[i, 3 + g] * near_scale
                ds = (a * (m.dp1[i, 3 + g] - delta)).astype(BF16)
                m.ds_far[i, (R + g) * BLOCK : (R + g + 1) * BLOCK] = ds
                m.wacc[near_slots + g, :, :DH] += dot(ds, q)
                m.wacc[near_slots + g, :, DH:] += dot(a.astype(BF16), do)

        unrolled(heads_x, step)
        for j in range(R):
            grad = (m.acc[j] * scale_lanes).astype(BF16)
            for to in range(heads_x):
                m.far_out[to, b, j] = grad[to * quarter : (to + 1) * quarter]
        m.far_in[x, b] = m.far_out[x, b]
        for d in range(1, heads_x):
            remote(m.far_out.at[peer(d), b], m.far_in.at[x, b], m.sem_e.at[b], (s, peer(d)))

    loop(blocks_x, far_block)

    glob_part = pl.ds(near_slots, G)
    near_part = pl.ds(1, blocks_x)

    def near_grad_out(j):
        grad = (m.wacc[j] * scale_lanes).astype(BF16)
        for to in range(heads_x):
            m.near_out[to, j] = grad[to * quarter : (to + 1) * quarter]
        m.near_in[x, j] = m.near_out[x, j]

    for g in range(G):
        near_grad_out(near_slots + g)
    for d in range(1, heads_x):
        remote(
            m.near_out.at[peer(d), glob_part], m.near_in.at[x, glob_part], m.sem_ng, (s, peer(d))
        )

    m.run[0] = jnp.zeros((quarter, PAIR), F32)
    for n in range(2):
        m.run2[n, 0] = jnp.zeros((quarter, DH), F32)
    for b in range(blocks_x):
        arrived(m.far_out.at[pl.ds(0, heads_x - 1), b], m.sem_e.at[b, 1])
    for j in range(R):

        def chain(i, j=j):
            entry = j * blocks + i
            grad = m.far_in[i // blocks_x, lax.rem(i, blocks_x), j].astype(F32)
            m.run[entry + 1] = grad + m.run[m.tsm[1, 0, entry]]

        loop(blocks, chain)

    def fill(e):
        value = m.run[m.tsm[2, 0, e]].astype(BF16)
        m.sbuf[0, e] = value[:, :DH]
        m.sbuf[1, e] = value[:, DH:]

    loop(seq, fill)
    for n in range(2):
        m.rbuf[n, s] = m.sbuf[n, s]

    def send_slot(n, j):
        to = lax.rem(s + j, seq)
        remote(m.sbuf.at[n, to], m.rbuf.at[n, s], m.sem_s.at[n], (to, x))

    lines = quarter // 8
    pieces2 = m.gp.shape[0]
    stride2, ppr2 = relays(seq, pieces2)
    count2 = pieces2 // ppr2
    is_relay2 = lax.rem(s, stride2) == 0
    mine2 = s // stride2
    arrived(m.near_out.at[pl.ds(0, heads_x - 1), glob_part], m.sem_ng.at[1])
    for g in range(G):
        value = m.near_in[0, near_slots + g].astype(F32)
        for src in range(1, heads_x):
            value = value + m.near_in[src, near_slots + g].astype(F32)
        for c in range(lines):
            for n in range(2):
                m.gp[(g * lines + c) * 2 + n] = value[
                    c * 8 : (c + 1) * 8, n * DH : (n + 1) * DH
                ]

    @pl.when(is_relay2)
    def _():
        m.gin2[s] = m.gp[pl.ds(mine2 * ppr2, ppr2)]

    loop(seq // 2, lambda j: send_slot(1, 2 * j + 1))

    def send_global(r):
        @pl.when(r * stride2 != s)
        def _():
            remote(m.gp.at[pl.ds(r * ppr2, ppr2)], m.gin2.at[s], m.sem_g2, (r * stride2, x))

    loop(count2, send_global)
    loop(seq // 2, lambda j: send_slot(1, 2 * j), 1)

    def near_grads(b):
        for j in range(3 + R + G):
            if j < 3:
                keys = near_block(0, b, j)
            elif j < 3 + R:
                keys = m.rnd[0, b, j - 3]
            else:
                keys = near_block(0, b, j - R)
            m.kt[:, j * BLOCK : (j + 1) * BLOCK] = keys.T

        def step(d):
            i = b * heads_x + d
            h = source(d)
            q = stacked(m.q, h, b)
            do = stacked(m.do, h, b)
            scale, delta = m.stats[i, 3:4], m.stats[i, 4:5]
            for j in range(3):
                a = m.e1[i, j] * scale
                m.p[d, j] = a.astype(BF16)
                m.ds[d, j * BLOCK : (j + 1) * BLOCK] = (a * (m.dp1[i, j] - delta)).astype(BF16)
            for j in range(3):
                m.wacc[b + j, :, :DH] += dot(m.ds[d, j * BLOCK : (j + 1) * BLOCK], q)
                m.wacc[b + j, :, DH:] += dot(m.p[d, j], do)
            dqt = dot(m.kt[:, : 3 * BLOCK], m.ds[d])
            dqt = (dqt + dot(m.kt[:, 3 * BLOCK :], m.ds_far[i])) * FACTOR
            m.dq[h, rows_of(b), :DH] = dqt[:, :BLOCK].T.astype(BF16)
            m.dq[h, rows_of(b), DH:] = dqt[:, BLOCK:].T.astype(BF16)

        unrolled(heads_x, step)

    def send_dq(b):
        out = pl.ds(pl.multiple_of(x * rows_x + b * BLOCK, BLOCK), BLOCK)
        for d in range(1, heads_x):
            remote(m.dq.at[peer(d), rows_of(b)], qg.at[out], m.sem_d, (s, peer(d)))
        pltpu.make_async_copy(m.dq.at[x, rows_of(b)], qg.at[out], m.sem_l.at[7]).start()

    last = blocks_x - 1

    def near_all(b):
        near_grads(b)
        send_dq(b)

    loop(1, near_all)
    loop(blocks_x, near_all, max(last, 1))
    for j in (0, near_slots - 1):
        near_grad_out(j)
        for d in range(1, heads_x):
            remote(m.near_out.at[peer(d), j], m.near_in.at[x, j], m.sem_ne, (s, peer(d)))

    @pl.when(is_relay2)
    def _():
        arrived(m.gin2.at[pl.ds(0, seq - 1)], m.sem_g2.at[1])
        m.relay2[...] = jnp.zeros_like(m.relay2)

        def add(e):
            m.relay2[...] += m.gin2[e]

        loop(seq, add)
        m.gtot[pl.ds(mine2 * ppr2, ppr2)] = m.relay2[...]
        loop(
            seq,
            lambda j: remote(
                m.relay2, m.gtot.at[pl.ds(mine2 * ppr2, ppr2)], m.sem_b2, (lax.rem(s + j, seq), x)
            ),
            1,
        )

    if last > 2:
        loop(last - 1, near_all, 1)
    arrived(m.near_out.at[pl.ds(0, heads_x - 1), pl.ds(0, 2)], m.sem_ne.at[1])
    remote(m.near_in.at[0, 0], m.edge.at[1], m.sem_n, before)
    remote(m.near_in.at[heads_x - 1, blocks_x + 1], m.edge.at[0], m.sem_n, after)
    loop(seq, lambda j: send_slot(0, j), 1)
    if last > 1:
        loop(last, near_grads, last - 1)
    for j in range(1, near_slots - 1):
        near_grad_out(j)
    for d in range(1, heads_x):
        remote(
            m.near_out.at[peer(d), near_part], m.near_in.at[x, near_part], m.sem_nw, (s, peer(d))
        )
    if last > 1:
        loop(last, send_dq, last - 1)
    arrived(m.near_out.at[pl.ds(0, heads_x - 1), near_part], m.sem_nw.at[1])
    arrived(m.edge, m.sem_n.at[1])

    @pl.when(is_relay2)
    def _():
        arrived(m.gtot.at[pl.ds(0, (count2 - 1) * ppr2)], m.sem_b2.at[1])

    @pl.when(jnp.logical_not(is_relay2))
    def _():
        arrived(m.gtot, m.sem_b2.at[1])

    for b in range(blocks):
        src, i = b // blocks_x, b % blocks_x
        total = m.near_in[src, 1 + i].astype(F32)
        if i == 0:
            more = m.edge[0] if src == 0 else m.near_in[src - 1, blocks_x + 1]
            total = total + more.astype(F32)
        if i == blocks_x - 1:
            more = m.edge[1] if src == heads_x - 1 else m.near_in[src + 1, 0]
            total = total + more.astype(F32)
        held = [jnp.where(gb_ref[g] == s * blocks + b, 1.0, 0.0) for g in range(G)]
        for c in range(lines):
            for n in range(2):
                value = total[c * 8 : (c + 1) * 8, n * DH : (n + 1) * DH]
                for g in range(G):
                    value = value + held[g] * m.gtot[(g * lines + c) * 2 + n]
                m.fin[n, b, c * 8 : (c + 1) * 8] = value

    table.wait()

    def finish(n, ref):
        arrived(m.rbuf.at[n, pl.ds(0, seq - 1)], m.sem_s.at[n, 1])

        def gather(e):
            m.run2[n, e + 1] = m.rbuf[n, e].astype(F32) + m.run2[n, m.rsm[0, 0, e]]

        loop(seq, gather)
        for b in range(blocks):
            ref[b, part, :] = (m.fin[n, b] + m.run2[n, m.rsm[1, 0, b]]).astype(BF16)
        for d in range(1, heads_x):
            remote(ref.at[:, part, :], ref.at[:, part, :], m.sem_o.at[n], (s, peer(d)))

    finish(1, vg)
    finish(0, kg)

    others = pl.ds(0, heads_x - 1)
    arrived(m.wbuf.at[pl.ds(0, seq - 1)], m.sem_w.at[0])
    for n in range(2):
        arrived(m.served.at[n, pl.ds(0, seq - 1)], m.sem_f.at[n, 0])
        arrived(m.rbuf.at[n, pl.ds(0, seq - 1)], m.sem_s.at[n, 0])
    for d in range(1, heads_x):
        arrived(m.q.at[pl.ds(0, 2)], m.sem_q.at[d, 0])
    arrived(m.halo, m.sem_h.at[0])
    arrived(m.glob.at[pl.ds(0, (heads_x - 1) * pieces)], m.sem_x.at[0])
    for b in range(blocks_x):
        for n in range(2):
            arrived(m.picked.at[n, b], m.sem_r.at[n, b, 0])
        arrived(m.far_out.at[others, b], m.sem_e.at[b, 0])
    arrived(m.near_out.at[others, glob_part], m.sem_ng.at[0])
    arrived(m.near_out.at[others, near_part], m.sem_nw.at[0])
    arrived(m.near_out.at[others, pl.ds(0, 2)], m.sem_ne.at[0])
    arrived(m.edge, m.sem_n.at[0])
    arrived(m.dq.at[others], m.sem_d.at[0])
    arrived(m.dq.at[others], m.sem_d.at[1])
    arrived(m.dq.at[0], m.sem_l.at[7])

    def drain(relay, count, gin, send_sem, relay_sem):
        @pl.when(relay)
        def _():
            arrived(gin.at[pl.ds(0, seq - 1)], relay_sem.at[0])
            if count > 1:
                arrived(gin.at[pl.ds(0, count - 1)], send_sem.at[0])

        @pl.when(jnp.logical_not(relay))
        def _():
            arrived(gin.at[pl.ds(0, count)], send_sem.at[0])

    drain(is_relay, count, m.gin, m.sem_g, m.sem_b)
    drain(is_relay2, count2, m.gin2, m.sem_g2, m.sem_b2)
    rest = pl.ds(0, (heads_x - 1) * quarter)
    for n, ref in enumerate((kg, vg)):
        arrived(ref.at[:, rest, :], m.sem_o.at[n, 0])
        arrived(ref.at[:, rest, :], m.sem_o.at[n, 1])


def body(query_vectors, key_vectors, value_vectors, output_grad, random_blocks, global_blocks):
    seq = lax.axis_size("seq")
    heads_x = lax.axis_size("head")
    rows, width = query_vectors.shape
    blocks = rows // BLOCK
    scratch = shapes(seq, heads_x, blocks)
    vmem = pl.BlockSpec(memory_space=pltpu.VMEM)
    anyspec = pl.BlockSpec(memory_space=pl.ANY)
    folded = jax.ShapeDtypeStruct((blocks, BLOCK, DH), BF16)
    query_grad, key_grad, value_grad = pl.pallas_call(
        functools.partial(kernel, seq, heads_x, tuple(scratch)),
        out_shape=(jax.ShapeDtypeStruct((rows, width), BF16), folded, folded),
        in_specs=[pl.BlockSpec(memory_space=pltpu.SMEM), vmem] + [anyspec] * 4,
        out_specs=(vmem, vmem, vmem),
        scratch_shapes=tuple(scratch.values()),
        compiler_params=pltpu.CompilerParams(
            vmem_limit_bytes=60 * 2**20, collective_id=0, has_side_effects=True
        ),
        name="attention_grad",
    )(
        global_blocks,
        random_blocks.T,
        query_vectors,
        output_grad,
        key_vectors.reshape(blocks, BLOCK, DH),
        value_vectors.reshape(blocks, BLOCK, DH),
    )
    return query_grad, key_grad.reshape(rows, DH), value_grad.reshape(rows, DH)


def solution(mesh):
    return jax.shard_map(
        body,
        mesh=mesh,
        in_specs=(
            P("seq", "head"),
            P("seq", None),
            P("seq", None),
            P("seq", "head"),
            P("seq", None),
            P(),
        ),
        out_specs=(P("seq", "head"), P("seq", None), P("seq", None)),
        check_vma=False,
    )
```

```python
import functools
import types

import jax
import jax.numpy as jnp
from jax import lax
from jax.experimental import pallas as pl
from jax.experimental.pallas import tpu as pltpu
from jax.sharding import PartitionSpec as P

DH = 128
BLOCK = 128
R = 3
G = 2
NEAR = 3 + G
PAIR = 2 * DH
FACTOR = float(DH) ** -0.5
LOG2E = 1.4426950408889634
NEG = -1e30
NT = (((1,), (1,)), ((), ()))
F32 = jnp.float32
BF16 = jnp.bfloat16
I32 = jnp.int32
MESH = pl.DeviceIdType.MESH


def dot(a, b, dims=(((1,), (0,)), ((), ()))):
    return lax.dot_general(a, b, dims, preferred_element_type=F32)


def fold(value, op):
    return op(value.reshape(BLOCK // 8, 8, PAIR), axis=0)


def arrived(ref, sem):
    pltpu.make_async_copy(ref, ref, sem).wait()


def relays(seq, pieces):
    return max(1, seq // pieces), max(1, pieces // seq)


def unrolled(count, step):
    for i in range(count):
        step(i)


def loop(count, step, first=0):
    def run(i, carry):
        step(i)
        return carry

    lax.fori_loop(first, count, run, 0)


def shapes(seq, heads_x, blocks):
    blocks_x = blocks // heads_x
    quarter = BLOCK // heads_x
    rows_x = blocks_x * BLOCK
    chunks = heads_x * blocks_x
    pieces = G * 2 * BLOCK // 16
    ppr = relays(seq, pieces // heads_x)[1]
    pieces2 = G * (quarter // 8) * 2
    ppr2 = relays(seq, pieces2)[1]
    v, dma = pltpu.VMEM, pltpu.SemaphoreType.DMA
    return dict(
        k=v((blocks, BLOCK, DH), BF16),
        v=v((blocks, BLOCK, DH), BF16),
        q=v((heads_x, rows_x, PAIR), BF16),
        do=v((heads_x, rows_x, PAIR), BF16),
        near=v((2, blocks_x + 2, BLOCK, DH), BF16),
        glob=v((G * 2 * BLOCK // 16, 16, DH), BF16),
        halo=v((2, 2, BLOCK, DH), BF16),
        rnd=v((2, blocks_x, R, BLOCK, DH), BF16),
        tcol=v((blocks * R, 128), I32),
        tvec=v((3, 1, 128), I32),
        tsm=pltpu.SMEM((3, 1, 128), I32),
        wvec=v((1, 128), I32),
        wbuf=v((seq, 1, 128), I32),
        wsm=pltpu.SMEM((seq, 1, 128), I32),
        rvec=v((2, 1, 128), I32),
        rsm=pltpu.SMEM((2, 1, 128), I32),
        served=v((2, seq, quarter, DH), BF16),
        fetched_k=v((seq, quarter, DH), BF16),
        fetched_v=v((seq, quarter, DH), BF16),
        picked=v((2, blocks_x, heads_x - 1, R, quarter, DH), BF16),
        cand=v((pieces, 16, DH), BF16),
        gin=v((seq, ppr, 16, DH), BF16),
        relay=v((ppr, 16, DH), BF16),
        e1=v((chunks, NEAR, BLOCK, PAIR), F32),
        dp1=v((chunks, NEAR, BLOCK, PAIR), F32),
        stats=v((chunks, 8, PAIR), F32),
        dp_buf=v((heads_x, R, BLOCK, PAIR), F32),
        s_far=v((chunks, R, BLOCK, PAIR), F32),
        ds_far=v((chunks, (R + G) * BLOCK, PAIR), BF16),
        ds=v((heads_x, 3 * BLOCK, PAIR), BF16),
        p=v((heads_x, 3, BLOCK, PAIR), BF16),
        kt=v((DH, (NEAR + R) * BLOCK), BF16),
        acc=v((R, BLOCK, PAIR), F32),
        wacc=v((blocks_x + 2 + G, BLOCK, PAIR), F32),
        dq=v((heads_x, rows_x, PAIR), BF16),
        far_out=v((heads_x, blocks_x, R, quarter, PAIR), BF16),
        far_in=v((heads_x, blocks_x, R, quarter, PAIR), BF16),
        near_out=v((heads_x, blocks_x + 2 + G, quarter, PAIR), BF16),
        near_in=v((heads_x, blocks_x + 2 + G, quarter, PAIR), BF16),
        run=v((blocks * R + 1, quarter, PAIR), F32),
        sbuf=v((2, seq, quarter, DH), BF16),
        rbuf=v((2, seq, quarter, DH), BF16),
        run2=v((2, seq + 1, quarter, DH), F32),
        edge=v((2, quarter, PAIR), BF16),
        gp=v((pieces2, 8, DH), F32),
        gin2=v((seq, ppr2, 8, DH), F32),
        relay2=v((ppr2, 8, DH), F32),
        gtot=v((pieces2, 8, DH), F32),
        fin=v((2, blocks, quarter, DH), F32),
        sem_l=dma((8,)),
        sem_w=dma((2,)),
        sem_g=dma((2,)),
        sem_b=dma((2,)),
        sem_x=dma((2,)),
        sem_ne=dma((2,)),
        sem_h=dma((2,)),
        sem_q=dma((heads_x, 2)),
        sem_f=dma((2, 2)),
        sem_r=dma((2, blocks_x, 2)),
        sem_e=dma((blocks_x, 2)),
        sem_d=dma((2,)),
        sem_s=dma((2, 2)),
        sem_ng=dma((2,)),
        sem_nw=dma((2,)),
        sem_n=dma((2,)),
        sem_g2=dma((2,)),
        sem_b2=dma((2,)),
        sem_o=dma((2, 2)),
    )


def kernel(seq, heads_x, names, gb_ref, rb_ref, q_hbm, do_hbm, k_hbm, v_hbm, qg, kg, vg, *scratch):
    m = types.SimpleNamespace(**dict(zip(names, scratch)))
    fetched = (m.fetched_k, m.fetched_v)
    s = lax.axis_index("seq")
    x = lax.axis_index("head")
    blocks = m.k.shape[0]
    blocks_x = blocks // heads_x
    rows_x = blocks_x * BLOCK
    quarter = BLOCK // heads_x
    per = BLOCK // 16
    entries = blocks * R
    part = pl.ds(pl.multiple_of(x * quarter, quarter), quarter)
    own_rows = pl.ds(pl.multiple_of(x * rows_x, rows_x), rows_x)

    def peer(d):
        return lax.rem(x + d, heads_x)

    def remote(src, dst, sems, to):
        pltpu.make_async_remote_copy(
            src_ref=src, dst_ref=dst, send_sem=sems.at[0], recv_sem=sems.at[1],
            device_id=to, device_id_type=MESH,
        ).start()

    barrier = pltpu.get_barrier_semaphore()

    def greet(j):
        pl.semaphore_signal(
            barrier, inc=1, device_id=(lax.rem(s + j, seq), x), device_id_type=MESH
        )

    loop(seq, greet, 1)
    for d in range(1, heads_x):
        pl.semaphore_signal(barrier, inc=1, device_id=(s, peer(d)), device_id_type=MESH)

    local = [
        pltpu.make_async_copy(k_hbm, m.k, m.sem_l.at[0]),
        pltpu.make_async_copy(v_hbm, m.v, m.sem_l.at[1]),
        pltpu.make_async_copy(q_hbm.at[own_rows], m.q.at[x], m.sem_l.at[2]),
        pltpu.make_async_copy(do_hbm.at[own_rows], m.do.at[x], m.sem_l.at[3]),
    ]
    for copy in local:
        copy.start()

    for r in range(R):
        row = jnp.broadcast_to(rb_ref[r : r + 1, :], (blocks, blocks))
        mine = lax.broadcasted_iota(I32, row.shape, 0) == lax.broadcasted_iota(I32, row.shape, 1)
        picked = jnp.max(jnp.where(mine, row, 0), axis=1, keepdims=True)
        m.tcol[r * blocks : (r + 1) * blocks] = jnp.broadcast_to(picked, (blocks, 128))
    column = m.tcol[...]
    owner = lax.div(column, jnp.full_like(column, blocks))
    within = column - owner * blocks
    at = lax.broadcasted_iota(I32, column.shape, 0)
    lane = lax.broadcasted_iota(I32, column.shape, 1)

    def pick(cond, value):
        return jnp.max(jnp.where(cond, value, 0), axis=0, keepdims=True)

    owner_row = pick(at == lane, owner)
    m.wvec[...] = pick(owner == lane, within)
    m.tvec[0] = owner_row
    m.tvec[1] = pick((owner == owner_row) & (at < lane), at + 1)
    m.tvec[2] = pick(owner == lane, at + 1)
    table = pltpu.make_async_copy(m.tvec, m.tsm, m.sem_l.at[4])
    table.start()
    m.wbuf[s] = m.wvec[...]
    local[0].wait()
    local[1].wait()
    for g in range(G):
        for n, ref in enumerate((m.k, m.v)):
            first = (g * 2 + n) * per
            m.cand[first : first + per] = ref[lax.rem(gb_ref[g], blocks)].reshape(per, 16, DH)
    table.wait()

    pl.semaphore_wait(barrier, seq - 1 + heads_x - 1)

    loop(
        seq,
        lambda j: remote(m.wvec, m.wbuf.at[s], m.sem_w, (lax.rem(s + j, seq), x)),
        1,
    )
    pieces = m.cand.shape[0] // heads_x
    base = x * pieces
    stride, ppr = relays(seq, pieces)
    count = pieces // ppr
    is_relay = lax.rem(s, stride) == 0
    mine = s // stride

    def send_cand(r):
        @pl.when(r * stride != s)
        def _():
            remote(m.cand.at[pl.ds(base + r * ppr, ppr)], m.gin.at[s], m.sem_g, (r * stride, x))

    loop(count, send_cand)

    @pl.when(is_relay)
    def _():
        m.gin[s] = m.cand[pl.ds(base + mine * ppr, ppr)]

    for d in range(1, heads_x):
        rows = pl.ds(pl.multiple_of(peer(d) * rows_x, rows_x), rows_x)
        remote(q_hbm.at[rows], m.q.at[x], m.sem_q.at[d], (s, peer(d)))
        remote(do_hbm.at[rows], m.do.at[x], m.sem_q.at[d], (s, peer(d)))
    after = (lax.rem(s + 1, seq), x)
    before = (lax.rem(s + seq - 1, seq), x)
    for n, ref in enumerate((m.k, m.v)):
        remote(ref.at[blocks - 1], m.halo.at[0, n], m.sem_h, after)
        remote(ref.at[0], m.halo.at[1, n], m.sem_h, before)

    arrived(m.wbuf.at[pl.ds(0, seq - 1)], m.sem_w.at[1])
    to_smem = pltpu.make_async_copy(m.wbuf, m.wsm, m.sem_l.at[5])
    to_smem.start()

    @pl.when(is_relay)
    def _():
        arrived(m.gin.at[pl.ds(0, seq - 1)], m.sem_g.at[1])
        for i in range(ppr):
            g = (base + mine * ppr + i) // (2 * per)
            m.relay[i] = m.gin[lax.div(gb_ref[g], blocks), i]
        m.glob[pl.ds(base + mine * ppr, ppr)] = m.relay[...]

    def serve(n, ref):
        def step(e):
            m.served[n, e] = ref[m.wsm[e, 0, s], part, :]

        loop(seq, step)
        fetched[n][s] = m.served[n, s]

    def send_served(n):
        loop(
            seq,
            lambda j: remote(
                m.served.at[n, lax.rem(s + j, seq)],
                fetched[n].at[s],
                m.sem_f.at[n],
                (lax.rem(s + j, seq), x),
            ),
            1,
        )

    to_smem.wait()
    serve(0, m.k)

    @pl.when(is_relay)
    def _():
        loop(
            seq,
            lambda j: remote(
                m.relay,
                m.glob.at[pl.ds(base + mine * ppr, ppr)],
                m.sem_b,
                (lax.rem(s + j, seq), x),
            ),
            1,
        )

    send_served(0)
    serve(1, m.v)
    send_served(1)

    asked = m.wbuf[...].reshape(seq, 128)
    at = lax.broadcasted_iota(I32, asked.shape, 0)
    lane = lax.broadcasted_iota(I32, asked.shape, 1)
    asked = jnp.max(jnp.where(lane == s, asked, 0), axis=1, keepdims=True)
    asked = jnp.broadcast_to(asked, (seq, 128))
    asked_row = jnp.max(jnp.where(at == lane, asked, -1), axis=0, keepdims=True)
    m.rvec[0] = pick((asked == asked_row) & (at < lane), at + 1)
    m.rvec[1] = pick(asked == lane, at + 1)
    table = pltpu.make_async_copy(m.rvec, m.rsm, m.sem_l.at[6])
    table.start()

    @pl.when(is_relay)
    def _():
        arrived(m.glob.at[pl.ds(0, (count - 1) * ppr)], m.sem_b.at[1])

    @pl.when(jnp.logical_not(is_relay))
    def _():
        arrived(m.glob.at[pl.ds(0, pieces)], m.sem_b.at[1])

    plane = pl.ds(base, pieces)
    for d in range(1, heads_x):
        remote(m.glob.at[plane], m.glob.at[plane], m.sem_x, (s, peer(d)))

    arrived(m.halo, m.sem_h.at[1])
    for i in range(blocks_x + 2):
        place = x * blocks_x + (i - 1)
        inner = jnp.clip(place, 0, blocks - 1)
        for n, ref in enumerate((m.k, m.v)):
            value = ref[inner]
            if i == 0:
                value = jnp.where(place < 0, m.halo[0, n], value)
            if i == blocks_x + 1:
                value = jnp.where(place >= blocks, m.halo[1, n], value)
            m.near[n, i] = value
    m.wacc[...] = jnp.zeros_like(m.wacc)

    arrived(m.glob.at[pl.ds(0, (heads_x - 1) * pieces)], m.sem_x.at[1])
    local[2].wait()
    local[3].wait()

    def near_block(n, b, j):
        if j < 3:
            return m.near[n, b + j]
        first = ((j - 3) * 2 + n) * per
        return m.glob[first : first + per].reshape(BLOCK, DH)

    def rows_of(b):
        return pl.ds(pl.multiple_of(b * BLOCK, BLOCK), BLOCK)

    def stacked(ref, h, b):
        return jnp.concatenate([ref[h, rows_of(b), :DH], ref[h, rows_of(b), DH:]], axis=0)

    def source(d):
        return lax.rem(x + heads_x - d, heads_x)

    def near_scores(d):
        @pl.when(d > 0)
        def _():
            arrived(m.q.at[pl.ds(0, 2)], m.sem_q.at[d, 1])

        def step(b):
            i = b * heads_x + d
            q = stacked(m.q, source(d), b)
            do = stacked(m.do, source(d), b)
            before_ok = (s + x + b) > 0
            after_ok = (seq - s + heads_x - x + blocks_x - b) > 3
            top = jnp.full((8, PAIR), NEG, F32)
            for j in range(NEAR):
                score = dot(near_block(0, b, j), q, NT)
                if j == 0:
                    score = jnp.where(before_ok, score, NEG)
                if j == 2:
                    score = jnp.where(after_ok, score, NEG)
                m.e1[i, j] = score
                top = jnp.maximum(top, fold(score, jnp.max))
            top = jnp.max(top, axis=0, keepdims=True)
            total = jnp.zeros((8, PAIR), F32)
            inner = jnp.zeros((8, PAIR), F32)
            for j in range(NEAR):
                dp = dot(near_block(1, b, j), do, NT)
                e = jnp.exp2((m.e1[i, j] - top) * (FACTOR * LOG2E))
                total = total + fold(e, jnp.sum)
                inner = inner + fold(e * dp, jnp.sum)
                m.e1[i, j] = e
                m.dp1[i, j] = dp
            m.stats[i, 0:1] = top
            m.stats[i, 1:2] = jnp.sum(total, axis=0, keepdims=True)
            m.stats[i, 2:3] = jnp.sum(inner, axis=0, keepdims=True)

        unrolled(blocks_x, step)

    loop(heads_x, near_scores)

    def hand_out(n):
        arrived(fetched[n].at[pl.ds(0, seq - 1)], m.sem_f.at[n, 1])

        def step(b):
            for d in range(1, heads_x):
                for j in range(R):
                    entry = m.tsm[0, 0, j * blocks + peer(d) * blocks_x + b]
                    m.picked[n, b, d - 1, j] = fetched[n][entry]
            for j in range(R):
                entry = m.tsm[0, 0, j * blocks + x * blocks_x + b]
                m.rnd[n, b, j, part, :] = fetched[n][entry]
            for d in range(1, heads_x):
                remote(
                    m.picked.at[n, b, d - 1],
                    m.rnd.at[n, b, :, part, :],
                    m.sem_r.at[n, b],
                    (s, peer(d)),
                )

        loop(blocks_x, step)

    def rnd_ready(n, b):
        rest = pl.ds(0, (heads_x - 1) * quarter)
        arrived(m.rnd.at[n, b, :, rest, :], m.sem_r.at[n, b, 1])

    hand_out(0)

    def far_scores(b):
        rnd_ready(0, b)

        def step(d):
            i = b * heads_x + d
            q = stacked(m.q, source(d), b)
            top = jnp.full((8, PAIR), NEG, F32)
            for j in range(R):
                score = dot(m.rnd[0, b, j], q, NT)
                m.s_far[i, j] = score
                top = jnp.maximum(top, fold(score, jnp.max))
            m.stats[i, 5:6] = jnp.max(top, axis=0, keepdims=True)

        unrolled(heads_x, step)

    loop(blocks_x, far_scores)
    hand_out(1)

    lane = lax.broadcasted_iota(I32, (BLOCK, PAIR), 1)
    scale_lanes = jnp.where(lane < DH, FACTOR, 1.0)

    near_slots = blocks_x + 2

    def far_block(b):
        rnd_ready(1, b)
        m.acc[...] = jnp.zeros_like(m.acc)

        def step(d):
            i = b * heads_x + d
            q = stacked(m.q, source(d), b)
            do = stacked(m.do, source(d), b)
            top1, total1, inner1 = m.stats[i, 0:1], m.stats[i, 1:2], m.stats[i, 2:3]
            top = jnp.maximum(m.stats[i, 5:6], top1)
            total = jnp.zeros((8, PAIR), F32)
            inner = jnp.zeros((8, PAIR), F32)
            for j in range(R):
                dp = dot(m.rnd[1, b, j], do, NT)
                e = jnp.exp2((m.s_far[i, j] - top) * (FACTOR * LOG2E))
                total = total + fold(e, jnp.sum)
                inner = inner + fold(e * dp, jnp.sum)
                m.s_far[i, j] = e
                m.dp_buf[d, j] = dp
            shrink = jnp.exp2((top1 - top) * (FACTOR * LOG2E))
            total = jnp.sum(total, axis=0, keepdims=True) + total1 * shrink
            inner = jnp.sum(inner, axis=0, keepdims=True) + inner1 * shrink
            scale = 1.0 / total
            delta = inner * scale
            near_scale = shrink * scale
            m.stats[i, 3:4] = near_scale
            m.stats[i, 4:5] = delta
            for j in range(R):
                a = m.s_far[i, j] * scale
                ds = (a * (m.dp_buf[d, j] - delta)).astype(BF16)
                m.ds_far[i, j * BLOCK : (j + 1) * BLOCK] = ds
                m.acc[j, :, :DH] += dot(ds, q)
                m.acc[j, :, DH:] += dot(a.astype(BF16), do)
            for g in range(G):
                a = m.e1[i, 3 + g] * near_scale
                ds = (a * (m.dp1[i, 3 + g] - delta)).astype(BF16)
                m.ds_far[i, (R + g) * BLOCK : (R + g + 1) * BLOCK] = ds
                m.wacc[near_slots + g, :, :DH] += dot(ds, q)
                m.wacc[near_slots + g, :, DH:] += dot(a.astype(BF16), do)

        unrolled(heads_x, step)
        for j in range(R):
            grad = (m.acc[j] * scale_lanes).astype(BF16)
            for to in range(heads_x):
                m.far_out[to, b, j] = grad[to * quarter : (to + 1) * quarter]
        m.far_in[x, b] = m.far_out[x, b]
        for d in range(1, heads_x):
            remote(m.far_out.at[peer(d), b], m.far_in.at[x, b], m.sem_e.at[b], (s, peer(d)))

    loop(blocks_x, far_block)

    glob_part = pl.ds(near_slots, G)
    near_part = pl.ds(1, blocks_x)

    def near_grad_out(j):
        grad = (m.wacc[j] * scale_lanes).astype(BF16)
        for to in range(heads_x):
            m.near_out[to, j] = grad[to * quarter : (to + 1) * quarter]
        m.near_in[x, j] = m.near_out[x, j]

    for g in range(G):
        near_grad_out(near_slots + g)
    for d in range(1, heads_x):
        remote(
            m.near_out.at[peer(d), glob_part], m.near_in.at[x, glob_part], m.sem_ng, (s, peer(d))
        )

    m.run[0] = jnp.zeros((quarter, PAIR), F32)
    for n in range(2):
        m.run2[n, 0] = jnp.zeros((quarter, DH), F32)
    for b in range(blocks_x):
        arrived(m.far_out.at[pl.ds(0, heads_x - 1), b], m.sem_e.at[b, 1])
    for j in range(R):

        def chain(i, j=j):
            entry = j * blocks + i
            grad = m.far_in[i // blocks_x, lax.rem(i, blocks_x), j].astype(F32)
            m.run[entry + 1] = grad + m.run[m.tsm[1, 0, entry]]

        loop(blocks, chain)

    def fill(e):
        value = m.run[m.tsm[2, 0, e]].astype(BF16)
        m.sbuf[0, e] = value[:, :DH]
        m.sbuf[1, e] = value[:, DH:]

    loop(seq, fill)
    for n in range(2):
        m.rbuf[n, s] = m.sbuf[n, s]

    def send_slot(n, j):
        to = lax.rem(s + j, seq)
        remote(m.sbuf.at[n, to], m.rbuf.at[n, s], m.sem_s.at[n], (to, x))

    lines = quarter // 8
    pieces2 = m.gp.shape[0]
    stride2, ppr2 = relays(seq, pieces2)
    count2 = pieces2 // ppr2
    is_relay2 = lax.rem(s, stride2) == 0
    mine2 = s // stride2
    arrived(m.near_out.at[pl.ds(0, heads_x - 1), glob_part], m.sem_ng.at[1])
    for g in range(G):
        value = m.near_in[0, near_slots + g].astype(F32)
        for src in range(1, heads_x):
            value = value + m.near_in[src, near_slots + g].astype(F32)
        for c in range(lines):
            for n in range(2):
                m.gp[(g * lines + c) * 2 + n] = value[
                    c * 8 : (c + 1) * 8, n * DH : (n + 1) * DH
                ]

    @pl.when(is_relay2)
    def _():
        m.gin2[s] = m.gp[pl.ds(mine2 * ppr2, ppr2)]

    loop(seq // 2, lambda j: send_slot(1, 2 * j + 1))

    def send_global(r):
        @pl.when(r * stride2 != s)
        def _():
            remote(m.gp.at[pl.ds(r * ppr2, ppr2)], m.gin2.at[s], m.sem_g2, (r * stride2, x))

    loop(count2, send_global)
    loop(seq // 2, lambda j: send_slot(1, 2 * j), 1)

    def near_grads(b):
        for j in range(3 + R + G):
            if j < 3:
                keys = near_block(0, b, j)
            elif j < 3 + R:
                keys = m.rnd[0, b, j - 3]
            else:
                keys = near_block(0, b, j - R)
            m.kt[:, j * BLOCK : (j + 1) * BLOCK] = keys.T

        def step(d):
            i = b * heads_x + d
            h = source(d)
            q = stacked(m.q, h, b)
            do = stacked(m.do, h, b)
            scale, delta = m.stats[i, 3:4], m.stats[i, 4:5]
            for j in range(3):
                a = m.e1[i, j] * scale
                m.p[d, j] = a.astype(BF16)
                m.ds[d, j * BLOCK : (j + 1) * BLOCK] = (a * (m.dp1[i, j] - delta)).astype(BF16)
            for j in range(3):
                m.wacc[b + j, :, :DH] += dot(m.ds[d, j * BLOCK : (j + 1) * BLOCK], q)
                m.wacc[b + j, :, DH:] += dot(m.p[d, j], do)
            dqt = dot(m.kt[:, : 3 * BLOCK], m.ds[d])
            dqt = (dqt + dot(m.kt[:, 3 * BLOCK :], m.ds_far[i])) * FACTOR
            m.dq[h, rows_of(b), :DH] = dqt[:, :BLOCK].T.astype(BF16)
            m.dq[h, rows_of(b), DH:] = dqt[:, BLOCK:].T.astype(BF16)

        unrolled(heads_x, step)

    def send_dq(b):
        out = pl.ds(pl.multiple_of(x * rows_x + b * BLOCK, BLOCK), BLOCK)
        for d in range(1, heads_x):
            remote(m.dq.at[peer(d), rows_of(b)], qg.at[out], m.sem_d, (s, peer(d)))
        pltpu.make_async_copy(m.dq.at[x, rows_of(b)], qg.at[out], m.sem_l.at[7]).start()

    last = blocks_x - 1

    def near_all(b):
        near_grads(b)
        send_dq(b)

    loop(1, near_all)
    loop(blocks_x, near_all, max(last, 1))
    for j in (0, near_slots - 1):
        near_grad_out(j)
        for d in range(1, heads_x):
            remote(m.near_out.at[peer(d), j], m.near_in.at[x, j], m.sem_ne, (s, peer(d)))

    @pl.when(is_relay2)
    def _():
        arrived(m.gin2.at[pl.ds(0, seq - 1)], m.sem_g2.at[1])
        m.relay2[...] = jnp.zeros_like(m.relay2)

        def add(e):
            m.relay2[...] += m.gin2[e]

        loop(seq, add)
        m.gtot[pl.ds(mine2 * ppr2, ppr2)] = m.relay2[...]
        loop(
            seq,
            lambda j: remote(
                m.relay2, m.gtot.at[pl.ds(mine2 * ppr2, ppr2)], m.sem_b2, (lax.rem(s + j, seq), x)
            ),
            1,
        )

    if last > 2:
        loop(last - 1, near_all, 1)
    arrived(m.near_out.at[pl.ds(0, heads_x - 1), pl.ds(0, 2)], m.sem_ne.at[1])
    remote(m.near_in.at[0, 0], m.edge.at[1], m.sem_n, before)
    remote(m.near_in.at[heads_x - 1, blocks_x + 1], m.edge.at[0], m.sem_n, after)
    loop(seq, lambda j: send_slot(0, j), 1)
    if last > 1:
        loop(last, near_grads, last - 1)
    for j in range(1, near_slots - 1):
        near_grad_out(j)
    for d in range(1, heads_x):
        remote(
            m.near_out.at[peer(d), near_part], m.near_in.at[x, near_part], m.sem_nw, (s, peer(d))
        )
    if last > 1:
        loop(last, send_dq, last - 1)
    arrived(m.near_out.at[pl.ds(0, heads_x - 1), near_part], m.sem_nw.at[1])
    arrived(m.edge, m.sem_n.at[1])

    @pl.when(is_relay2)
    def _():
        arrived(m.gtot.at[pl.ds(0, (count2 - 1) * ppr2)], m.sem_b2.at[1])

    @pl.when(jnp.logical_not(is_relay2))
    def _():
        arrived(m.gtot, m.sem_b2.at[1])

    for b in range(blocks):
        src, i = b // blocks_x, b % blocks_x
        total = m.near_in[src, 1 + i].astype(F32)
        if i == 0:
            more = m.edge[0] if src == 0 else m.near_in[src - 1, blocks_x + 1]
            total = total + more.astype(F32)
        if i == blocks_x - 1:
            more = m.edge[1] if src == heads_x - 1 else m.near_in[src + 1, 0]
            total = total + more.astype(F32)
        held = [jnp.where(gb_ref[g] == s * blocks + b, 1.0, 0.0) for g in range(G)]
        for c in range(lines):
            for n in range(2):
                value = total[c * 8 : (c + 1) * 8, n * DH : (n + 1) * DH]
                for g in range(G):
                    value = value + held[g] * m.gtot[(g * lines + c) * 2 + n]
                m.fin[n, b, c * 8 : (c + 1) * 8] = value

    table.wait()

    def finish(n, ref):
        arrived(m.rbuf.at[n, pl.ds(0, seq - 1)], m.sem_s.at[n, 1])

        def gather(e):
            m.run2[n, e + 1] = m.rbuf[n, e].astype(F32) + m.run2[n, m.rsm[0, 0, e]]

        loop(seq, gather)
        for b in range(blocks):
            ref[b, part, :] = (m.fin[n, b] + m.run2[n, m.rsm[1, 0, b]]).astype(BF16)
        for d in range(1, heads_x):
            remote(ref.at[:, part, :], ref.at[:, part, :], m.sem_o.at[n], (s, peer(d)))

    finish(1, vg)
    finish(0, kg)

    others = pl.ds(0, heads_x - 1)
    arrived(m.wbuf.at[pl.ds(0, seq - 1)], m.sem_w.at[0])
    for n in range(2):
        arrived(m.served.at[n, pl.ds(0, seq - 1)], m.sem_f.at[n, 0])
        arrived(m.rbuf.at[n, pl.ds(0, seq - 1)], m.sem_s.at[n, 0])
    for d in range(1, heads_x):
        arrived(m.q.at[pl.ds(0, 2)], m.sem_q.at[d, 0])
    arrived(m.halo, m.sem_h.at[0])
    arrived(m.glob.at[pl.ds(0, (heads_x - 1) * pieces)], m.sem_x.at[0])
    for b in range(blocks_x):
        for n in range(2):
            arrived(m.picked.at[n, b], m.sem_r.at[n, b, 0])
        arrived(m.far_out.at[others, b], m.sem_e.at[b, 0])
    arrived(m.near_out.at[others, glob_part], m.sem_ng.at[0])
    arrived(m.near_out.at[others, near_part], m.sem_nw.at[0])
    arrived(m.near_out.at[others, pl.ds(0, 2)], m.sem_ne.at[0])
    arrived(m.edge, m.sem_n.at[0])
    arrived(m.dq.at[others], m.sem_d.at[0])
    arrived(m.dq.at[others], m.sem_d.at[1])
    arrived(m.dq.at[0], m.sem_l.at[7])

    def drain(relay, count, gin, send_sem, relay_sem):
        @pl.when(relay)
        def _():
            arrived(gin.at[pl.ds(0, seq - 1)], relay_sem.at[0])
            if count > 1:
                arrived(gin.at[pl.ds(0, count - 1)], send_sem.at[0])

        @pl.when(jnp.logical_not(relay))
        def _():
            arrived(gin.at[pl.ds(0, count)], send_sem.at[0])

    drain(is_relay, count, m.gin, m.sem_g, m.sem_b)
    drain(is_relay2, count2, m.gin2, m.sem_g2, m.sem_b2)
    rest = pl.ds(0, (heads_x - 1) * quarter)
    for n, ref in enumerate((kg, vg)):
        arrived(ref.at[:, rest, :], m.sem_o.at[n, 0])
        arrived(ref.at[:, rest, :], m.sem_o.at[n, 1])


def hand_over_kernel(*refs):
    half = len(refs) // 2
    for source, target in zip(refs[:half], refs[half:]):
        target[...] = source[...]


def hand_over(arrays, steps=4):
    specs = [
        pl.BlockSpec((a.shape[0] // steps, a.shape[1]), lambda i: (i, 0)) for a in arrays
    ]
    return pl.pallas_call(
        hand_over_kernel,
        grid=(steps,),
        out_shape=tuple(jax.ShapeDtypeStruct(a.shape, a.dtype) for a in arrays),
        in_specs=specs,
        out_specs=tuple(specs),
        name="hand_over",
    )(*arrays)


def body(query_vectors, key_vectors, value_vectors, output_grad, random_blocks, global_blocks):
    seq = lax.axis_size("seq")
    heads_x = lax.axis_size("head")
    rows, width = query_vectors.shape
    blocks = rows // BLOCK
    scratch = shapes(seq, heads_x, blocks)
    vmem = pl.BlockSpec(memory_space=pltpu.VMEM)
    anyspec = pl.BlockSpec(memory_space=pl.ANY)
    folded = jax.ShapeDtypeStruct((blocks, BLOCK, DH), BF16)
    query_grad, key_grad, value_grad = pl.pallas_call(
        functools.partial(kernel, seq, heads_x, tuple(scratch)),
        out_shape=(jax.ShapeDtypeStruct((rows, width), BF16), folded, folded),
        in_specs=[pl.BlockSpec(memory_space=pltpu.SMEM), vmem] + [anyspec] * 4,
        out_specs=(vmem, vmem, vmem),
        scratch_shapes=tuple(scratch.values()),
        compiler_params=pltpu.CompilerParams(
            vmem_limit_bytes=60 * 2**20, collective_id=0, has_side_effects=True
        ),
        name="attention_grad",
    )(
        global_blocks,
        random_blocks.T,
        query_vectors,
        output_grad,
        key_vectors.reshape(blocks, BLOCK, DH),
        value_vectors.reshape(blocks, BLOCK, DH),
    )
    return hand_over((query_grad, key_grad.reshape(rows, DH), value_grad.reshape(rows, DH)))


def solution(mesh):
    return jax.shard_map(
        body,
        mesh=mesh,
        in_specs=(
            P("seq", "head"),
            P("seq", None),
            P("seq", None),
            P("seq", "head"),
            P("seq", None),
            P(),
        ),
        out_specs=(P("seq", "head"), P("seq", None), P("seq", None)),
        check_vma=False,
    )
```
